32 devices in a mesh: star: 2 (over core), dev: 16 (over z, y, x).
Axes of the slice: x: 2, y: 2, z: 4, core: 2. Of those that a mesh axis runs over, the one named last changes fastest.
Arguments:
- screens: bfloat16 [3, 32, 256, 8192], P(None, None, 'dev', 'star'), may hold values from -4 to 4
- foot_rows: int32 [3, 2], replicated, may hold values from 0 to 8191
- foot_cols: int32 [3, 2], replicated, may hold values from 0 to 6784
- wind: int32 [3, 3, 2], replicated, may hold values from 0 to 15
- amplitude: float32 [256, 1280], P('dev'), may hold values from 0.5 to 1.5
- owner: int32 [2, 16], P('star', 'dev'), may hold values from 0 to 5
- refs: float32 [6, 16, 16], replicated, may hold values from 0.1 to 1
Outputs:
- correlation: float32 [3, 2, 16, 80, 256], P(None, 'star', 'dev')
The draws below stay inside these ranges and needn't reach their ends.
All inputs are finite; a program needn't handle non-finite values.
Results may differ from the reference program's by a relative error of at most 0.0003.
Values may be sent and summed in bfloat16 or wider, within the bound.
No kernel may reach another device: no remote copies, remote signals or barrier semaphores. Data moves between devices by JAX's collectives and lax.ppermute only.
A program may use at most 128 MiB of HBM per device.

```python
import math
import jax
import jax.numpy as jnp
from jax import lax

SUBPX = 16
NSUBC = 80
BIN = 4
MARGIN = 128
WIDTH = 8192
ROWS = 8192
LAYERS = 3
STEPS = 3
NCAM = 6
NSTAR = 2
NSUBR = 16
FOOT = 256
BANDS = 32
PUPIL = 1280
FFTN = 64
DET = 16


def touch_ends(drawn, rng, smallest, top_value):
    dims = drawn.shape
    index_at = [jax.random.randint(jax.random.fold_in(rng, axis), (), 0, dims[axis]) for axis in range(len(dims))]
    drawn = drawn.at[tuple(index_at)].set(smallest)
    longest = dims.index(max(dims))
    index_at[longest] = (index_at[longest] + 1) % dims[longest]
    return drawn.at[tuple(index_at)].set(top_value)


def block_scale(key, shape, cuts, low, largest):
    def one(axis_at, parts):
        steps = jax.random.uniform(jax.random.fold_in(jax.random.fold_in(key, 6), axis_at), (parts,), jnp.float32, low / len(cuts), largest / len(cuts))
        return jnp.repeat(jnp.exp(steps), shape[axis_at] // parts).reshape((-1,) + (1,) * (len(shape) - axis_at - 1))

    level = one(*cuts[0])
    for cut in cuts[1:]:
        level = level * one(*cut)
    return level


def bell_draw(key, shape, spread, bound, shards=(), kind=jnp.bfloat16):
    values = jax.random.normal(key, shape, jnp.float32) * spread
    if len(shards) > 0:
        values = block_scale(key, shape, shards, -0.22, 0.18) * values
    return jnp.clip(values, min=-bound, max=bound).astype(kind)


def setup_inputs(seed: int = 0) -> dict:
    key_of = jax.random.split(jax.random.key(seed), 8)
    screens = bell_draw(key_of[0], (LAYERS, BANDS, FOOT, WIDTH), 0.6, 4.0, ((2, 16), (3, 2)))
    foot_rows = touch_ends(jax.random.randint(key_of[1], (LAYERS, NSTAR), 0, ROWS), jax.random.fold_in(key_of[1], 1), 0, ROWS - 1).astype(jnp.int32)
    foot_cols = touch_ends(jax.random.randint(key_of[2], (LAYERS, NSTAR), 0, WIDTH - PUPIL - MARGIN + 1), jax.random.fold_in(key_of[2], 1), 0, WIDTH - PUPIL - MARGIN).astype(jnp.int32)
    wind = touch_ends(jax.random.randint(key_of[3], (STEPS, LAYERS, 2), 0, SUBPX), jax.random.fold_in(key_of[3], 1), 0, SUBPX - 1).astype(jnp.int32)
    amplitude = jnp.clip(0.5 + 1.0 * jax.random.uniform(key_of[4], (FOOT, PUPIL), jnp.float32) ** block_scale(key_of[4], (FOOT, PUPIL), ((0, 16),), -0.2, 0.2), 0.5, 1.5)
    owner = touch_ends(jax.random.randint(key_of[5], (NSTAR, NSUBR), 0, NCAM), jax.random.fold_in(key_of[5], 1), 0, NCAM - 1).astype(jnp.int32)
    refs = jnp.clip(jnp.exp(jax.random.uniform(key_of[6], (NCAM, DET, DET), jnp.float32, math.log(0.1), math.log(1.0))), 0.1, 1.0)
    return dict(screens=screens, foot_rows=foot_rows, foot_cols=foot_cols, wind=wind, amplitude=amplitude, owner=owner, refs=refs)


def spots_one(row_phase, row_amp, camera, refs):
    blocks = row_phase.reshape(SUBPX, NSUBC, SUBPX).transpose(1, 0, 2)
    amps = row_amp.reshape(SUBPX, NSUBC, SUBPX).transpose(1, 0, 2)
    field = amps * jnp.cos(blocks) + 1j * (amps * jnp.sin(blocks))
    spec = jnp.fft.fft2(field, s=(FFTN, FFTN))
    power = spec.real * spec.real + spec.imag * spec.imag
    power = jnp.fft.fftshift(power, axes=(1, 2))
    binned = power.reshape(NSUBC, DET, BIN, DET, BIN).sum(axis=(2, 4))
    image = binned / jnp.sum(binned, axis=(1, 2), keepdims=True)
    refer = refs[camera]
    corr = jnp.fft.ifft2(jnp.fft.fft2(image) * jnp.conj(jnp.fft.fft2(refer))[None]).real
    return corr.reshape(NSUBC, DET * DET).astype(jnp.float32)


def reference(screens, foot_rows, foot_cols, wind, amplitude, owner, refs):
    row_amps = amplitude.reshape(NSUBR, SUBPX, PUPIL)
    per_step = []
    for step in range(STEPS):
        per_star = []
        for star in range(NSTAR):
            phase = jnp.zeros((FOOT, PUPIL), jnp.float32)
            for layer in range(LAYERS):
                full = screens[layer].reshape(ROWS, WIDTH)
                left = (foot_cols[layer, star] + wind[step, layer, 1]).astype(jnp.int32)
                columns = lax.dynamic_slice_in_dim(full, left, PUPIL, 1)
                offset = (foot_rows[layer, star] + wind[step, layer, 0]).astype(jnp.int32)
                picks = ((offset + jnp.arange(FOOT, dtype=jnp.int32)) % ROWS).astype(jnp.int32)
                phase = phase + jnp.take(columns, picks, axis=0).astype(jnp.float32)
            row_phases = phase.reshape(NSUBR, SUBPX, PUPIL)

            def one_row(items):
                return spots_one(items[0], items[1], items[2], refs)

            per_star.append(lax.map(one_row, (row_phases, row_amps, owner[star])))
        per_step.append(jnp.stack(per_star))
    return jnp.stack(per_step)
```

```python
import functools
import math

import jax
import jax.numpy as jnp
import numpy as np
from jax import lax
from jax.experimental import pallas as pl
from jax.experimental.pallas import tpu as pltpu
from jax.sharding import PartitionSpec as P

BIN = 4
SIDE = 16
LANES = 128
SPAN = 12
QUART = 4
THIRD = SPAN // QUART

F32 = jnp.float32
BF16 = jnp.bfloat16


def split_np(table):
    high = table.astype(jnp.bfloat16)
    low = (table - high.astype(np.float64)).astype(jnp.bfloat16)
    return high, low


def split(value):
    high = value.astype(BF16)
    return high, (value - high.astype(F32)).astype(BF16)


def across_tables():
    length = BIN * SIDE
    freq = (np.arange(length) + length // 2) % length
    angle = 2.0 * math.pi * (np.outer(np.arange(SIDE), freq) % length) / length
    real, imag = np.cos(angle), -np.sin(angle)
    out = np.zeros((2, 8, SIDE, 2, BIN, SIDE, 8))
    for i in range(8):
        for b in range(BIN):
            re, im = real[:, b::BIN], imag[:, b::BIN]
            out[0, i, :, 0, b, :, i] = re
            out[1, i, :, 0, b, :, i] = -im
            out[0, i, :, 1, b, :, i] = im
            out[1, i, :, 1, b, :, i] = re
    return split_np(out.reshape(2 * 8 * SIDE, 2 * BIN * SIDE * 8))


def down_table():
    length = BIN * SIDE
    freq = (np.arange(length) + length // 2) % length
    angle = 2.0 * math.pi * (np.outer(freq, np.arange(SIDE)) % length) / length
    real, imag = np.cos(angle), -np.sin(angle)
    order = np.concatenate([np.arange(a, length, BIN) for a in range(BIN)])
    real, imag = real[order], imag[order]
    table = np.block([[real, -imag], [imag, real]])
    high, low = split_np(table)
    return np.concatenate([high, high, low], axis=1)


def place_of(rows_ref, cols_ref, layer, star, devices, total_tiles):
    offset = rows_ref[layer, star]
    strip = lax.div(offset, SIDE)
    part = lax.rem(offset, SIDE)
    tile = jnp.minimum(lax.div(cols_ref[layer, star], LANES), total_tiles - SPAN)
    return strip, part, tile


def first_tile(tile, panel, tiles, held):
    return jnp.clip(tile - panel * tiles, 0, tiles - held)


def crop_kernel(stars, devices, rows_ref, cols_ref, screens_ref, *rest):
    outs, sem = rest[:stars], rest[stars]
    layers, bands, side, width = screens_ref.shape
    tiles = width // LANES
    held = min(SPAN, tiles)
    me = lax.axis_index("star")
    place = lax.axis_index("dev")
    copies = []
    for turn in range(stars):
        star = lax.rem(me + turn, stars)
        for layer in range(layers):
            strip, _, tile = place_of(rows_ref, cols_ref, layer, star, devices, stars * tiles)
            behind = lax.rem(place + bands * devices - strip, devices)
            band = lax.div(strip + behind, devices)
            start = first_tile(tile, me, tiles, held)
            columns = pl.ds(pl.multiple_of(start * LANES, LANES), held * LANES)
            for slot in range(2):
                copy = pltpu.make_async_copy(
                    screens_ref.at[layer, lax.rem(band + slot, bands), :, columns],
                    outs[turn].at[2 * layer + slot],
                    sem.at[turn, 2 * layer + slot],
                )
                copy.start()
                copies.append(copy)
    for copy in copies:
        copy.wait()


def spread_kernel(stars, devices, tiles, rows_ref, cols_ref, *rest):
    parts, out_ref, turned = rest[:stars], rest[stars], rest[stars + 1]
    layers = parts[0].shape[0] // 2
    held = parts[0].shape[2] // LANES
    groups = devices // SIDE
    sub = QUART // groups
    me = lax.axis_index("star")
    place = lax.axis_index("dev")
    row = lax.broadcasted_iota(jnp.int32, (SIDE, LANES), 0)
    for layer in range(layers):
        strip, part, tile = place_of(rows_ref, cols_ref, layer, me, devices, stars * tiles)
        behind = lax.rem(place + (1 << 20) * devices - strip, devices)
        bound = jnp.where(behind == 0, part, 0)
        wraps = row < bound
        for a in range(QUART):
            for b in range(THIRD):
                spot = tile + (THIRD * a + b)
                panel = lax.div(spot, tiles)
                pair = []
                for slot in range(2):
                    value = None
                    for turn in range(stars):
                        sender = lax.rem(me + stars - turn, stars)
                        start = first_tile(tile, sender, tiles, held)
                        local = jnp.clip(spot - sender * tiles - start, 0, held - 1)
                        lanes = pl.ds(pl.multiple_of(local * LANES, LANES), LANES)
                        seen = parts[turn][2 * layer + slot, :, lanes].astype(F32)
                        if value is None:
                            value = seen
                        else:
                            value = jnp.where(panel == sender, seen, value)
                    pair.append(value)
                first = jnp.where(wraps, pair[1], pair[0])
                at = (a // sub) * 2 * sub + a % sub
                turned[layer * THIRD + b, pl.ds(at * SIDE, SIDE), :] = first
                turned[layer * THIRD + b, pl.ds((at + sub) * SIDE, SIDE), :] = pair[1]
    for group in range(groups):
        for r in range(SIDE):
            pieces = [
                turned[unit, pl.ds(group * 2 * sub * SIDE + r, 2 * sub, stride=SIDE), :]
                for unit in range(layers * THIRD)
            ]
            out_ref[group * SIDE + r] = jnp.concatenate(pieces, axis=1).astype(BF16)


def choose_kernel(devices, rows_ref, in_ref, out_ref):
    layers = rows_ref.shape[0]
    width = in_ref.shape[2] // layers
    half = in_ref.shape[1] // 2
    me = lax.axis_index("star")
    mine = lax.rem(lax.axis_index("dev"), SIDE)
    upper = lax.broadcasted_iota(jnp.int32, (2 * half, width), 0) < half
    for layer in range(layers):
        offset = rows_ref[layer, me]
        base = lax.div(offset, SIDE) + (mine < lax.rem(offset, SIDE)).astype(jnp.int32)
        lanes = slice(layer * width, (layer + 1) * width)
        now = in_ref[lax.rem(base, devices), :, lanes].astype(F32)
        last = now
        for j in range(devices):
            if j < devices - 1:
                after = in_ref[lax.rem(base + j + 1, devices), :, lanes].astype(F32)
                low = pltpu.roll(after, half, axis=0)
            else:
                after, low = None, last
            out_ref[j, :, lanes] = jnp.where(upper, now, low).astype(BF16)
            now = after


def sin_cos(value):
    turns = jnp.floor(value * (2.0 / math.pi) + 0.5)
    rest = value - turns * 1.5703125
    rest = rest - turns * 4.837512969970703125e-4
    rest = rest - turns * 7.549789948768648e-8
    square = rest * rest
    sine = rest + rest * square * (
        -1.6666654611e-1 + square * (8.3321608736e-3 - square * 1.9515295891e-4)
    )
    cosine = (
        1.0
        - 0.5 * square
        + square
        * square
        * (4.166664568298827e-2 + square * (-1.388731625493765e-3 + square * 2.443315711809948e-5))
    )
    quarter = turns.astype(jnp.int32)
    odd = (quarter & 1) == 1
    flip_sine = (quarter & 2) == 2
    flip_cosine = ((quarter + 1) & 2) == 2
    s = jnp.where(odd, cosine, sine)
    c = jnp.where(odd, sine, cosine)
    return jnp.where(flip_sine, -s, s), jnp.where(flip_cosine, -c, c)


def matmul(left, right):
    return lax.dot_general(
        left, right, (((1,), (0,)), ((), ())), preferred_element_type=F32
    )


def spots_kernel(
    stars,
    devices,
    total_tiles,
    rows_ref,
    cols_ref,
    wind_ref,
    owner_ref,
    in_ref,
    amp_ref,
    refs_ref,
    high_ref,
    low_ref,
    down_ref,
    out_ref,
    turned,
    window,
    field,
    first,
    binned,
    table,
):
    steps, layers = wind_ref.shape[0], wind_ref.shape[1]
    across = amp_ref.shape[1] // LANES
    groups = devices // SIDE
    sub = QUART // groups
    me = lax.axis_index("star")
    row = lax.broadcasted_iota(jnp.int32, (SIDE, LANES), 0)
    lane = lax.broadcasted_iota(jnp.int32, (SIDE, LANES), 1)

    refer = refs_ref[owner_ref[0, 0]]
    wide = SIDE * SIDE
    pick_row = lax.broadcasted_iota(jnp.int32, (SIDE, wide), 0)
    pick_lane = lax.broadcasted_iota(jnp.int32, (SIDE, wide), 1)
    pick = (pick_row == ((SIDE - (pick_lane & 15)) & 15)).astype(F32)
    base = lax.dot_general(
        refer,
        pick,
        (((1,), (0,)), ((), ())),
        precision=lax.Precision.HIGHEST,
        preferred_element_type=F32,
    )
    for bit in range(4):
        moved = pltpu.roll(base, 1 << bit, axis=0)
        base = jnp.where(((pick_lane >> (4 + bit)) & 1) == 1, moved, base)
    for q in range(SIDE):
        if q == 0:
            block = base
        else:
            block = jnp.where(
                (pick_lane & 15) >= q,
                pltpu.roll(base, q, axis=1),
                pltpu.roll(base, wide + q - SIDE, axis=1),
            )
        high, low = split(block)
        table[pl.ds(q * SIDE, SIDE), :] = high
        table[pl.ds(wide + q * SIDE, SIDE), :] = high
        table[pl.ds(2 * wide + q * SIDE, SIDE), :] = low

    for x in range(devices):
        seen = in_ref[x].astype(F32)
        for unit in range(layers * THIRD):
            turned[unit, pl.ds(x * 2 * sub, 2 * sub), :] = seen[:, unit * LANES : (unit + 1) * LANES]
    for layer in range(layers):
        part = lax.rem(rows_ref[layer, me], SIDE)
        early = row < part
        for a in range(QUART):
            for b in range(THIRD):
                at = (a // sub) * SIDE * 2 * sub + a % sub
                unit = layer * THIRD + b
                one = turned[unit, pl.ds(at, SIDE, stride=2 * sub), :]
                two = turned[unit, pl.ds(at + sub, SIDE, stride=2 * sub), :]
                slot = layer * SPAN + THIRD * a + b
                window[slot, pl.ds(0, SIDE), :] = one
                window[slot, pl.ds(SIDE, SIDE), :] = jnp.where(early, one, two)
                window[slot, pl.ds(2 * SIDE, SIDE), :] = two

    binned[pl.ds(steps * across * SIDE, binned.shape[0] - steps * across * SIDE), :] = jnp.ones(
        (binned.shape[0] - steps * across * SIDE, LANES), F32
    )

    def one_step(step, carry):
        phase = [None] * across
        for layer in range(layers):
            left = cols_ref[layer, me]
            tile = jnp.minimum(lax.div(left, LANES), total_tiles - SPAN)
            shift = left - tile * LANES + wind_ref[step, layer, 1]
            skip = lax.div(shift, LANES)
            fine = lax.rem(shift, LANES)
            start = lax.rem(rows_ref[layer, me], SIDE) + wind_ref[step, layer, 0]
            inside = lane < LANES - fine
            rolled = [
                pltpu.roll(
                    window[layer * SPAN + skip + t, pl.ds(start, SIDE), :],
                    lax.rem(LANES - fine, LANES),
                    axis=1,
                )
                for t in range(across + 1)
            ]
            for t in range(across):
                value = jnp.where(inside, rolled[t], rolled[t + 1])
                phase[t] = value if phase[t] is None else phase[t] + value
        for t in range(across):
            sine, cosine = sin_cos(phase[t])
            amp = amp_ref[:, t * LANES : (t + 1) * LANES]
            for part, value in enumerate((amp * cosine, amp * sine)):
                high, low = split(value)
                lanes = slice(part * LANES, (part + 1) * LANES)
                field[0, pl.ds(t * SIDE, SIDE), lanes] = high
                field[1, pl.ds(t * SIDE, SIDE), lanes] = low
        first[...] = (
            matmul(field[0], high_ref[...])
            + matmul(field[1], high_ref[...])
            + matmul(field[0], low_ref[...])
        )
        wide_out = first.shape[1] // 2
        for t in range(across):
            rows = pl.ds(t * SIDE, SIDE)
            real_high, real_low = split(first[rows, 0:wide_out])
            imag_high, imag_low = split(first[rows, wide_out : 2 * wide_out])
            stacked = jnp.concatenate(
                [real_high, imag_high, real_low, imag_low, real_high, imag_high], axis=0
            )
            spectrum = matmul(down_ref[...], stacked)
            power = spectrum * spectrum
            total = power[0:SIDE]
            for k in range(1, 2 * BIN):
                total = total + power[k * SIDE : (k + 1) * SIDE]
            small = total[:, 0:LANES]
            for k in range(1, BIN):
                small = small + total[:, k * LANES : (k + 1) * LANES]
            binned[pl.ds((step * across + t) * SIDE, SIDE), :] = small
        return carry

    lax.fori_loop(0, steps, one_step, 0)

    lane8 = lax.broadcasted_iota(jnp.int32, (8, LANES), 1)
    for big in range(binned.shape[0] // LANES):
        flipped = binned[pl.ds(big * LANES, LANES), :].T
        halves = []
        for half in range(2):
            regs = [flipped[(half * 8 + q) * 8 : (half * 8 + q + 1) * 8] for q in range(8)]
            for jump in (4, 2, 1):
                keep = ((lane8 >> 4) & jump) == 0
                for i in range(8):
                    if i & jump == 0:
                        one, two = regs[i], regs[i + jump]
                        regs[i] = jnp.where(keep, one, pltpu.roll(two, jump * SIDE, axis=1))
                        regs[i + jump] = jnp.where(
                            keep, pltpu.roll(one, LANES - jump * SIDE, axis=1), two
                        )
            halves.append(regs)
        image = jnp.concatenate(
            [jnp.concatenate([halves[0][g], halves[1][g]], axis=1) for g in range(8)], axis=0
        )
        image = image / jnp.sum(image, axis=1, keepdims=True)
        high, low = split(image)
        found = matmul(jnp.concatenate([high, low, high], axis=1), table[...])
        count = min(64, steps * across * 8 - big * 64)
        out_ref[pl.ds(big * 64, count), :] = found[0:count]


def shards(screens, foot_rows, foot_cols, wind, amplitude, owner, refs):
    stars, devices = lax.axis_size("star"), lax.axis_size("dev")
    layers, _, side, width = screens.shape
    steps = wind.shape[0]
    tiles = width // LANES
    held = min(SPAN, tiles)
    subs = amplitude.shape[1] // side
    smem = pl.BlockSpec(memory_space=pltpu.SMEM)
    vmem = pl.BlockSpec(memory_space=pltpu.VMEM)
    hbm = pl.BlockSpec(memory_space=pl.ANY)
    crops = pl.pallas_call(
        functools.partial(crop_kernel, stars, devices),
        out_shape=[jax.ShapeDtypeStruct((2 * layers, side, held * LANES), BF16)] * stars,
        in_specs=[smem, smem, hbm],
        out_specs=[vmem] * stars,
        scratch_shapes=[pltpu.SemaphoreType.DMA((stars, 2 * layers))],
        name="crop",
    )(foot_rows, foot_cols, screens)
    parts = [crops[0]]
    for turn in range(1, stars):
        parts.append(
            lax.ppermute(crops[turn], "star", [(i, (i + turn) % stars) for i in range(stars)])
        )
    groups = devices // SIDE
    depth = 2 * QUART // groups
    block = jax.ShapeDtypeStruct((devices, depth, layers * THIRD * LANES), BF16)
    sent = pl.pallas_call(
        functools.partial(spread_kernel, stars, devices, tiles),
        out_shape=block,
        in_specs=[smem, smem] + [vmem] * stars,
        out_specs=vmem,
        scratch_shapes=[pltpu.VMEM((layers * THIRD, 2 * QUART * SIDE, LANES), F32)],
        name="spread",
    )(foot_rows, foot_cols, *parts)
    held_rows = lax.all_to_all(sent, "dev", 0, 0, tiled=True)
    chosen = pl.pallas_call(
        functools.partial(choose_kernel, devices),
        out_shape=block,
        in_specs=[smem, vmem],
        out_specs=vmem,
        name="choose",
    )(foot_rows, held_rows)
    strips = lax.all_to_all(chosen, "dev", 0, 0, tiled=True)
    high, low = across_tables()
    count = steps * subs
    padded = -(-count // 64) * 64
    found = pl.pallas_call(
        functools.partial(spots_kernel, stars, devices, stars * tiles),
        out_shape=jax.ShapeDtypeStruct((count, SIDE * SIDE), F32),
        in_specs=[smem] * 4 + [vmem] * 6,
        out_specs=vmem,
        scratch_shapes=[
            pltpu.VMEM((layers * THIRD, devices * depth, LANES), F32),
            pltpu.VMEM((layers * SPAN, 3 * SIDE, LANES), F32),
            pltpu.VMEM((2, subs // 8 * SIDE, 2 * LANES), BF16),
            pltpu.VMEM((subs // 8 * SIDE, high.shape[1]), F32),
            pltpu.VMEM((padded // 8 * SIDE, LANES), F32),
            pltpu.VMEM((3 * SIDE * SIDE, SIDE * SIDE), BF16),
        ],
        compiler_params=pltpu.CompilerParams(vmem_limit_bytes=48 << 20),
        name="spots",
    )(foot_rows, foot_cols, wind, owner, strips, amplitude, refs, high, low, down_table())
    return found.reshape(steps, 1, 1, subs, SIDE * SIDE)


def solution(mesh):
    in_specs = (P(None, None, "dev", "star"), P(), P(), P(), P("dev", None), P("star", "dev"), P())
    out_specs = P(None, "star", "dev", None, None)
    return jax.shard_map(shards, mesh=mesh, in_specs=in_specs, out_specs=out_specs, check_vma=False)
```

```python
import functools
import math

import jax
import jax.numpy as jnp
import numpy as np
from jax import lax
from jax.experimental import pallas as pl
from jax.experimental.pallas import tpu as pltpu
from jax.sharding import PartitionSpec as P

BIN = 4
SIDE = 16
LANES = 128
SPAN = 12
QUART = 4
THIRD = SPAN // QUART

F32 = jnp.float32
BF16 = jnp.bfloat16


def split_np(table):
    high = table.astype(jnp.bfloat16)
    low = (table - high.astype(np.float64)).astype(jnp.bfloat16)
    return high, low


def split(value):
    high = value.astype(BF16)
    return high, (value - high.astype(F32)).astype(BF16)


def across_tables():
    length = BIN * SIDE
    freq = (np.arange(length) + length // 2) % length
    angle = 2.0 * math.pi * (np.outer(np.arange(SIDE), freq) % length) / length
    real, imag = np.cos(angle), -np.sin(angle)
    out = np.zeros((2, 8, SIDE, 2, BIN, SIDE, 8))
    for i in range(8):
        for b in range(BIN):
            re, im = real[:, b::BIN], imag[:, b::BIN]
            out[0, i, :, 0, b, :, i] = re
            out[1, i, :, 0, b, :, i] = -im
            out[0, i, :, 1, b, :, i] = im
            out[1, i, :, 1, b, :, i] = re
    return split_np(out.reshape(2 * 8 * SIDE, 2 * BIN * SIDE * 8))


def down_table():
    length = BIN * SIDE
    freq = (np.arange(length) + length // 2) % length
    angle = 2.0 * math.pi * (np.outer(freq, np.arange(SIDE)) % length) / length
    real, imag = np.cos(angle), -np.sin(angle)
    order = np.concatenate([np.arange(a, length, BIN) for a in range(BIN)])
    real, imag = real[order], imag[order]
    table = np.block([[real, -imag], [imag, real]])
    high, low = split_np(table)
    return np.concatenate([high, high, low], axis=1)


def place_of(rows_ref, cols_ref, layer, star, devices, total_tiles):
    offset = rows_ref[star, layer]
    strip = lax.div(offset, SIDE)
    part = lax.rem(offset, SIDE)
    tile = jnp.minimum(lax.div(cols_ref[star, layer], LANES), total_tiles - SPAN)
    return strip, part, tile


def first_tile(tile, panel, tiles, held):
    return jnp.clip(tile - panel * tiles, 0, tiles - held)


def crop_kernel(stars, devices, rows_ref, cols_ref, screens_ref, *rest):
    outs, sem = rest[:stars], rest[stars]
    layers, bands, side, width = screens_ref.shape
    tiles = width // LANES
    held = min(SPAN, tiles)
    me = lax.axis_index("star")
    place = lax.axis_index("dev")
    copies = []
    for turn in range(stars):
        star = lax.rem(me + turn, stars)
        for layer in range(layers):
            strip, _, tile = place_of(rows_ref, cols_ref, layer, star, devices, stars * tiles)
            behind = lax.rem(place + bands * devices - strip, devices)
            band = lax.div(strip + behind, devices)
            start = first_tile(tile, me, tiles, held)
            columns = pl.ds(pl.multiple_of(start * LANES, LANES), held * LANES)
            for slot in range(2):
                copy = pltpu.make_async_copy(
                    screens_ref.at[layer, lax.rem(band + slot, bands), :, columns],
                    outs[turn].at[2 * layer + slot],
                    sem.at[turn, 2 * layer + slot],
                )
                copy.start()
                copies.append(copy)
    for copy in copies:
        copy.wait()


def spread_kernel(stars, devices, tiles, rows_ref, cols_ref, *rest):
    parts, out_ref, turned = rest[:stars], rest[stars], rest[stars + 1]
    layers = parts[0].shape[0] // 2
    held = parts[0].shape[2] // LANES
    groups = devices // SIDE
    sub = QUART // groups
    me = lax.axis_index("star")
    place = lax.axis_index("dev")
    row = lax.broadcasted_iota(jnp.int32, (SIDE, LANES), 0)
    for layer in range(layers):
        strip, part, tile = place_of(rows_ref, cols_ref, layer, me, devices, stars * tiles)
        behind = lax.rem(place + (1 << 20) * devices - strip, devices)
        bound = jnp.where(behind == 0, part, 0)
        wraps = row < bound
        for a in range(QUART):
            for b in range(THIRD):
                spot = tile + (THIRD * a + b)
                panel = lax.div(spot, tiles)
                pair = []
                for slot in range(2):
                    value = None
                    for turn in range(stars):
                        sender = lax.rem(me + stars - turn, stars)
                        start = first_tile(tile, sender, tiles, held)
                        local = jnp.clip(spot - sender * tiles - start, 0, held - 1)
                        lanes = pl.ds(pl.multiple_of(local * LANES, LANES), LANES)
                        seen = parts[turn][2 * layer + slot, :, lanes].astype(F32)
                        if value is None:
                            value = seen
                        else:
                            value = jnp.where(panel == sender, seen, value)
                    pair.append(value)
                first = jnp.where(wraps, pair[1], pair[0])
                at = (a // sub) * 2 * sub + a % sub
                turned[layer * THIRD + b, pl.ds(at * SIDE, SIDE), :] = first
                turned[layer * THIRD + b, pl.ds((at + sub) * SIDE, SIDE), :] = pair[1]
    for group in range(groups):
        for r in range(SIDE):
            pieces = [
                turned[unit, pl.ds(group * 2 * sub * SIDE + r, 2 * sub, stride=SIDE), :]
                for unit in range(layers * THIRD)
            ]
            out_ref[group * SIDE + r] = jnp.concatenate(pieces, axis=1).astype(BF16)


def choose_kernel(devices, rows_ref, in_ref, out_ref):
    layers = rows_ref.shape[1]
    width = in_ref.shape[2] // layers
    half = in_ref.shape[1] // 2
    me = lax.axis_index("star")
    mine = lax.rem(lax.axis_index("dev"), SIDE)
    upper = lax.broadcasted_iota(jnp.int32, (2 * half, width), 0) < half
    for layer in range(layers):
        offset = rows_ref[me, layer]
        base = lax.div(offset, SIDE) + (mine < lax.rem(offset, SIDE)).astype(jnp.int32)
        lanes = slice(layer * width, (layer + 1) * width)
        now = in_ref[lax.rem(base, devices), :, lanes].astype(F32)
        last = now
        for j in range(devices):
            if j < devices - 1:
                after = in_ref[lax.rem(base + j + 1, devices), :, lanes].astype(F32)
                low = pltpu.roll(after, half, axis=0)
            else:
                after, low = None, last
            out_ref[j, :, lanes] = jnp.where(upper, now, low).astype(BF16)
            now = after


def sin_cos(value):
    turns = jnp.floor(value * (2.0 / math.pi) + 0.5)
    rest = value - turns * 1.5703125
    rest = rest - turns * 4.837512969970703125e-4
    rest = rest - turns * 7.549789948768648e-8
    square = rest * rest
    sine = rest + rest * square * (
        -1.6666654611e-1 + square * (8.3321608736e-3 - square * 1.9515295891e-4)
    )
    cosine = (
        1.0
        - 0.5 * square
        + square
        * square
        * (4.166664568298827e-2 + square * (-1.388731625493765e-3 + square * 2.443315711809948e-5))
    )
    quarter = turns.astype(jnp.int32)
    odd = (quarter & 1) == 1
    flip_sine = (quarter & 2) == 2
    flip_cosine = ((quarter + 1) & 2) == 2
    s = jnp.where(odd, cosine, sine)
    c = jnp.where(odd, sine, cosine)
    return jnp.where(flip_sine, -s, s), jnp.where(flip_cosine, -c, c)


def matmul(left, right):
    return lax.dot_general(
        left, right, (((1,), (0,)), ((), ())), preferred_element_type=F32
    )


def table_kernel(owner_ref, refs_ref, table):
    refer = refs_ref[owner_ref[0, 0]]
    wide = SIDE * SIDE
    pick_row = lax.broadcasted_iota(jnp.int32, (SIDE, wide), 0)
    pick_lane = lax.broadcasted_iota(jnp.int32, (SIDE, wide), 1)
    pick = (pick_row == ((SIDE - (pick_lane & 15)) & 15)).astype(F32)
    base = lax.dot_general(
        refer,
        pick,
        (((1,), (0,)), ((), ())),
        precision=lax.Precision.HIGHEST,
        preferred_element_type=F32,
    )
    for bit in range(4):
        moved = pltpu.roll(base, 1 << bit, axis=0)
        base = jnp.where(((pick_lane >> (4 + bit)) & 1) == 1, moved, base)
    for q in range(SIDE):
        if q == 0:
            block = base
        else:
            block = jnp.where(
                (pick_lane & 15) >= q,
                pltpu.roll(base, q, axis=1),
                pltpu.roll(base, wide + q - SIDE, axis=1),
            )
        high, low = split(block)
        table[pl.ds(q * SIDE, SIDE), :] = high
        table[pl.ds(wide + q * SIDE, SIDE), :] = high
        table[pl.ds(2 * wide + q * SIDE, SIDE), :] = low


def spots_kernel(
    stars,
    devices,
    total_tiles,
    rows_ref,
    cols_ref,
    wind_ref,
    in_ref,
    amp_ref,
    table,
    high_ref,
    low_ref,
    down_ref,
    out_ref,
    turned,
    window,
    field,
    first,
    binned,
):
    steps, layers = wind_ref.shape[0], wind_ref.shape[2]
    across = amp_ref.shape[1] // LANES
    groups = devices // SIDE
    sub = QUART // groups
    me = lax.axis_index("star")
    row = lax.broadcasted_iota(jnp.int32, (SIDE, LANES), 0)
    lane = lax.broadcasted_iota(jnp.int32, (SIDE, LANES), 1)

    for x in range(devices):
        seen = in_ref[x].astype(F32)
        for unit in range(layers * THIRD):
            turned[unit, pl.ds(x * 2 * sub, 2 * sub), :] = seen[:, unit * LANES : (unit + 1) * LANES]
    for layer in range(layers):
        part = lax.rem(rows_ref[me, layer], SIDE)
        early = row < part
        for a in range(QUART):
            for b in range(THIRD):
                at = (a // sub) * SIDE * 2 * sub + a % sub
                unit = layer * THIRD + b
                one = turned[unit, pl.ds(at, SIDE, stride=2 * sub), :]
                two = turned[unit, pl.ds(at + sub, SIDE, stride=2 * sub), :]
                slot = layer * SPAN + THIRD * a + b
                window[slot, pl.ds(0, SIDE), :] = one
                window[slot, pl.ds(SIDE, SIDE), :] = jnp.where(early, one, two)
                window[slot, pl.ds(2 * SIDE, SIDE), :] = two

    binned[pl.ds(steps * across * SIDE, binned.shape[0] - steps * across * SIDE), :] = jnp.ones(
        (binned.shape[0] - steps * across * SIDE, LANES), F32
    )

    def one_step(step, carry):
        phase = [None] * across
        for layer in range(layers):
            left = cols_ref[me, layer]
            tile = jnp.minimum(lax.div(left, LANES), total_tiles - SPAN)
            shift = left - tile * LANES + wind_ref[step, 1, layer]
            skip = lax.div(shift, LANES)
            fine = lax.rem(shift, LANES)
            start = lax.rem(rows_ref[me, layer], SIDE) + wind_ref[step, 0, layer]
            inside = lane < LANES - fine
            rolled = [
                pltpu.roll(
                    window[layer * SPAN + skip + t, pl.ds(start, SIDE), :],
                    lax.rem(LANES - fine, LANES),
                    axis=1,
                )
                for t in range(across + 1)
            ]
            for t in range(across):
                value = jnp.where(inside, rolled[t], rolled[t + 1])
                phase[t] = value if phase[t] is None else phase[t] + value
        for t in range(across):
            sine, cosine = sin_cos(phase[t])
            amp = amp_ref[:, t * LANES : (t + 1) * LANES]
            for part, value in enumerate((amp * cosine, amp * sine)):
                high, low = split(value)
                lanes = slice(part * LANES, (part + 1) * LANES)
                field[0, pl.ds(t * SIDE, SIDE), lanes] = high
                field[1, pl.ds(t * SIDE, SIDE), lanes] = low
        first[...] = (
            matmul(field[0], high_ref[...])
            + matmul(field[1], high_ref[...])
            + matmul(field[0], low_ref[...])
        )
        wide_out = first.shape[1] // 2
        for t in range(across):
            rows = pl.ds(t * SIDE, SIDE)
            real_high, real_low = split(first[rows, 0:wide_out])
            imag_high, imag_low = split(first[rows, wide_out : 2 * wide_out])
            stacked = jnp.concatenate(
                [real_high, imag_high, real_low, imag_low, real_high, imag_high], axis=0
            )
            spectrum = matmul(down_ref[...], stacked)
            power = spectrum * spectrum
            total = power[0:SIDE]
            for k in range(1, 2 * BIN):
                total = total + power[k * SIDE : (k + 1) * SIDE]
            small = total[:, 0:LANES]
            for k in range(1, BIN):
                small = small + total[:, k * LANES : (k + 1) * LANES]
            binned[pl.ds((step * across + t) * SIDE, SIDE), :] = small
        return carry

    lax.fori_loop(0, steps, one_step, 0)

    lane8 = lax.broadcasted_iota(jnp.int32, (8, LANES), 1)
    for big in range(binned.shape[0] // LANES):
        flipped = binned[pl.ds(big * LANES, LANES), :].T
        halves = []
        for half in range(2):
            regs = [flipped[(half * 8 + q) * 8 : (half * 8 + q + 1) * 8] for q in range(8)]
            for jump in (4, 2, 1):
                keep = ((lane8 >> 4) & jump) == 0
                for i in range(8):
                    if i & jump == 0:
                        one, two = regs[i], regs[i + jump]
                        regs[i] = jnp.where(keep, one, pltpu.roll(two, jump * SIDE, axis=1))
                        regs[i + jump] = jnp.where(
                            keep, pltpu.roll(one, LANES - jump * SIDE, axis=1), two
                        )
            halves.append(regs)
        image = jnp.concatenate(
            [jnp.concatenate([halves[0][g], halves[1][g]], axis=1) for g in range(8)], axis=0
        )
        image = image / jnp.sum(image, axis=1, keepdims=True)
        high, low = split(image)
        found = matmul(jnp.concatenate([high, low, high], axis=1), table[...])
        count = min(64, steps * across * 8 - big * 64)
        out_ref[pl.ds(big * 64, count), :] = found[0:count]


def shards(screens, foot_rows, foot_cols, wind, amplitude, owner, refs):
    stars, devices = lax.axis_size("star"), lax.axis_size("dev")
    layers, _, side, width = screens.shape
    steps = wind.shape[0]
    foot_rows, foot_cols = foot_rows.T, foot_cols.T
    wind = wind.transpose(0, 2, 1)
    tiles = width // LANES
    held = min(SPAN, tiles)
    subs = amplitude.shape[1] // side
    smem = pl.BlockSpec(memory_space=pltpu.SMEM)
    vmem = pl.BlockSpec(memory_space=pltpu.VMEM)
    hbm = pl.BlockSpec(memory_space=pltpu.HBM)
    screens = pltpu.with_memory_space_constraint(screens, pltpu.HBM)
    crops = pl.pallas_call(
        functools.partial(crop_kernel, stars, devices),
        out_shape=[jax.ShapeDtypeStruct((2 * layers, side, held * LANES), BF16)] * stars,
        in_specs=[smem, smem, hbm],
        out_specs=[vmem] * stars,
        scratch_shapes=[pltpu.SemaphoreType.DMA((stars, 2 * layers))],
        compiler_params=pltpu.CompilerParams(vmem_limit_bytes=2 << 20),
        name="crop",
    )(foot_rows, foot_cols, screens)
    parts = [crops[0]]
    for turn in range(1, stars):
        parts.append(
            lax.ppermute(crops[turn], "star", [(i, (i + turn) % stars) for i in range(stars)])
        )
    groups = devices // SIDE
    depth = 2 * QUART // groups
    block = jax.ShapeDtypeStruct((devices, depth, layers * THIRD * LANES), BF16)
    sent = pl.pallas_call(
        functools.partial(spread_kernel, stars, devices, tiles),
        out_shape=block,
        in_specs=[smem, smem] + [vmem] * stars,
        out_specs=vmem,
        scratch_shapes=[pltpu.VMEM((layers * THIRD, 2 * QUART * SIDE, LANES), F32)],
        compiler_params=pltpu.CompilerParams(vmem_limit_bytes=4 << 20),
        name="spread",
    )(foot_rows, foot_cols, *parts)
    held_rows = lax.all_to_all(sent, "dev", 0, 0, tiled=True)
    chosen = pl.pallas_call(
        functools.partial(choose_kernel, devices),
        out_shape=block,
        in_specs=[smem, vmem],
        out_specs=vmem,
        compiler_params=pltpu.CompilerParams(vmem_limit_bytes=2 << 20),
        name="choose",
    )(foot_rows, held_rows)
    strips = lax.all_to_all(chosen, "dev", 0, 0, tiled=True)
    wide = SIDE * SIDE
    table = pl.pallas_call(
        table_kernel,
        out_shape=jax.ShapeDtypeStruct((3 * wide, wide), BF16),
        in_specs=[smem, vmem],
        out_specs=vmem,
        compiler_params=pltpu.CompilerParams(vmem_limit_bytes=2 << 20),
        name="table",
    )(owner, refs)
    high, low = across_tables()
    count = steps * subs
    padded = -(-count // 64) * 64
    found = pl.pallas_call(
        functools.partial(spots_kernel, stars, devices, stars * tiles),
        out_shape=jax.ShapeDtypeStruct((count, SIDE * SIDE), F32),
        in_specs=[smem] * 3 + [vmem] * 6,
        out_specs=vmem,
        scratch_shapes=[
            pltpu.VMEM((layers * THIRD, devices * depth, LANES), F32),
            pltpu.VMEM((layers * SPAN, 3 * SIDE, LANES), F32),
            pltpu.VMEM((2, subs // 8 * SIDE, 2 * LANES), BF16),
            pltpu.VMEM((subs // 8 * SIDE, high.shape[1]), F32),
            pltpu.VMEM((padded // 8 * SIDE, LANES), F32),
        ],
        compiler_params=pltpu.CompilerParams(vmem_limit_bytes=16 << 20),
        name="spots",
    )(foot_rows, foot_cols, wind, strips, amplitude, table, high, low, down_table())
    return found.reshape(steps, 1, 1, subs, SIDE * SIDE)


def solution(mesh):
    in_specs = (P(None, None, "dev", "star"), P(), P(), P(), P("dev", None), P("star", "dev"), P())
    out_specs = P(None, "star", "dev", None, None)
    return jax.shard_map(shards, mesh=mesh, in_specs=in_specs, out_specs=out_specs, check_vma=False)
```

```python
import functools
import math

import jax
import jax.numpy as jnp
import numpy as np
from jax import lax
from jax.experimental import pallas as pl
from jax.experimental.pallas import tpu as pltpu
from jax.sharding import PartitionSpec as P

BIN = 4
SIDE = 16
LANES = 128
SPAN = 12
QUART = 4
THIRD = SPAN // QUART

F32 = jnp.float32
BF16 = jnp.bfloat16


def split_np(table):
    high = table.astype(jnp.bfloat16)
    low = (table - high.astype(np.float64)).astype(jnp.bfloat16)
    return high, low


def split(value):
    high = value.astype(BF16)
    return high, (value - high.astype(F32)).astype(BF16)


def across_tables():
    length = BIN * SIDE
    freq = (np.arange(length) + length // 2) % length
    angle = 2.0 * math.pi * (np.outer(np.arange(SIDE), freq) % length) / length
    real, imag = np.cos(angle), -np.sin(angle)
    out = np.zeros((2, 8, SIDE, 2, BIN, SIDE, 8))
    for i in range(8):
        for b in range(BIN):
            re, im = real[:, b::BIN], imag[:, b::BIN]
            out[0, i, :, 0, b, :, i] = re
            out[1, i, :, 0, b, :, i] = -im
            out[0, i, :, 1, b, :, i] = im
            out[1, i, :, 1, b, :, i] = re
    return split_np(out.reshape(2 * 8 * SIDE, 2 * BIN * SIDE * 8))


def down_table():
    length = BIN * SIDE
    freq = (np.arange(length) + length // 2) % length
    angle = 2.0 * math.pi * (np.outer(freq, np.arange(SIDE)) % length) / length
    real, imag = np.cos(angle), -np.sin(angle)
    order = np.concatenate([np.arange(a, length, BIN) for a in range(BIN)])
    real, imag = real[order], imag[order]
    table = np.block([[real, -imag], [imag, real]])
    high, low = split_np(table)
    return np.concatenate([high, high, low], axis=1)


def place_of(rows_ref, cols_ref, layer, star, devices, total_tiles):
    offset = rows_ref[star, layer]
    strip = lax.div(offset, SIDE)
    part = lax.rem(offset, SIDE)
    tile = jnp.minimum(lax.div(cols_ref[star, layer], LANES), total_tiles - SPAN)
    return strip, part, tile


def first_tile(tile, panel, tiles, held):
    return jnp.clip(tile - panel * tiles, 0, tiles - held)


def crop_kernel(stars, devices, rows_hbm, cols_hbm, screens_ref, *rest):
    outs, (sem, rows_ref, cols_ref, scalar_sem) = rest[:stars], rest[stars:]
    scalars = [
        pltpu.make_async_copy(rows_hbm, rows_ref, scalar_sem.at[0]),
        pltpu.make_async_copy(cols_hbm, cols_ref, scalar_sem.at[1]),
    ]
    for copy in scalars:
        copy.start()
    for copy in scalars:
        copy.wait()
    layers, bands, side, width = screens_ref.shape
    tiles = width // LANES
    held = min(SPAN, tiles)
    me = lax.axis_index("star")
    place = lax.axis_index("dev")
    copies = []
    for turn in range(stars):
        star = lax.rem(me + turn, stars)
        for layer in range(layers):
            strip, _, tile = place_of(rows_ref, cols_ref, layer, star, devices, stars * tiles)
            behind = lax.rem(place + bands * devices - strip, devices)
            band = lax.div(strip + behind, devices)
            start = first_tile(tile, me, tiles, held)
            columns = pl.ds(pl.multiple_of(start * LANES, LANES), held * LANES)
            for slot in range(2):
                copy = pltpu.make_async_copy(
                    screens_ref.at[layer, lax.rem(band + slot, bands), :, columns],
                    outs[turn].at[2 * layer + slot],
                    sem.at[turn, 2 * layer + slot],
                )
                copy.start()
                copies.append(copy)
    for copy in copies:
        copy.wait()


def spread_kernel(stars, devices, tiles, rows_ref, cols_ref, *rest):
    parts, out_ref, turned = rest[:stars], rest[stars], rest[stars + 1]
    layers = parts[0].shape[0] // 2
    held = parts[0].shape[2] // LANES
    groups = devices // SIDE
    sub = QUART // groups
    me = lax.axis_index("star")
    place = lax.axis_index("dev")
    row = lax.broadcasted_iota(jnp.int32, (SIDE, LANES), 0)
    for layer in range(layers):
        strip, part, tile = place_of(rows_ref, cols_ref, layer, me, devices, stars * tiles)
        behind = lax.rem(place + (1 << 20) * devices - strip, devices)
        bound = jnp.where(behind == 0, part, 0)
        wraps = row < bound
        for a in range(QUART):
            for b in range(THIRD):
                spot = tile + (THIRD * a + b)
                panel = lax.div(spot, tiles)
                pair = []
                for slot in range(2):
                    value = None
                    for turn in range(stars):
                        sender = lax.rem(me + stars - turn, stars)
                        start = first_tile(tile, sender, tiles, held)
                        local = jnp.clip(spot - sender * tiles - start, 0, held - 1)
                        lanes = pl.ds(pl.multiple_of(local * LANES, LANES), LANES)
                        seen = parts[turn][2 * layer + slot, :, lanes].astype(F32)
                        if value is None:
                            value = seen
                        else:
                            value = jnp.where(panel == sender, seen, value)
                    pair.append(value)
                first = jnp.where(wraps, pair[1], pair[0])
                at = (a // sub) * 2 * sub + a % sub
                turned[layer * THIRD + b, pl.ds(at * SIDE, SIDE), :] = first
                turned[layer * THIRD + b, pl.ds((at + sub) * SIDE, SIDE), :] = pair[1]
    for group in range(groups):
        for r in range(SIDE):
            pieces = [
                turned[unit, pl.ds(group * 2 * sub * SIDE + r, 2 * sub, stride=SIDE), :]
                for unit in range(layers * THIRD)
            ]
            out_ref[group * SIDE + r] = jnp.concatenate(pieces, axis=1).astype(BF16)


def choose_kernel(devices, rows_ref, in_ref, out_ref):
    layers = rows_ref.shape[1]
    width = in_ref.shape[2] // layers
    half = in_ref.shape[1] // 2
    me = lax.axis_index("star")
    mine = lax.rem(lax.axis_index("dev"), SIDE)
    upper = lax.broadcasted_iota(jnp.int32, (2 * half, width), 0) < half
    for layer in range(layers):
        offset = rows_ref[me, layer]
        base = lax.div(offset, SIDE) + (mine < lax.rem(offset, SIDE)).astype(jnp.int32)
        lanes = slice(layer * width, (layer + 1) * width)
        now = in_ref[lax.rem(base, devices), :, lanes].astype(F32)
        last = now
        for j in range(devices):
            if j < devices - 1:
                after = in_ref[lax.rem(base + j + 1, devices), :, lanes].astype(F32)
                low = pltpu.roll(after, half, axis=0)
            else:
                after, low = None, last
            out_ref[j, :, lanes] = jnp.where(upper, now, low).astype(BF16)
            now = after


def sin_cos(value):
    turns = jnp.floor(value * (2.0 / math.pi) + 0.5)
    rest = value - turns * 1.5703125
    rest = rest - turns * 4.837512969970703125e-4
    rest = rest - turns * 7.549789948768648e-8
    square = rest * rest
    sine = rest + rest * square * (
        -1.6666654611e-1 + square * (8.3321608736e-3 - square * 1.9515295891e-4)
    )
    cosine = (
        1.0
        - 0.5 * square
        + square
        * square
        * (4.166664568298827e-2 + square * (-1.388731625493765e-3 + square * 2.443315711809948e-5))
    )
    quarter = turns.astype(jnp.int32)
    odd = (quarter & 1) == 1
    flip_sine = (quarter & 2) == 2
    flip_cosine = ((quarter + 1) & 2) == 2
    s = jnp.where(odd, cosine, sine)
    c = jnp.where(odd, sine, cosine)
    return jnp.where(flip_sine, -s, s), jnp.where(flip_cosine, -c, c)


def matmul(left, right):
    return lax.dot_general(
        left, right, (((1,), (0,)), ((), ())), preferred_element_type=F32
    )


def table_kernel(owner_ref, refs_ref, table):
    refer = refs_ref[owner_ref[0, 0]]
    wide = SIDE * SIDE
    pick_row = lax.broadcasted_iota(jnp.int32, (SIDE, wide), 0)
    pick_lane = lax.broadcasted_iota(jnp.int32, (SIDE, wide), 1)
    pick = (pick_row == ((SIDE - (pick_lane & 15)) & 15)).astype(F32)
    base = lax.dot_general(
        refer,
        pick,
        (((1,), (0,)), ((), ())),
        precision=lax.Precision.HIGHEST,
        preferred_element_type=F32,
    )
    for bit in range(4):
        moved = pltpu.roll(base, 1 << bit, axis=0)
        base = jnp.where(((pick_lane >> (4 + bit)) & 1) == 1, moved, base)
    for q in range(SIDE):
        if q == 0:
            block = base
        else:
            block = jnp.where(
                (pick_lane & 15) >= q,
                pltpu.roll(base, q, axis=1),
                pltpu.roll(base, wide + q - SIDE, axis=1),
            )
        high, low = split(block)
        table[pl.ds(q * SIDE, SIDE), :] = high
        table[pl.ds(wide + q * SIDE, SIDE), :] = high
        table[pl.ds(2 * wide + q * SIDE, SIDE), :] = low


def spots_kernel(
    stars,
    devices,
    total_tiles,
    rows_ref,
    cols_ref,
    wind_ref,
    in_ref,
    amp_ref,
    table,
    across_ref,
    down_ref,
    out_ref,
    turned,
    window,
    field,
    first,
    binned,
    images,
):
    steps, layers = wind_ref.shape[0], wind_ref.shape[2]
    across = amp_ref.shape[1] // LANES
    groups = devices // SIDE
    sub = QUART // groups
    me = lax.axis_index("star")
    row = lax.broadcasted_iota(jnp.int32, (SIDE, LANES), 0)
    lane = lax.broadcasted_iota(jnp.int32, (SIDE, LANES), 1)

    for x in range(devices):
        seen = in_ref[x].astype(F32)
        for unit in range(layers * THIRD):
            turned[unit, pl.ds(x * 2 * sub, 2 * sub), :] = seen[:, unit * LANES : (unit + 1) * LANES]
    for layer in range(layers):
        part = lax.rem(rows_ref[me, layer], SIDE)
        early = row < part
        for a in range(QUART):
            for b in range(THIRD):
                at = (a // sub) * SIDE * 2 * sub + a % sub
                unit = layer * THIRD + b
                one = turned[unit, pl.ds(at, SIDE, stride=2 * sub), :]
                two = turned[unit, pl.ds(at + sub, SIDE, stride=2 * sub), :]
                slot = layer * SPAN + THIRD * a + b
                window[slot, pl.ds(0, SIDE), :] = one
                window[slot, pl.ds(SIDE, SIDE), :] = jnp.where(early, one, two)
                window[slot, pl.ds(2 * SIDE, SIDE), :] = two

    binned[pl.ds(steps * across * SIDE, binned.shape[0] - steps * across * SIDE), :] = jnp.ones(
        (binned.shape[0] - steps * across * SIDE, LANES), F32
    )

    for step in range(steps):
        phase = [None] * across
        for layer in range(layers):
            left = cols_ref[me, layer]
            tile = jnp.minimum(lax.div(left, LANES), total_tiles - SPAN)
            shift = left - tile * LANES + wind_ref[step, 1, layer]
            skip = lax.div(shift, LANES)
            fine = lax.rem(shift, LANES)
            start = lax.rem(rows_ref[me, layer], SIDE) + wind_ref[step, 0, layer]
            inside = lane < LANES - fine
            rolled = [
                pltpu.roll(
                    window[layer * SPAN + skip + t, pl.ds(start, SIDE), :],
                    lax.rem(LANES - fine, LANES),
                    axis=1,
                )
                for t in range(across + 1)
            ]
            for t in range(across):
                value = jnp.where(inside, rolled[t], rolled[t + 1])
                phase[t] = value if phase[t] is None else phase[t] + value
        for t in range(across):
            sine, cosine = sin_cos(phase[t])
            amp = amp_ref[:, t * LANES : (t + 1) * LANES]
            rows = pl.ds((step * across + t) * SIDE, SIDE)
            for part, value in enumerate((amp * cosine, amp * sine)):
                high, low = split(value)
                at = part * LANES
                field[rows, at : at + LANES] = high
                field[rows, at + 2 * LANES : at + 3 * LANES] = low
                field[rows, at + 4 * LANES : at + 5 * LANES] = high

    first[...] = matmul(field[...], across_ref[...])

    wide_out = first.shape[1] // 2

    for turn in range(steps * across):
        rows = pl.ds(turn * SIDE, SIDE)
        real_high, real_low = split(first[rows, 0:wide_out])
        imag_high, imag_low = split(first[rows, wide_out : 2 * wide_out])
        stacked = jnp.concatenate(
            [real_high, imag_high, real_low, imag_low, real_high, imag_high], axis=0
        )
        spectrum = matmul(down_ref[...], stacked)
        power = spectrum * spectrum
        total = power[0:SIDE]
        for k in range(1, 2 * BIN):
            total = total + power[k * SIDE : (k + 1) * SIDE]
        small = total[:, 0:LANES]
        for k in range(1, BIN):
            small = small + total[:, k * LANES : (k + 1) * LANES]
        binned[rows, :] = small

    lane8 = lax.broadcasted_iota(jnp.int32, (8, LANES), 1)
    for big in range(binned.shape[0] // LANES):
        flipped = binned[pl.ds(big * LANES, LANES), :].T
        halves = []
        for half in range(2):
            regs = [flipped[(half * 8 + q) * 8 : (half * 8 + q + 1) * 8] for q in range(8)]
            for jump in (4, 2, 1):
                keep = ((lane8 >> 4) & jump) == 0
                for i in range(8):
                    if i & jump == 0:
                        one, two = regs[i], regs[i + jump]
                        regs[i] = jnp.where(keep, one, pltpu.roll(two, jump * SIDE, axis=1))
                        regs[i + jump] = jnp.where(
                            keep, pltpu.roll(one, LANES - jump * SIDE, axis=1), two
                        )
            halves.append(regs)
        image = jnp.concatenate(
            [jnp.concatenate([halves[0][g], halves[1][g]], axis=1) for g in range(8)], axis=0
        )
        image = image / jnp.sum(image, axis=1, keepdims=True)
        high, low = split(image)
        rows = pl.ds(big * 64, 64)
        wide = SIDE * SIDE
        images[rows, 0:wide] = high
        images[rows, wide : 2 * wide] = low
        images[rows, 2 * wide : 3 * wide] = high
    out_ref[...] = matmul(images[...], table[...])[0 : out_ref.shape[0]]


def spots_call(stars, devices, total_tiles, foot_rows, foot_cols, wind, strips, amplitude, table):
    smem = pl.BlockSpec(memory_space=pltpu.SMEM)
    vmem = pl.BlockSpec(memory_space=pltpu.VMEM)
    steps, layers = wind.shape[0], wind.shape[2]
    depth = strips.shape[1]
    subs = amplitude.shape[1] // SIDE
    high, low = across_tables()
    table_across = np.concatenate([high, high, low], axis=0)
    count = steps * subs
    padded = -(-count // 64) * 64
    return pl.pallas_call(
        functools.partial(spots_kernel, stars, devices, total_tiles),
        out_shape=jax.ShapeDtypeStruct((count, SIDE * SIDE), F32),
        in_specs=[smem] * 3 + [vmem] * 5,
        out_specs=vmem,
        scratch_shapes=[
            pltpu.VMEM((layers * THIRD, devices * depth, LANES), F32),
            pltpu.VMEM((layers * SPAN, 3 * SIDE, LANES), F32),
            pltpu.VMEM((count // 8 * SIDE, 6 * LANES), BF16),
            pltpu.VMEM((count // 8 * SIDE, high.shape[1]), F32),
            pltpu.VMEM((padded // 8 * SIDE, LANES), F32),
            pltpu.VMEM((padded, 3 * SIDE * SIDE), BF16),
        ],
        compiler_params=pltpu.CompilerParams(vmem_limit_bytes=16 << 20),
        name="spots",
    )(foot_rows, foot_cols, wind, strips, amplitude, table, table_across, down_table())


def shards(screens, foot_rows, foot_cols, wind, amplitude, owner, refs):
    stars, devices = lax.axis_size("star"), lax.axis_size("dev")
    layers, _, side, width = screens.shape
    steps = wind.shape[0]
    foot_rows, foot_cols = foot_rows.T, foot_cols.T
    wind = wind.transpose(0, 2, 1)
    tiles = width // LANES
    held = min(SPAN, tiles)
    subs = amplitude.shape[1] // side
    smem = pl.BlockSpec(memory_space=pltpu.SMEM)
    vmem = pl.BlockSpec(memory_space=pltpu.VMEM)
    hbm = pl.BlockSpec(memory_space=pltpu.HBM)
    screens = pltpu.with_memory_space_constraint(screens, pltpu.HBM)
    crops = pl.pallas_call(
        functools.partial(crop_kernel, stars, devices),
        out_shape=[jax.ShapeDtypeStruct((2 * layers, side, held * LANES), BF16)] * stars,
        in_specs=[hbm] * 3,
        out_specs=[vmem] * stars,
        scratch_shapes=[
            pltpu.SemaphoreType.DMA((stars, 2 * layers)),
            pltpu.SMEM(foot_rows.shape, jnp.int32),
            pltpu.SMEM(foot_cols.shape, jnp.int32),
            pltpu.SemaphoreType.DMA((2,)),
        ],
        compiler_params=pltpu.CompilerParams(vmem_limit_bytes=2 << 20),
        name="crop",
    )(
        pltpu.with_memory_space_constraint(foot_rows, pltpu.HBM),
        pltpu.with_memory_space_constraint(foot_cols, pltpu.HBM),
        screens,
    )
    parts = [crops[0]]
    for turn in range(1, stars):
        parts.append(
            lax.ppermute(crops[turn], "star", [(i, (i + turn) % stars) for i in range(stars)])
        )
    groups = devices // SIDE
    depth = 2 * QUART // groups
    block = jax.ShapeDtypeStruct((devices, depth, layers * THIRD * LANES), BF16)
    sent = pl.pallas_call(
        functools.partial(spread_kernel, stars, devices, tiles),
        out_shape=block,
        in_specs=[smem, smem] + [vmem] * stars,
        out_specs=vmem,
        scratch_shapes=[pltpu.VMEM((layers * THIRD, 2 * QUART * SIDE, LANES), F32)],
        compiler_params=pltpu.CompilerParams(vmem_limit_bytes=4 << 20),
        name="spread",
    )(foot_rows, foot_cols, *parts)
    held_rows = lax.all_to_all(sent, "dev", 0, 0, tiled=True)
    chosen = pl.pallas_call(
        functools.partial(choose_kernel, devices),
        out_shape=block,
        in_specs=[smem, vmem],
        out_specs=vmem,
        compiler_params=pltpu.CompilerParams(vmem_limit_bytes=2 << 20),
        name="choose",
    )(foot_rows, held_rows)
    strips = lax.all_to_all(chosen, "dev", 0, 0, tiled=True)
    wide = SIDE * SIDE
    table = pl.pallas_call(
        table_kernel,
        out_shape=jax.ShapeDtypeStruct((3 * wide, wide), BF16),
        in_specs=[smem, vmem],
        out_specs=vmem,
        compiler_params=pltpu.CompilerParams(vmem_limit_bytes=2 << 20),
        name="table",
    )(owner, refs)
    found = spots_call(
        stars, devices, stars * tiles, foot_rows, foot_cols, wind, strips, amplitude, table
    )
    return found.reshape(steps, 1, 1, subs, SIDE * SIDE)


def solution(mesh):
    in_specs = (P(None, None, "dev", "star"), P(), P(), P(), P("dev", None), P("star", "dev"), P())
    out_specs = P(None, "star", "dev", None, None)
    return jax.shard_map(shards, mesh=mesh, in_specs=in_specs, out_specs=out_specs, check_vma=False)
```

```python
import functools
import math

import jax
import jax.numpy as jnp
import numpy as np
from jax import lax
from jax.experimental import pallas as pl
from jax.experimental.pallas import tpu as pltpu
from jax.sharding import PartitionSpec as P

BIN = 4
SIDE = 16
LANES = 128
SPAN = 12
QUART = 4
THIRD = SPAN // QUART

F32 = jnp.float32
BF16 = jnp.bfloat16


def split_np(table):
    high = table.astype(jnp.bfloat16)
    low = (table - high.astype(np.float64)).astype(jnp.bfloat16)
    return high, low


def split(value):
    high = value.astype(BF16)
    return high, (value - high.astype(F32)).astype(BF16)


def across_tables():
    length = BIN * SIDE
    freq = (np.arange(length) + length // 2) % length
    angle = 2.0 * math.pi * (np.outer(np.arange(SIDE), freq) % length) / length
    real, imag = np.cos(angle), -np.sin(angle)
    out = np.zeros((2, 8, SIDE, 2, BIN, SIDE, 8))
    for i in range(8):
        for b in range(BIN):
            re, im = real[:, b::BIN], imag[:, b::BIN]
            out[0, i, :, 0, b, :, i] = re
            out[1, i, :, 0, b, :, i] = -im
            out[0, i, :, 1, b, :, i] = im
            out[1, i, :, 1, b, :, i] = re
    return split_np(out.reshape(2 * 8 * SIDE, 2 * BIN * SIDE * 8))


def down_table():
    length = BIN * SIDE
    freq = (np.arange(length) + length // 2) % length
    angle = 2.0 * math.pi * (np.outer(freq, np.arange(SIDE)) % length) / length
    real, imag = np.cos(angle), -np.sin(angle)
    order = np.concatenate([np.arange(a, length, BIN) for a in range(BIN)])
    real, imag = real[order], imag[order]
    table = np.block([[real, -imag], [imag, real]])
    high, low = split_np(table)
    return np.concatenate([high, high, low], axis=1)


def place_of(rows_ref, cols_ref, layer, star, devices, total_tiles):
    offset = rows_ref[star, layer]
    strip = lax.div(offset, SIDE)
    part = lax.rem(offset, SIDE)
    tile = jnp.minimum(lax.div(cols_ref[star, layer], LANES), total_tiles - SPAN)
    return strip, part, tile


def first_tile(tile, panel, tiles, held):
    return jnp.clip(tile - panel * tiles, 0, tiles - held)


def crop_kernel(stars, devices, rows_hbm, cols_hbm, screens_ref, *rest):
    outs, (sem, rows_ref, cols_ref, scalar_sem) = rest[:stars], rest[stars:]
    scalars = [
        pltpu.make_async_copy(rows_hbm, rows_ref, scalar_sem.at[0]),
        pltpu.make_async_copy(cols_hbm, cols_ref, scalar_sem.at[1]),
    ]
    for copy in scalars:
        copy.start()
    for copy in scalars:
        copy.wait()
    layers, bands, side, width = screens_ref.shape
    tiles = width // LANES
    held = min(SPAN, tiles)
    me = lax.axis_index("star")
    place = lax.axis_index("dev")
    copies = []
    for turn in range(stars):
        star = lax.rem(me + turn, stars)
        for layer in range(layers):
            strip, _, tile = place_of(rows_ref, cols_ref, layer, star, devices, stars * tiles)
            behind = lax.rem(place + bands * devices - strip, devices)
            band = lax.div(strip + behind, devices)
            start = first_tile(tile, me, tiles, held)
            columns = pl.ds(pl.multiple_of(start * LANES, LANES), held * LANES)
            for slot in range(2):
                copy = pltpu.make_async_copy(
                    screens_ref.at[layer, lax.rem(band + slot, bands), :, columns],
                    outs[turn].at[2 * layer + slot],
                    sem.at[turn, 2 * layer + slot],
                )
                copy.start()
                copies.append(copy)
    for copy in copies:
        copy.wait()


def spread_kernel(stars, devices, tiles, rows_ref, cols_ref, _, *rest):
    parts, out_ref, turned = rest[:stars], rest[stars], rest[stars + 1]
    layers = parts[0].shape[0] // 2
    held = parts[0].shape[2] // LANES
    groups = devices // SIDE
    sub = QUART // groups
    me = lax.axis_index("star")
    place = lax.axis_index("dev")
    row = lax.broadcasted_iota(jnp.int32, (SIDE, LANES), 0)
    for layer in range(layers):
        strip, part, tile = place_of(rows_ref, cols_ref, layer, me, devices, stars * tiles)
        behind = lax.rem(place + (1 << 20) * devices - strip, devices)
        bound = jnp.where(behind == 0, part, 0)
        wraps = row < bound
        for a in range(QUART):
            for b in range(THIRD):
                spot = tile + (THIRD * a + b)
                panel = lax.div(spot, tiles)
                pair = []
                for slot in range(2):
                    value = None
                    for turn in range(stars):
                        sender = lax.rem(me + stars - turn, stars)
                        start = first_tile(tile, sender, tiles, held)
                        local = jnp.clip(spot - sender * tiles - start, 0, held - 1)
                        lanes = pl.ds(pl.multiple_of(local * LANES, LANES), LANES)
                        seen = parts[turn][2 * layer + slot, :, lanes].astype(F32)
                        if value is None:
                            value = seen
                        else:
                            value = jnp.where(panel == sender, seen, value)
                    pair.append(value)
                first = jnp.where(wraps, pair[1], pair[0])
                at = (a // sub) * 2 * sub + a % sub
                turned[layer * THIRD + b, pl.ds(at * SIDE, SIDE), :] = first
                turned[layer * THIRD + b, pl.ds((at + sub) * SIDE, SIDE), :] = pair[1]
    for group in range(groups):
        for r in range(SIDE):
            pieces = [
                turned[unit, pl.ds(group * 2 * sub * SIDE + r, 2 * sub, stride=SIDE), :]
                for unit in range(layers * THIRD)
            ]
            out_ref[group * SIDE + r] = jnp.concatenate(pieces, axis=1).astype(BF16)


def choose_kernel(devices, rows_ref, in_ref, out_ref):
    layers = rows_ref.shape[1]
    width = in_ref.shape[2] // layers
    half = in_ref.shape[1] // 2
    me = lax.axis_index("star")
    mine = lax.rem(lax.axis_index("dev"), SIDE)
    upper = lax.broadcasted_iota(jnp.int32, (2 * half, width), 0) < half
    for layer in range(layers):
        offset = rows_ref[me, layer]
        base = lax.div(offset, SIDE) + (mine < lax.rem(offset, SIDE)).astype(jnp.int32)
        lanes = slice(layer * width, (layer + 1) * width)
        now = in_ref[lax.rem(base, devices), :, lanes].astype(F32)
        last = now
        for j in range(devices):
            if j < devices - 1:
                after = in_ref[lax.rem(base + j + 1, devices), :, lanes].astype(F32)
                low = pltpu.roll(after, half, axis=0)
            else:
                after, low = None, last
            out_ref[j, :, lanes] = jnp.where(upper, now, low).astype(BF16)
            now = after


def sin_cos(value):
    turns = jnp.floor(value * (2.0 / math.pi) + 0.5)
    rest = value - turns * 1.5703125
    rest = rest - turns * 4.837512969970703125e-4
    rest = rest - turns * 7.549789948768648e-8
    square = rest * rest
    sine = rest + rest * square * (
        -1.6666654611e-1 + square * (8.3321608736e-3 - square * 1.9515295891e-4)
    )
    cosine = (
        1.0
        - 0.5 * square
        + square
        * square
        * (4.166664568298827e-2 + square * (-1.388731625493765e-3 + square * 2.443315711809948e-5))
    )
    quarter = turns.astype(jnp.int32)
    odd = (quarter & 1) == 1
    flip_sine = (quarter & 2) == 2
    flip_cosine = ((quarter + 1) & 2) == 2
    s = jnp.where(odd, cosine, sine)
    c = jnp.where(odd, sine, cosine)
    return jnp.where(flip_sine, -s, s), jnp.where(flip_cosine, -c, c)


def matmul(left, right):
    return lax.dot_general(
        left, right, (((1,), (0,)), ((), ())), preferred_element_type=F32
    )


def table_kernel(owner_ref, refs_ref, table):
    refer = refs_ref[owner_ref[0, 0]]
    wide = SIDE * SIDE
    pick_row = lax.broadcasted_iota(jnp.int32, (SIDE, wide), 0)
    pick_lane = lax.broadcasted_iota(jnp.int32, (SIDE, wide), 1)
    pick = (pick_row == ((SIDE - (pick_lane & 15)) & 15)).astype(F32)
    base = lax.dot_general(
        refer,
        pick,
        (((1,), (0,)), ((), ())),
        precision=lax.Precision.HIGHEST,
        preferred_element_type=F32,
    )
    for bit in range(4):
        moved = pltpu.roll(base, 1 << bit, axis=0)
        base = jnp.where(((pick_lane >> (4 + bit)) & 1) == 1, moved, base)
    for q in range(SIDE):
        if q == 0:
            block = base
        else:
            block = jnp.where(
                (pick_lane & 15) >= q,
                pltpu.roll(base, q, axis=1),
                pltpu.roll(base, wide + q - SIDE, axis=1),
            )
        high, low = split(block)
        table[pl.ds(q * SIDE, SIDE), :] = high
        table[pl.ds(wide + q * SIDE, SIDE), :] = high
        table[pl.ds(2 * wide + q * SIDE, SIDE), :] = low


def spots_kernel(
    stars,
    devices,
    total_tiles,
    rows_ref,
    cols_ref,
    wind_ref,
    in_ref,
    amp_ref,
    table,
    across_ref,
    down_ref,
    out_ref,
    turned,
    window,
    field,
    first,
    binned,
    images,
):
    steps, layers = wind_ref.shape[0], wind_ref.shape[2]
    across = amp_ref.shape[1] // LANES
    groups = devices // SIDE
    sub = QUART // groups
    me = lax.axis_index("star")
    row = lax.broadcasted_iota(jnp.int32, (SIDE, LANES), 0)
    lane = lax.broadcasted_iota(jnp.int32, (SIDE, LANES), 1)

    for x in range(devices):
        seen = in_ref[x].astype(F32)
        for unit in range(layers * THIRD):
            turned[unit, pl.ds(x * 2 * sub, 2 * sub), :] = seen[:, unit * LANES : (unit + 1) * LANES]
    for layer in range(layers):
        part = lax.rem(rows_ref[me, layer], SIDE)
        early = row < part
        for a in range(QUART):
            for b in range(THIRD):
                at = (a // sub) * SIDE * 2 * sub + a % sub
                unit = layer * THIRD + b
                one = turned[unit, pl.ds(at, SIDE, stride=2 * sub), :]
                two = turned[unit, pl.ds(at + sub, SIDE, stride=2 * sub), :]
                slot = layer * SPAN + THIRD * a + b
                window[slot, pl.ds(0, SIDE), :] = one
                window[slot, pl.ds(SIDE, SIDE), :] = jnp.where(early, one, two)
                window[slot, pl.ds(2 * SIDE, SIDE), :] = two

    binned[pl.ds(steps * across * SIDE, binned.shape[0] - steps * across * SIDE), :] = jnp.ones(
        (binned.shape[0] - steps * across * SIDE, LANES), F32
    )

    for step in range(steps):
        phase = [None] * across
        for layer in range(layers):
            left = cols_ref[me, layer]
            tile = jnp.minimum(lax.div(left, LANES), total_tiles - SPAN)
            shift = left - tile * LANES + wind_ref[step, 1, layer]
            skip = lax.div(shift, LANES)
            fine = lax.rem(shift, LANES)
            start = lax.rem(rows_ref[me, layer], SIDE) + wind_ref[step, 0, layer]
            inside = lane < LANES - fine
            rolled = [
                pltpu.roll(
                    window[layer * SPAN + skip + t, pl.ds(start, SIDE), :],
                    lax.rem(LANES - fine, LANES),
                    axis=1,
                )
                for t in range(across + 1)
            ]
            for t in range(across):
                value = jnp.where(inside, rolled[t], rolled[t + 1])
                phase[t] = value if phase[t] is None else phase[t] + value
        for t in range(across):
            sine, cosine = sin_cos(phase[t])
            amp = amp_ref[:, t * LANES : (t + 1) * LANES]
            rows = pl.ds((step * across + t) * SIDE, SIDE)
            for part, value in enumerate((amp * cosine, amp * sine)):
                high, low = split(value)
                at = part * LANES
                field[rows, at : at + LANES] = high
                field[rows, at + 2 * LANES : at + 3 * LANES] = low
                field[rows, at + 4 * LANES : at + 5 * LANES] = high

    first[...] = matmul(field[...], across_ref[...])

    wide_out = first.shape[1] // 2

    for turn in range(steps * across):
        rows = pl.ds(turn * SIDE, SIDE)
        real_high, real_low = split(first[rows, 0:wide_out])
        imag_high, imag_low = split(first[rows, wide_out : 2 * wide_out])
        stacked = jnp.concatenate(
            [real_high, imag_high, real_low, imag_low, real_high, imag_high], axis=0
        )
        spectrum = matmul(down_ref[...], stacked)
        power = spectrum * spectrum
        total = power[0:SIDE]
        for k in range(1, 2 * BIN):
            total = total + power[k * SIDE : (k + 1) * SIDE]
        small = total[:, 0:LANES]
        for k in range(1, BIN):
            small = small + total[:, k * LANES : (k + 1) * LANES]
        binned[rows, :] = small

    lane8 = lax.broadcasted_iota(jnp.int32, (8, LANES), 1)
    for big in range(binned.shape[0] // LANES):
        flipped = binned[pl.ds(big * LANES, LANES), :].T
        halves = []
        for half in range(2):
            regs = [flipped[(half * 8 + q) * 8 : (half * 8 + q + 1) * 8] for q in range(8)]
            for jump in (4, 2, 1):
                keep = ((lane8 >> 4) & jump) == 0
                for i in range(8):
                    if i & jump == 0:
                        one, two = regs[i], regs[i + jump]
                        regs[i] = jnp.where(keep, one, pltpu.roll(two, jump * SIDE, axis=1))
                        regs[i + jump] = jnp.where(
                            keep, pltpu.roll(one, LANES - jump * SIDE, axis=1), two
                        )
            halves.append(regs)
        image = jnp.concatenate(
            [jnp.concatenate([halves[0][g], halves[1][g]], axis=1) for g in range(8)], axis=0
        )
        image = image / jnp.sum(image, axis=1, keepdims=True)
        high, low = split(image)
        rows = pl.ds(big * 64, 64)
        wide = SIDE * SIDE
        images[rows, 0:wide] = high
        images[rows, wide : 2 * wide] = low
        images[rows, 2 * wide : 3 * wide] = high
    out_ref[...] = matmul(images[...], table[...])[0 : out_ref.shape[0]]


def spots_call(stars, devices, total_tiles, foot_rows, foot_cols, wind, strips, amplitude, table):
    smem = pl.BlockSpec(memory_space=pltpu.SMEM)
    vmem = pl.BlockSpec(memory_space=pltpu.VMEM)
    steps, layers = wind.shape[0], wind.shape[2]
    depth = strips.shape[1]
    subs = amplitude.shape[1] // SIDE
    high, low = across_tables()
    table_across = np.concatenate([high, high, low], axis=0)
    count = steps * subs
    padded = -(-count // 64) * 64
    return pl.pallas_call(
        functools.partial(spots_kernel, stars, devices, total_tiles),
        out_shape=jax.ShapeDtypeStruct((count, SIDE * SIDE), F32),
        in_specs=[smem] * 3 + [vmem] * 5,
        out_specs=vmem,
        scratch_shapes=[
            pltpu.VMEM((layers * THIRD, devices * depth, LANES), F32),
            pltpu.VMEM((layers * SPAN, 3 * SIDE, LANES), F32),
            pltpu.VMEM((count // 8 * SIDE, 6 * LANES), BF16),
            pltpu.VMEM((count // 8 * SIDE, high.shape[1]), F32),
            pltpu.VMEM((padded // 8 * SIDE, LANES), F32),
            pltpu.VMEM((padded, 3 * SIDE * SIDE), BF16),
        ],
        compiler_params=pltpu.CompilerParams(vmem_limit_bytes=16 << 20),
        name="spots",
    )(foot_rows, foot_cols, wind, strips, amplitude, table, table_across, down_table())


def shards(screens, foot_rows, foot_cols, wind, amplitude, owner, refs):
    stars, devices = lax.axis_size("star"), lax.axis_size("dev")
    layers, _, side, width = screens.shape
    steps = wind.shape[0]
    foot_rows, foot_cols = foot_rows.T, foot_cols.T
    wind = wind.transpose(0, 2, 1)
    tiles = width // LANES
    held = min(SPAN, tiles)
    subs = amplitude.shape[1] // side
    smem = pl.BlockSpec(memory_space=pltpu.SMEM)
    vmem = pl.BlockSpec(memory_space=pltpu.VMEM)
    hbm = pl.BlockSpec(memory_space=pltpu.HBM)
    screens = pltpu.with_memory_space_constraint(screens, pltpu.HBM)
    crops = pl.pallas_call(
        functools.partial(crop_kernel, stars, devices),
        out_shape=[jax.ShapeDtypeStruct((2 * layers, side, held * LANES), BF16)] * stars,
        in_specs=[hbm] * 3,
        out_specs=[vmem] * stars,
        scratch_shapes=[
            pltpu.SemaphoreType.DMA((stars, 2 * layers)),
            pltpu.SMEM(foot_rows.shape, jnp.int32),
            pltpu.SMEM(foot_cols.shape, jnp.int32),
            pltpu.SemaphoreType.DMA((2,)),
        ],
        compiler_params=pltpu.CompilerParams(vmem_limit_bytes=2 << 20),
        name="crop",
    )(
        pltpu.with_memory_space_constraint(foot_rows, pltpu.HBM),
        pltpu.with_memory_space_constraint(foot_cols, pltpu.HBM),
        screens,
    )
    parts = [crops[0]]
    for turn in range(1, stars):
        parts.append(
            lax.ppermute(crops[turn], "star", [(i, (i + turn) % stars) for i in range(stars)])
        )
    groups = devices // SIDE
    depth = 2 * QUART // groups
    block = jax.ShapeDtypeStruct((devices, depth, layers * THIRD * LANES), BF16)
    wide = SIDE * SIDE
    table = pl.pallas_call(
        table_kernel,
        out_shape=jax.ShapeDtypeStruct((3 * wide, wide), BF16),
        in_specs=[smem, vmem],
        out_specs=vmem,
        compiler_params=pltpu.CompilerParams(vmem_limit_bytes=2 << 20),
        name="table",
    )(owner, refs)
    sent = pl.pallas_call(
        functools.partial(spread_kernel, stars, devices, tiles),
        out_shape=block,
        in_specs=[smem, smem, pl.BlockSpec(memory_space=pl.ANY)] + [vmem] * stars,
        out_specs=vmem,
        scratch_shapes=[pltpu.VMEM((layers * THIRD, 2 * QUART * SIDE, LANES), F32)],
        compiler_params=pltpu.CompilerParams(vmem_limit_bytes=4 << 20),
        name="spread",
    )(foot_rows, foot_cols, table, *parts)
    held_rows = lax.all_to_all(sent, "dev", 0, 0, tiled=True)
    chosen = pl.pallas_call(
        functools.partial(choose_kernel, devices),
        out_shape=block,
        in_specs=[smem, vmem],
        out_specs=vmem,
        compiler_params=pltpu.CompilerParams(vmem_limit_bytes=2 << 20),
        name="choose",
    )(foot_rows, held_rows)
    strips = lax.all_to_all(chosen, "dev", 0, 0, tiled=True)
    found = spots_call(
        stars, devices, stars * tiles, foot_rows, foot_cols, wind, strips, amplitude, table
    )
    return found.reshape(steps, 1, 1, subs, SIDE * SIDE)


def solution(mesh):
    in_specs = (P(None, None, "dev", "star"), P(), P(), P(), P("dev", None), P("star", "dev"), P())
    out_specs = P(None, "star", "dev", None, None)
    return jax.shard_map(shards, mesh=mesh, in_specs=in_specs, out_specs=out_specs, check_vma=False)
```

```python
import functools
import math

import jax
import jax.numpy as jnp
import numpy as np
from jax import lax
from jax.experimental import pallas as pl
from jax.experimental.pallas import tpu as pltpu
from jax.sharding import PartitionSpec as P

BIN = 4
SIDE = 16
LANES = 128
SPAN = 12
QUART = 4
THIRD = SPAN // QUART

F32 = jnp.float32
BF16 = jnp.bfloat16


def split_np(table):
    high = table.astype(jnp.bfloat16)
    low = (table - high.astype(np.float64)).astype(jnp.bfloat16)
    return high, low


def split(value):
    high = value.astype(BF16)
    return high, (value - high.astype(F32)).astype(BF16)


def across_tables():
    length = BIN * SIDE
    freq = (np.arange(length) + length // 2) % length
    angle = 2.0 * math.pi * (np.outer(np.arange(SIDE), freq) % length) / length
    real, imag = np.cos(angle), -np.sin(angle)
    out = np.zeros((2, 8, SIDE, 2, BIN, SIDE, 8))
    for i in range(8):
        for b in range(BIN):
            re, im = real[:, b::BIN], imag[:, b::BIN]
            out[0, i, :, 0, b, :, i] = re
            out[1, i, :, 0, b, :, i] = -im
            out[0, i, :, 1, b, :, i] = im
            out[1, i, :, 1, b, :, i] = re
    return split_np(out.reshape(2 * 8 * SIDE, 2 * BIN * SIDE * 8))


def down_table():
    length = BIN * SIDE
    freq = (np.arange(length) + length // 2) % length
    angle = 2.0 * math.pi * (np.outer(freq, np.arange(SIDE)) % length) / length
    real, imag = np.cos(angle), -np.sin(angle)
    order = np.concatenate([np.arange(a, length, BIN) for a in range(BIN)])
    real, imag = real[order], imag[order]
    table = np.block([[real, -imag], [imag, real]])
    high, low = split_np(table)
    return np.concatenate([high, high, low], axis=1)


def place_of(rows_ref, cols_ref, layer, star, devices, total_tiles):
    offset = rows_ref[star, layer]
    strip = lax.div(offset, SIDE)
    part = lax.rem(offset, SIDE)
    tile = jnp.minimum(lax.div(cols_ref[star, layer], LANES), total_tiles - SPAN)
    return strip, part, tile


def own_row(ref, star):
    row = ref[pl.ds(star, 1), :]
    return [row[0, layer] for layer in range(ref.shape[1])]


def place_of_own(offset, left, total_tiles):
    strip = lax.div(offset, SIDE)
    part = lax.rem(offset, SIDE)
    tile = jnp.minimum(lax.div(left, LANES), total_tiles - SPAN)
    return strip, part, tile


def first_tile(tile, panel, tiles, held):
    return jnp.clip(tile - panel * tiles, 0, tiles - held)


def crop_kernel(stars, devices, rows_hbm, cols_hbm, screens_ref, *rest):
    outs, (sem, rows_ref, cols_ref, scalar_sem) = rest[:stars], rest[stars:]
    scalars = [
        pltpu.make_async_copy(rows_hbm, rows_ref, scalar_sem.at[0]),
        pltpu.make_async_copy(cols_hbm, cols_ref, scalar_sem.at[1]),
    ]
    for copy in scalars:
        copy.start()
    for copy in scalars:
        copy.wait()
    layers, bands, side, width = screens_ref.shape
    tiles = width // LANES
    held = min(SPAN, tiles)
    me = lax.axis_index("star")
    place = lax.axis_index("dev")
    copies = []
    for turn in range(stars):
        star = lax.rem(me + turn, stars)
        for layer in range(layers):
            strip, _, tile = place_of(rows_ref, cols_ref, layer, star, devices, stars * tiles)
            behind = lax.rem(place + bands * devices - strip, devices)
            band = lax.div(strip + behind, devices)
            start = first_tile(tile, me, tiles, held)
            columns = pl.ds(pl.multiple_of(start * LANES, LANES), held * LANES)
            for slot in range(2):
                copy = pltpu.make_async_copy(
                    screens_ref.at[layer, lax.rem(band + slot, bands), :, columns],
                    outs[turn].at[2 * layer + slot],
                    sem.at[turn, 2 * layer + slot],
                )
                copy.start()
                copies.append(copy)
    for copy in copies:
        copy.wait()


def spread_kernel(stars, devices, tiles, rows_ref, cols_ref, _, *rest):
    parts, out_ref, turned = rest[:stars], rest[stars], rest[stars + 1]
    layers = parts[0].shape[0] // 2
    held = parts[0].shape[2] // LANES
    groups = devices // SIDE
    sub = QUART // groups
    me = lax.axis_index("star")
    place = lax.axis_index("dev")
    row = lax.broadcasted_iota(jnp.int32, (SIDE, LANES), 0)
    offsets, lefts = own_row(rows_ref, me), own_row(cols_ref, me)
    for layer in range(layers):
        strip, part, tile = place_of_own(offsets[layer], lefts[layer], stars * tiles)
        behind = lax.rem(place + (1 << 20) * devices - strip, devices)
        bound = jnp.where(behind == 0, part, 0)
        wraps = row < bound
        for a in range(QUART):
            for b in range(THIRD):
                spot = tile + (THIRD * a + b)
                panel = lax.div(spot, tiles)
                pair = []
                for slot in range(2):
                    value = None
                    for turn in range(stars):
                        sender = lax.rem(me + stars - turn, stars)
                        start = first_tile(tile, sender, tiles, held)
                        local = jnp.clip(spot - sender * tiles - start, 0, held - 1)
                        lanes = pl.ds(pl.multiple_of(local * LANES, LANES), LANES)
                        seen = parts[turn][2 * layer + slot, :, lanes].astype(F32)
                        if value is None:
                            value = seen
                        else:
                            value = jnp.where(panel == sender, seen, value)
                    pair.append(value)
                first = jnp.where(wraps, pair[1], pair[0])
                at = (a // sub) * 2 * sub + a % sub
                turned[layer * THIRD + b, pl.ds(at * SIDE, SIDE), :] = first
                turned[layer * THIRD + b, pl.ds((at + sub) * SIDE, SIDE), :] = pair[1]
    for group in range(groups):
        for r in range(SIDE):
            pieces = [
                turned[unit, pl.ds(group * 2 * sub * SIDE + r, 2 * sub, stride=SIDE), :]
                for unit in range(layers * THIRD)
            ]
            out_ref[group * SIDE + r] = jnp.concatenate(pieces, axis=1).astype(BF16)


def choose_kernel(devices, rows_ref, in_ref, out_ref):
    layers = rows_ref.shape[1]
    width = in_ref.shape[2] // layers
    half = in_ref.shape[1] // 2
    me = lax.axis_index("star")
    mine = lax.rem(lax.axis_index("dev"), SIDE)
    upper = lax.broadcasted_iota(jnp.int32, (2 * half, width), 0) < half
    offsets = own_row(rows_ref, me)
    for layer in range(layers):
        offset = offsets[layer]
        base = lax.div(offset, SIDE) + (mine < lax.rem(offset, SIDE)).astype(jnp.int32)
        lanes = slice(layer * width, (layer + 1) * width)
        now = in_ref[lax.rem(base, devices), :, lanes].astype(F32)
        last = now
        for j in range(devices):
            if j < devices - 1:
                after = in_ref[lax.rem(base + j + 1, devices), :, lanes].astype(F32)
                low = pltpu.roll(after, half, axis=0)
            else:
                after, low = None, last
            out_ref[j, :, lanes] = jnp.where(upper, now, low).astype(BF16)
            now = after


def sin_cos(value):
    turns = jnp.floor(value * (2.0 / math.pi) + 0.5)
    rest = value - turns * 1.5703125
    rest = rest - turns * 4.837512969970703125e-4
    rest = rest - turns * 7.549789948768648e-8
    square = rest * rest
    sine = rest + rest * square * (
        -1.6666654611e-1 + square * (8.3321608736e-3 - square * 1.9515295891e-4)
    )
    cosine = (
        1.0
        - 0.5 * square
        + square
        * square
        * (4.166664568298827e-2 + square * (-1.388731625493765e-3 + square * 2.443315711809948e-5))
    )
    quarter = turns.astype(jnp.int32)
    odd = (quarter & 1) == 1
    flip_sine = (quarter & 2) == 2
    flip_cosine = ((quarter + 1) & 2) == 2
    s = jnp.where(odd, cosine, sine)
    c = jnp.where(odd, sine, cosine)
    return jnp.where(flip_sine, -s, s), jnp.where(flip_cosine, -c, c)


def matmul(left, right):
    return lax.dot_general(
        left, right, (((1,), (0,)), ((), ())), preferred_element_type=F32
    )


def table_kernel(owner_ref, refs_ref, table):
    refer = refs_ref[owner_ref[0, 0]]
    wide = SIDE * SIDE
    pick_row = lax.broadcasted_iota(jnp.int32, (SIDE, wide), 0)
    pick_lane = lax.broadcasted_iota(jnp.int32, (SIDE, wide), 1)
    pick = (pick_row == ((SIDE - (pick_lane & 15)) & 15)).astype(F32)
    base = lax.dot_general(
        refer,
        pick,
        (((1,), (0,)), ((), ())),
        precision=lax.Precision.HIGHEST,
        preferred_element_type=F32,
    )
    for bit in range(4):
        moved = pltpu.roll(base, 1 << bit, axis=0)
        base = jnp.where(((pick_lane >> (4 + bit)) & 1) == 1, moved, base)
    for q in range(SIDE):
        if q == 0:
            block = base
        else:
            block = jnp.where(
                (pick_lane & 15) >= q,
                pltpu.roll(base, q, axis=1),
                pltpu.roll(base, wide + q - SIDE, axis=1),
            )
        high, low = split(block)
        table[pl.ds(q * SIDE, SIDE), :] = high
        table[pl.ds(wide + q * SIDE, SIDE), :] = high
        table[pl.ds(2 * wide + q * SIDE, SIDE), :] = low


def spots_kernel(
    stars,
    devices,
    total_tiles,
    rows_ref,
    cols_ref,
    wind_ref,
    in_ref,
    amp_ref,
    table,
    across_ref,
    down_ref,
    out_ref,
    turned,
    window,
    field,
):
    steps, layers = wind_ref.shape[0], wind_ref.shape[2]
    across = amp_ref.shape[1] // LANES
    groups = devices // SIDE
    sub = QUART // groups
    me = lax.axis_index("star")
    row = lax.broadcasted_iota(jnp.int32, (SIDE, LANES), 0)
    lane = lax.broadcasted_iota(jnp.int32, (SIDE, LANES), 1)
    offsets, lefts = own_row(rows_ref, me), own_row(cols_ref, me)
    shifts = [wind_ref[step] for step in range(steps)]

    for x in range(devices):
        seen = in_ref[x].astype(F32)
        for unit in range(layers * THIRD):
            turned[unit, pl.ds(x * 2 * sub, 2 * sub), :] = seen[:, unit * LANES : (unit + 1) * LANES]
    for layer in range(layers):
        part = lax.rem(offsets[layer], SIDE)
        early = row < part
        for a in range(QUART):
            for b in range(THIRD):
                at = (a // sub) * SIDE * 2 * sub + a % sub
                unit = layer * THIRD + b
                one = turned[unit, pl.ds(at, SIDE, stride=2 * sub), :]
                two = turned[unit, pl.ds(at + sub, SIDE, stride=2 * sub), :]
                slot = layer * SPAN + THIRD * a + b
                window[slot, pl.ds(0, SIDE), :] = one
                window[slot, pl.ds(SIDE, SIDE), :] = jnp.where(early, one, two)
                window[slot, pl.ds(2 * SIDE, SIDE), :] = two

    for step in range(steps):
        phase = [None] * across
        for layer in range(layers):
            left = lefts[layer]
            tile = jnp.minimum(lax.div(left, LANES), total_tiles - SPAN)
            shift = left - tile * LANES + shifts[step][1, layer]
            skip = lax.div(shift, LANES)
            fine = lax.rem(shift, LANES)
            start = lax.rem(offsets[layer], SIDE) + shifts[step][0, layer]
            inside = lane < LANES - fine
            rolled = [
                pltpu.roll(
                    window[layer * SPAN + skip + t, pl.ds(start, SIDE), :],
                    lax.rem(LANES - fine, LANES),
                    axis=1,
                )
                for t in range(across + 1)
            ]
            for t in range(across):
                value = jnp.where(inside, rolled[t], rolled[t + 1])
                phase[t] = value if phase[t] is None else phase[t] + value
        for t in range(across):
            sine, cosine = sin_cos(phase[t])
            amp = amp_ref[:, t * LANES : (t + 1) * LANES]
            rows = pl.ds((step * across + t) * SIDE, SIDE)
            for part, value in enumerate((amp * cosine, amp * sine)):
                high, low = split(value)
                at = part * LANES
                field[rows, at : at + LANES] = high
                field[rows, at + 2 * LANES : at + 3 * LANES] = low
                field[rows, at + 4 * LANES : at + 5 * LANES] = high

    first = matmul(field[...], across_ref[...])

    wide_out = first.shape[1] // 2
    wide = SIDE * SIDE
    lane8 = lax.broadcasted_iota(jnp.int32, (8, LANES), 1)
    turns = steps * across
    found = []
    for big in range(0, turns, 8):
        smalls = []
        for turn in range(big, min(big + 8, turns)):
            rows = pl.ds(turn * SIDE, SIDE)
            real_high, real_low = split(first[turn * SIDE : (turn + 1) * SIDE, 0:wide_out])
            imag_high, imag_low = split(first[turn * SIDE : (turn + 1) * SIDE, wide_out : 2 * wide_out])
            stacked = jnp.concatenate(
                [real_high, imag_high, real_low, imag_low, real_high, imag_high], axis=0
            )
            spectrum = matmul(down_ref[...], stacked)
            power = spectrum * spectrum
            total = power[0:SIDE]
            for k in range(1, 2 * BIN):
                total = total + power[k * SIDE : (k + 1) * SIDE]
            small = total[:, 0:LANES]
            for k in range(1, BIN):
                small = small + total[:, k * LANES : (k + 1) * LANES]
            smalls.append(small)
        while len(smalls) < 8:
            smalls.append(jnp.ones((SIDE, LANES), F32))
        flipped = jnp.concatenate(smalls, axis=0).T
        halves = []
        for half in range(2):
            regs = [flipped[(half * 8 + q) * 8 : (half * 8 + q + 1) * 8] for q in range(8)]
            for jump in (4, 2, 1):
                keep = ((lane8 >> 4) & jump) == 0
                for i in range(8):
                    if i & jump == 0:
                        one, two = regs[i], regs[i + jump]
                        regs[i] = jnp.where(keep, one, pltpu.roll(two, jump * SIDE, axis=1))
                        regs[i + jump] = jnp.where(
                            keep, pltpu.roll(one, LANES - jump * SIDE, axis=1), two
                        )
            halves.append(regs)
        image = jnp.concatenate(
            [jnp.concatenate([halves[0][g], halves[1][g]], axis=1) for g in range(8)], axis=0
        )
        image = image * (1.0 / jnp.sum(image, axis=1, keepdims=True))
        high, low = split(image)
        found.append(jnp.concatenate([high, low, high], axis=1))
    out_ref[...] = matmul(jnp.concatenate(found, axis=0), table[...])[0 : out_ref.shape[0]]


def spots_call(stars, devices, total_tiles, foot_rows, foot_cols, wind, strips, amplitude, table):
    vmem = pl.BlockSpec(memory_space=pltpu.VMEM)
    steps, layers = wind.shape[0], wind.shape[2]
    depth = strips.shape[1]
    subs = amplitude.shape[1] // SIDE
    high, low = across_tables()
    table_across = np.concatenate([high, high, low], axis=0)
    count = steps * subs
    padded = -(-count // 64) * 64
    return pl.pallas_call(
        functools.partial(spots_kernel, stars, devices, total_tiles),
        out_shape=jax.ShapeDtypeStruct((count, SIDE * SIDE), F32),
        in_specs=[vmem] * 8,
        out_specs=vmem,
        scratch_shapes=[
            pltpu.VMEM((layers * THIRD, devices * depth, LANES), F32),
            pltpu.VMEM((layers * SPAN, 3 * SIDE, LANES), F32),
            pltpu.VMEM((count // 8 * SIDE, 6 * LANES), BF16),
        ],
        compiler_params=pltpu.CompilerParams(vmem_limit_bytes=16 << 20),
        name="spots",
    )(foot_rows, foot_cols, wind, strips, amplitude, table, table_across, down_table())


def shards(screens, foot_rows, foot_cols, wind, amplitude, owner, refs):
    stars, devices = lax.axis_size("star"), lax.axis_size("dev")
    layers, _, side, width = screens.shape
    steps = wind.shape[0]
    foot_rows, foot_cols = foot_rows.T, foot_cols.T
    wind = wind.transpose(0, 2, 1)
    tiles = width // LANES
    held = min(SPAN, tiles)
    subs = amplitude.shape[1] // side
    smem = pl.BlockSpec(memory_space=pltpu.SMEM)
    vmem = pl.BlockSpec(memory_space=pltpu.VMEM)
    hbm = pl.BlockSpec(memory_space=pltpu.HBM)
    screens = pltpu.with_memory_space_constraint(screens, pltpu.HBM)
    crops = pl.pallas_call(
        functools.partial(crop_kernel, stars, devices),
        out_shape=[jax.ShapeDtypeStruct((2 * layers, side, held * LANES), BF16)] * stars,
        in_specs=[hbm] * 3,
        out_specs=[vmem] * stars,
        scratch_shapes=[
            pltpu.SemaphoreType.DMA((stars, 2 * layers)),
            pltpu.SMEM(foot_rows.shape, jnp.int32),
            pltpu.SMEM(foot_cols.shape, jnp.int32),
            pltpu.SemaphoreType.DMA((2,)),
        ],
        compiler_params=pltpu.CompilerParams(vmem_limit_bytes=2 << 20),
        name="crop",
    )(
        pltpu.with_memory_space_constraint(foot_rows, pltpu.HBM),
        pltpu.with_memory_space_constraint(foot_cols, pltpu.HBM),
        screens,
    )
    parts = [crops[0]]
    for turn in range(1, stars):
        parts.append(
            lax.ppermute(crops[turn], "star", [(i, (i + turn) % stars) for i in range(stars)])
        )
    groups = devices // SIDE
    depth = 2 * QUART // groups
    block = jax.ShapeDtypeStruct((devices, depth, layers * THIRD * LANES), BF16)
    wide = SIDE * SIDE
    table = pl.pallas_call(
        table_kernel,
        out_shape=jax.ShapeDtypeStruct((3 * wide, wide), BF16),
        in_specs=[smem, vmem],
        out_specs=vmem,
        compiler_params=pltpu.CompilerParams(vmem_limit_bytes=2 << 20),
        name="table",
    )(owner, refs)
    sent = pl.pallas_call(
        functools.partial(spread_kernel, stars, devices, tiles),
        out_shape=block,
        in_specs=[vmem, vmem, pl.BlockSpec(memory_space=pl.ANY)] + [vmem] * stars,
        out_specs=vmem,
        scratch_shapes=[pltpu.VMEM((layers * THIRD, 2 * QUART * SIDE, LANES), F32)],
        compiler_params=pltpu.CompilerParams(vmem_limit_bytes=4 << 20),
        name="spread",
    )(foot_rows, foot_cols, table, *parts)
    held_rows = lax.all_to_all(sent, "dev", 0, 0, tiled=True)
    chosen = pl.pallas_call(
        functools.partial(choose_kernel, devices),
        out_shape=block,
        in_specs=[vmem, vmem],
        out_specs=vmem,
        compiler_params=pltpu.CompilerParams(vmem_limit_bytes=2 << 20),
        name="choose",
    )(foot_rows, held_rows)
    strips = lax.all_to_all(chosen, "dev", 0, 0, tiled=True)
    found = spots_call(
        stars, devices, stars * tiles, foot_rows, foot_cols, wind, strips, amplitude, table
    )
    return found.reshape(steps, 1, 1, subs, SIDE * SIDE)


def solution(mesh):
    in_specs = (P(None, None, "dev", "star"), P(), P(), P(), P("dev", None), P("star", "dev"), P())
    out_specs = P(None, "star", "dev", None, None)
    return jax.shard_map(shards, mesh=mesh, in_specs=in_specs, out_specs=out_specs, check_vma=False)
```

```python
import functools
import math

import jax
import jax.numpy as jnp
import numpy as np
from jax import lax
from jax.experimental import pallas as pl
from jax.experimental.pallas import tpu as pltpu
from jax.sharding import PartitionSpec as P

BIN = 4
SIDE = 16
LANES = 128
SPAN = 12
QUART = 4
THIRD = SPAN // QUART
GROUP = 8

F32 = jnp.float32
BF16 = jnp.bfloat16


def split_np(table):
    high = table.astype(jnp.bfloat16)
    low = (table - high.astype(np.float64)).astype(jnp.bfloat16)
    return high, low


def split(value):
    high = value.astype(BF16)
    return high, (value - high.astype(F32)).astype(BF16)


def across_tables():
    length = BIN * SIDE
    freq = (np.arange(length) + length // 2) % length
    angle = 2.0 * math.pi * (np.outer(np.arange(SIDE), freq) % length) / length
    real, imag = np.cos(angle), -np.sin(angle)
    out = np.zeros((2, 8, SIDE, 2, BIN, SIDE, 8))
    for i in range(8):
        for b in range(BIN):
            re, im = real[:, b::BIN], imag[:, b::BIN]
            out[0, i, :, 0, b, :, i] = re
            out[1, i, :, 0, b, :, i] = -im
            out[0, i, :, 1, b, :, i] = im
            out[1, i, :, 1, b, :, i] = re
    return split_np(out.reshape(2 * 8 * SIDE, 2 * BIN * SIDE * 8))


def down_table():
    length = BIN * SIDE
    freq = (np.arange(length) + length // 2) % length
    angle = 2.0 * math.pi * (np.outer(freq, np.arange(SIDE)) % length) / length
    real, imag = np.cos(angle), -np.sin(angle)
    order = np.concatenate([np.arange(a, length, BIN) for a in range(BIN)])
    real, imag = real[order], imag[order]
    table = np.block([[real, -imag], [imag, real]])
    high, low = split_np(table)
    return np.concatenate([high, high, low], axis=1)


def place_of(rows_ref, cols_ref, layer, star, devices, total_tiles):
    offset = rows_ref[star, layer]
    strip = lax.div(offset, SIDE)
    part = lax.rem(offset, SIDE)
    tile = jnp.minimum(lax.div(cols_ref[star, layer], LANES), total_tiles - SPAN)
    return strip, part, tile


def own_row(ref, star):
    row = ref[pl.ds(star, 1), :]
    return [row[0, layer] for layer in range(ref.shape[1])]


def place_of_own(offset, left, total_tiles):
    strip = lax.div(offset, SIDE)
    part = lax.rem(offset, SIDE)
    tile = jnp.minimum(lax.div(left, LANES), total_tiles - SPAN)
    return strip, part, tile


def first_tile(tile, panel, tiles, held):
    return jnp.clip(tile - panel * tiles, 0, tiles - held)


def crop_kernel(stars, devices, rows_hbm, cols_hbm, screens_ref, *rest):
    outs, (sem, rows_ref, cols_ref, scalar_sem) = rest[:stars], rest[stars:]
    scalars = [
        pltpu.make_async_copy(rows_hbm, rows_ref, scalar_sem.at[0]),
        pltpu.make_async_copy(cols_hbm, cols_ref, scalar_sem.at[1]),
    ]
    for copy in scalars:
        copy.start()
    for copy in scalars:
        copy.wait()
    layers, bands, side, width = screens_ref.shape
    tiles = width // LANES
    held = min(SPAN, tiles)
    me = lax.axis_index("star")
    place = lax.axis_index("dev")
    copies = []
    for turn in range(stars):
        star = lax.rem(me + turn, stars)
        for layer in range(layers):
            strip, _, tile = place_of(rows_ref, cols_ref, layer, star, devices, stars * tiles)
            behind = lax.rem(place + bands * devices - strip, devices)
            band = lax.div(strip + behind, devices)
            start = first_tile(tile, me, tiles, held)
            columns = pl.ds(pl.multiple_of(start * LANES, LANES), held * LANES)
            for slot in range(2):
                copy = pltpu.make_async_copy(
                    screens_ref.at[layer, lax.rem(band + slot, bands), :, columns],
                    outs[turn].at[2 * layer + slot],
                    sem.at[turn, 2 * layer + slot],
                )
                copy.start()
                copies.append(copy)
    for copy in copies:
        copy.wait()


def spread_kernel(stars, devices, tiles, rows_ref, cols_ref, _, *rest):
    parts, out_ref, turned = rest[:stars], rest[stars], rest[stars + 1]
    layers = parts[0].shape[0] // 2
    held = parts[0].shape[2] // LANES
    me = lax.axis_index("star")
    place = lax.axis_index("dev")
    row = lax.broadcasted_iota(jnp.int32, (SIDE, LANES), 0)
    offsets, lefts = own_row(rows_ref, me), own_row(cols_ref, me)
    for layer in range(layers):
        strip, part, tile = place_of_own(offsets[layer], lefts[layer], stars * tiles)
        behind = lax.rem(place + (1 << 20) * devices - strip, devices)
        wraps = row < jnp.where(behind == 0, SIDE, jnp.where(behind == 1, part, 0))
        for a in range(QUART):
            for b in range(THIRD):
                spot = tile + (THIRD * a + b)
                panel = lax.div(spot, tiles)
                pair = []
                for slot in range(2):
                    value = None
                    for turn in range(stars):
                        sender = lax.rem(me + stars - turn, stars)
                        start = first_tile(tile, sender, tiles, held)
                        local = jnp.clip(spot - sender * tiles - start, 0, held - 1)
                        lanes = pl.ds(pl.multiple_of(local * LANES, LANES), LANES)
                        seen = parts[turn][2 * layer + slot, :, lanes].astype(F32)
                        if value is None:
                            value = seen
                        else:
                            value = jnp.where(panel == sender, seen, value)
                    pair.append(value)
                turned[0, layer * THIRD + b, pl.ds(a * SIDE, SIDE), :] = pair[0]
                turned[1, layer * THIRD + b, pl.ds(a * SIDE, SIDE), :] = jnp.where(
                    wraps, pair[1], pair[0]
                )
    last = devices // GROUP - 1
    for x in range(GROUP):
        for kind in range(2):
            pieces = [
                turned[kind, unit, pl.ds(x, 2 * QUART, stride=GROUP), :]
                for unit in range(layers * THIRD)
            ]
            block = jnp.concatenate(pieces, axis=1).astype(BF16)
            if kind == 1:
                out_ref[last * GROUP + x] = block
            else:
                for group in range(last):
                    out_ref[group * GROUP + x] = block


def choose_kernel(devices, rows_ref, in_ref, out_ref):
    layers = rows_ref.shape[1]
    width = in_ref.shape[2] // layers
    me = lax.axis_index("star")
    place = lax.axis_index("dev")
    mine = lax.rem(place, GROUP)
    first = place - mine
    even = lax.broadcasted_iota(jnp.int32, (2 * QUART, width), 0) % 2 == 0
    offsets = own_row(rows_ref, me)
    for layer in range(layers):
        offset = offsets[layer]
        part = lax.rem(offset, SIDE)
        strip = lax.div(offset, SIDE) + first
        base = [strip + (mine + GROUP * u < part).astype(jnp.int32) for u in range(2)]
        lanes = slice(layer * width, (layer + 1) * width)
        for j in range(GROUP + 1):
            one, two = (
                in_ref[lax.rem(base[u] + j, devices), :, lanes].astype(F32) for u in range(2)
            )
            item = jnp.where(even, one, two).astype(BF16)
            if j < GROUP:
                out_ref[j, pl.ds(0, 2 * QUART), lanes] = item
            if j > 0:
                out_ref[j - 1, pl.ds(2 * QUART, 2 * QUART), lanes] = item


def sin_cos(value):
    turns = jnp.floor(value * (2.0 / math.pi) + 0.5)
    rest = value - turns * 1.5703125
    rest = rest - turns * 4.837512969970703125e-4
    rest = rest - turns * 7.549789948768648e-8
    square = rest * rest
    sine = rest + rest * square * (
        -1.6666654611e-1 + square * (8.3321608736e-3 - square * 1.9515295891e-4)
    )
    cosine = (
        1.0
        - 0.5 * square
        + square
        * square
        * (4.166664568298827e-2 + square * (-1.388731625493765e-3 + square * 2.443315711809948e-5))
    )
    quarter = turns.astype(jnp.int32)
    odd = (quarter & 1) == 1
    flip_sine = (quarter & 2) == 2
    flip_cosine = ((quarter + 1) & 2) == 2
    s = jnp.where(odd, cosine, sine)
    c = jnp.where(odd, sine, cosine)
    return jnp.where(flip_sine, -s, s), jnp.where(flip_cosine, -c, c)


def matmul(left, right):
    return lax.dot_general(
        left, right, (((1,), (0,)), ((), ())), preferred_element_type=F32
    )


def table_kernel(owner_ref, refs_ref, table):
    refer = refs_ref[owner_ref[0, 0]]
    wide = SIDE * SIDE
    pick_row = lax.broadcasted_iota(jnp.int32, (SIDE, wide), 0)
    pick_lane = lax.broadcasted_iota(jnp.int32, (SIDE, wide), 1)
    pick = (pick_row == ((SIDE - (pick_lane & 15)) & 15)).astype(F32)
    base = lax.dot_general(
        refer,
        pick,
        (((1,), (0,)), ((), ())),
        precision=lax.Precision.HIGHEST,
        preferred_element_type=F32,
    )
    for bit in range(4):
        moved = pltpu.roll(base, 1 << bit, axis=0)
        base = jnp.where(((pick_lane >> (4 + bit)) & 1) == 1, moved, base)
    for q in range(SIDE):
        if q == 0:
            block = base
        else:
            block = jnp.where(
                (pick_lane & 15) >= q,
                pltpu.roll(base, q, axis=1),
                pltpu.roll(base, wide + q - SIDE, axis=1),
            )
        high, low = split(block)
        table[pl.ds(q * SIDE, SIDE), :] = high
        table[pl.ds(wide + q * SIDE, SIDE), :] = high
        table[pl.ds(2 * wide + q * SIDE, SIDE), :] = low


def spots_kernel(
    stars,
    devices,
    total_tiles,
    rows_ref,
    cols_ref,
    wind_ref,
    in_ref,
    amp_ref,
    table,
    across_ref,
    down_ref,
    out_ref,
    turned,
    window,
    field,
):
    steps, layers = wind_ref.shape[0], wind_ref.shape[2]
    across = amp_ref.shape[1] // LANES
    me = lax.axis_index("star")
    row = lax.broadcasted_iota(jnp.int32, (SIDE, LANES), 0)
    lane = lax.broadcasted_iota(jnp.int32, (SIDE, LANES), 1)
    offsets, lefts = own_row(rows_ref, me), own_row(cols_ref, me)
    shifts = [wind_ref[step] for step in range(steps)]

    depth = in_ref.shape[1]
    for x in range(GROUP):
        seen = in_ref[x].astype(F32)
        for unit in range(layers * THIRD):
            turned[unit, pl.ds(x * depth, depth), :] = seen[:, unit * LANES : (unit + 1) * LANES]
    for layer in range(layers):
        part = lax.rem(offsets[layer], SIDE)
        for a in range(QUART):
            for b in range(THIRD):
                unit = layer * THIRD + b
                slot = layer * SPAN + THIRD * a + b
                for u in range(2):
                    early = row[0:GROUP] + GROUP * u < part
                    one, two = (
                        turned[unit, pl.ds(e * 2 * QUART + 2 * a + u, GROUP, stride=depth), :]
                        for e in range(2)
                    )
                    for turn, value in enumerate((one, jnp.where(early, one, two), two)):
                        window[slot, pl.ds(turn * SIDE + u * GROUP, GROUP), :] = value

    for step in range(steps):
        phase = [None] * across
        for layer in range(layers):
            left = lefts[layer]
            tile = jnp.minimum(lax.div(left, LANES), total_tiles - SPAN)
            shift = left - tile * LANES + shifts[step][1, layer]
            skip = lax.div(shift, LANES)
            fine = lax.rem(shift, LANES)
            start = lax.rem(offsets[layer], SIDE) + shifts[step][0, layer]
            inside = lane < LANES - fine
            rolled = [
                pltpu.roll(
                    window[layer * SPAN + skip + t, pl.ds(start, SIDE), :],
                    lax.rem(LANES - fine, LANES),
                    axis=1,
                )
                for t in range(across + 1)
            ]
            for t in range(across):
                value = jnp.where(inside, rolled[t], rolled[t + 1])
                phase[t] = value if phase[t] is None else phase[t] + value
        for t in range(across):
            sine, cosine = sin_cos(phase[t])
            amp = amp_ref[:, t * LANES : (t + 1) * LANES]
            rows = pl.ds((step * across + t) * SIDE, SIDE)
            for part, value in enumerate((amp * cosine, amp * sine)):
                high, low = split(value)
                at = part * LANES
                field[rows, at : at + LANES] = high
                field[rows, at + 2 * LANES : at + 3 * LANES] = low
                field[rows, at + 4 * LANES : at + 5 * LANES] = high

    first = matmul(field[...], across_ref[...])

    wide_out = first.shape[1] // 2
    wide = SIDE * SIDE
    lane8 = lax.broadcasted_iota(jnp.int32, (8, LANES), 1)
    turns = steps * across
    found = []
    for big in range(0, turns, 8):
        smalls = []
        for turn in range(big, min(big + 8, turns)):
            rows = pl.ds(turn * SIDE, SIDE)
            real_high, real_low = split(first[turn * SIDE : (turn + 1) * SIDE, 0:wide_out])
            imag_high, imag_low = split(first[turn * SIDE : (turn + 1) * SIDE, wide_out : 2 * wide_out])
            stacked = jnp.concatenate(
                [real_high, imag_high, real_low, imag_low, real_high, imag_high], axis=0
            )
            spectrum = matmul(down_ref[...], stacked)
            power = spectrum * spectrum
            total = power[0:SIDE]
            for k in range(1, 2 * BIN):
                total = total + power[k * SIDE : (k + 1) * SIDE]
            small = total[:, 0:LANES]
            for k in range(1, BIN):
                small = small + total[:, k * LANES : (k + 1) * LANES]
            smalls.append(small)
        while len(smalls) < 8:
            smalls.append(jnp.ones((SIDE, LANES), F32))
        flipped = jnp.concatenate(smalls, axis=0).T
        halves = []
        for half in range(2):
            regs = [flipped[(half * 8 + q) * 8 : (half * 8 + q + 1) * 8] for q in range(8)]
            for jump in (4, 2, 1):
                keep = ((lane8 >> 4) & jump) == 0
                for i in range(8):
                    if i & jump == 0:
                        one, two = regs[i], regs[i + jump]
                        regs[i] = jnp.where(keep, one, pltpu.roll(two, jump * SIDE, axis=1))
                        regs[i + jump] = jnp.where(
                            keep, pltpu.roll(one, LANES - jump * SIDE, axis=1), two
                        )
            halves.append(regs)
        image = jnp.concatenate(
            [jnp.concatenate([halves[0][g], halves[1][g]], axis=1) for g in range(8)], axis=0
        )
        image = image * (1.0 / jnp.sum(image, axis=1, keepdims=True))
        high, low = split(image)
        found.append(jnp.concatenate([high, low, high], axis=1))
    out_ref[...] = matmul(jnp.concatenate(found, axis=0), table[...])[0 : out_ref.shape[0]]


def spots_call(stars, devices, total_tiles, foot_rows, foot_cols, wind, strips, amplitude, table):
    vmem = pl.BlockSpec(memory_space=pltpu.VMEM)
    steps, layers = wind.shape[0], wind.shape[2]
    depth = strips.shape[1]
    subs = amplitude.shape[1] // SIDE
    high, low = across_tables()
    table_across = np.concatenate([high, high, low], axis=0)
    count = steps * subs
    padded = -(-count // 64) * 64
    return pl.pallas_call(
        functools.partial(spots_kernel, stars, devices, total_tiles),
        out_shape=jax.ShapeDtypeStruct((count, SIDE * SIDE), F32),
        in_specs=[vmem] * 8,
        out_specs=vmem,
        scratch_shapes=[
            pltpu.VMEM((layers * THIRD, GROUP * depth, LANES), F32),
            pltpu.VMEM((layers * SPAN, 3 * SIDE, LANES), F32),
            pltpu.VMEM((count // 8 * SIDE, 6 * LANES), BF16),
        ],
        compiler_params=pltpu.CompilerParams(vmem_limit_bytes=16 << 20),
        name="spots",
    )(foot_rows, foot_cols, wind, strips, amplitude, table, table_across, down_table())


def shards(screens, foot_rows, foot_cols, wind, amplitude, owner, refs):
    stars, devices = lax.axis_size("star"), lax.axis_size("dev")
    layers, _, side, width = screens.shape
    steps = wind.shape[0]
    foot_rows, foot_cols = foot_rows.T, foot_cols.T
    wind = wind.transpose(0, 2, 1)
    tiles = width // LANES
    held = min(SPAN, tiles)
    subs = amplitude.shape[1] // side
    smem = pl.BlockSpec(memory_space=pltpu.SMEM)
    vmem = pl.BlockSpec(memory_space=pltpu.VMEM)
    hbm = pl.BlockSpec(memory_space=pltpu.HBM)
    screens = pltpu.with_memory_space_constraint(screens, pltpu.HBM)
    crops = pl.pallas_call(
        functools.partial(crop_kernel, stars, devices),
        out_shape=[jax.ShapeDtypeStruct((2 * layers, side, held * LANES), BF16)] * stars,
        in_specs=[hbm] * 3,
        out_specs=[vmem] * stars,
        scratch_shapes=[
            pltpu.SemaphoreType.DMA((stars, 2 * layers)),
            pltpu.SMEM(foot_rows.shape, jnp.int32),
            pltpu.SMEM(foot_cols.shape, jnp.int32),
            pltpu.SemaphoreType.DMA((2,)),
        ],
        compiler_params=pltpu.CompilerParams(vmem_limit_bytes=2 << 20),
        name="crop",
    )(
        pltpu.with_memory_space_constraint(foot_rows, pltpu.HBM),
        pltpu.with_memory_space_constraint(foot_cols, pltpu.HBM),
        screens,
    )
    parts = [crops[0]]
    for turn in range(1, stars):
        parts.append(
            lax.ppermute(crops[turn], "star", [(i, (i + turn) % stars) for i in range(stars)])
        )
    block = jax.ShapeDtypeStruct((devices, 2 * QUART, layers * THIRD * LANES), BF16)
    groups = [[g + x for x in range(GROUP)] for g in range(0, devices, GROUP)]
    wide = SIDE * SIDE
    table = pl.pallas_call(
        table_kernel,
        out_shape=jax.ShapeDtypeStruct((3 * wide, wide), BF16),
        in_specs=[smem, vmem],
        out_specs=vmem,
        compiler_params=pltpu.CompilerParams(vmem_limit_bytes=2 << 20),
        name="table",
    )(owner, refs)
    sent = pl.pallas_call(
        functools.partial(spread_kernel, stars, devices, tiles),
        out_shape=block,
        in_specs=[vmem, vmem, pl.BlockSpec(memory_space=pl.ANY)] + [vmem] * stars,
        out_specs=vmem,
        scratch_shapes=[pltpu.VMEM((2, layers * THIRD, QUART * SIDE, LANES), F32)],
        compiler_params=pltpu.CompilerParams(vmem_limit_bytes=4 << 20),
        name="spread",
    )(foot_rows, foot_cols, table, *parts)
    held_rows = lax.all_to_all(sent, "dev", 0, 0, tiled=True)
    chosen = pl.pallas_call(
        functools.partial(choose_kernel, devices),
        out_shape=jax.ShapeDtypeStruct((GROUP, 4 * QUART, block.shape[2]), BF16),
        in_specs=[vmem, vmem],
        out_specs=vmem,
        compiler_params=pltpu.CompilerParams(vmem_limit_bytes=2 << 20),
        name="choose",
    )(foot_rows, held_rows)
    strips = lax.all_to_all(chosen, "dev", 0, 0, axis_index_groups=groups, tiled=True)
    found = spots_call(
        stars, devices, stars * tiles, foot_rows, foot_cols, wind, strips, amplitude, table
    )
    return found.reshape(steps, 1, 1, subs, SIDE * SIDE)


def solution(mesh):
    in_specs = (P(None, None, "dev", "star"), P(), P(), P(), P("dev", None), P("star", "dev"), P())
    out_specs = P(None, "star", "dev", None, None)
    return jax.shard_map(shards, mesh=mesh, in_specs=in_specs, out_specs=out_specs, check_vma=False)
```

```python
import functools
import math

import jax
import jax.numpy as jnp
import numpy as np
from jax import lax
from jax.experimental import pallas as pl
from jax.experimental.pallas import tpu as pltpu
from jax.sharding import PartitionSpec as P

BIN = 4
SIDE = 16
LANES = 128
SPAN = 12
QUART = 4
THIRD = SPAN // QUART
GROUP = 8

F32 = jnp.float32
BF16 = jnp.bfloat16


def split_np(table):
    high = table.astype(jnp.bfloat16)
    low = (table - high.astype(np.float64)).astype(jnp.bfloat16)
    return high, low


def split(value):
    high = value.astype(BF16)
    return high, (value - high.astype(F32)).astype(BF16)


def across_tables():
    length = BIN * SIDE
    freq = (np.arange(length) + length // 2) % length
    angle = 2.0 * math.pi * (np.outer(np.arange(SIDE), freq) % length) / length
    real, imag = np.cos(angle), -np.sin(angle)
    out = np.zeros((2, 8, SIDE, 2, BIN, SIDE, 8))
    for i in range(8):
        for b in range(BIN):
            re, im = real[:, b::BIN], imag[:, b::BIN]
            out[0, i, :, 0, b, :, i] = re
            out[1, i, :, 0, b, :, i] = -im
            out[0, i, :, 1, b, :, i] = im
            out[1, i, :, 1, b, :, i] = re
    return split_np(out.reshape(2 * 8 * SIDE, 2 * BIN * SIDE * 8))


def down_table():
    length = BIN * SIDE
    freq = (np.arange(length) + length // 2) % length
    angle = 2.0 * math.pi * (np.outer(freq, np.arange(SIDE)) % length) / length
    real, imag = np.cos(angle), -np.sin(angle)
    order = np.concatenate([np.arange(a, length, BIN) for a in range(BIN)])
    real, imag = real[order], imag[order]
    table = np.block([[real, -imag], [imag, real]])
    high, low = split_np(table)
    return np.concatenate([high, high, low], axis=1)


def place_of(rows_ref, cols_ref, layer, star, devices, total_tiles):
    offset = rows_ref[star, layer]
    strip = lax.div(offset, SIDE)
    part = lax.rem(offset, SIDE)
    tile = jnp.minimum(lax.div(cols_ref[star, layer], LANES), total_tiles - SPAN)
    return strip, part, tile


def own_row(ref, star):
    row = ref[pl.ds(star, 1), :]
    return [row[0, layer] for layer in range(ref.shape[1])]


def place_of_own(offset, left, total_tiles):
    strip = lax.div(offset, SIDE)
    part = lax.rem(offset, SIDE)
    tile = jnp.minimum(lax.div(left, LANES), total_tiles - SPAN)
    return strip, part, tile


def first_tile(tile, panel, tiles, held):
    return jnp.clip(tile - panel * tiles, 0, tiles - held)


def crop_kernel(stars, devices, rows_hbm, cols_hbm, screens_ref, *rest):
    outs, (sem, rows_ref, cols_ref, scalar_sem) = rest[:stars], rest[stars:]
    scalars = [
        pltpu.make_async_copy(rows_hbm, rows_ref, scalar_sem.at[0]),
        pltpu.make_async_copy(cols_hbm, cols_ref, scalar_sem.at[1]),
    ]
    for copy in scalars:
        copy.start()
    for copy in scalars:
        copy.wait()
    layers, bands, side, width = screens_ref.shape
    tiles = width // LANES
    held = min(SPAN, tiles)
    me = lax.axis_index("star")
    place = lax.axis_index("dev")
    copies = []
    for turn in range(stars):
        star = lax.rem(me + turn, stars)
        for layer in range(layers):
            strip, _, tile = place_of(rows_ref, cols_ref, layer, star, devices, stars * tiles)
            behind = lax.rem(place + bands * devices - strip, devices)
            band = lax.div(strip + behind, devices)
            start = first_tile(tile, me, tiles, held)
            columns = pl.ds(pl.multiple_of(start * LANES, LANES), held * LANES)
            for slot in range(2):
                copy = pltpu.make_async_copy(
                    screens_ref.at[layer, lax.rem(band + slot, bands), :, columns],
                    outs[turn].at[2 * layer + slot],
                    sem.at[turn, 2 * layer + slot],
                )
                copy.start()
                copies.append(copy)
    for copy in copies:
        copy.wait()


def spread_kernel(stars, devices, tiles, rows_ref, cols_ref, _, *rest):
    parts, out_ref, turned = rest[:stars], rest[stars], rest[stars + 1]
    layers = parts[0].shape[0] // 2
    held = parts[0].shape[2] // LANES
    me = lax.axis_index("star")
    place = lax.axis_index("dev")
    row = lax.broadcasted_iota(jnp.int32, (SIDE, LANES), 0)
    offsets, lefts = own_row(rows_ref, me), own_row(cols_ref, me)
    for layer in range(layers):
        strip, part, tile = place_of_own(offsets[layer], lefts[layer], stars * tiles)
        behind = lax.rem(place + (1 << 20) * devices - strip, devices)
        wraps = row < jnp.where(behind == 0, SIDE, jnp.where(behind == 1, part, 0))
        for a in range(QUART):
            for b in range(THIRD):
                spot = tile + (THIRD * a + b)
                panel = lax.div(spot, tiles)
                pair = []
                for slot in range(2):
                    value = None
                    for turn in range(stars):
                        sender = lax.rem(me + stars - turn, stars)
                        start = first_tile(tile, sender, tiles, held)
                        local = jnp.clip(spot - sender * tiles - start, 0, held - 1)
                        lanes = pl.ds(pl.multiple_of(local * LANES, LANES), LANES)
                        seen = parts[turn][2 * layer + slot, :, lanes].astype(F32)
                        if value is None:
                            value = seen
                        else:
                            value = jnp.where(panel == sender, seen, value)
                    pair.append(value)
                rows = pl.ds(a, SIDE, stride=QUART)
                turned[0, layer * THIRD + b, rows, :] = pair[0]
                turned[1, layer * THIRD + b, rows, :] = jnp.where(wraps, pair[1], pair[0])
    half = GROUP // 2
    last = devices // GROUP - 1
    for m in range(half):
        for kind in range(2):
            rows = slice(m * SIDE, (m + 1) * SIDE)
            pieces = [turned[kind, unit, rows, :] for unit in range(layers * THIRD)]
            block = jnp.concatenate(pieces, axis=1).astype(BF16)
            if kind == 1:
                out_ref[last * half + m] = block
            else:
                for group in range(last):
                    out_ref[group * half + m] = block


def choose_kernel(devices, rows_ref, in_ref, out_ref):
    layers = rows_ref.shape[1]
    width = in_ref.shape[2] // layers
    me = lax.axis_index("star")
    place = lax.axis_index("dev")
    first = place - lax.rem(place, GROUP)
    odd = lax.rem(place, 2)
    m = lax.div(place - first, 2)
    row = lax.broadcasted_iota(jnp.int32, (SIDE, width), 0)
    residue = m * QUART + lax.div(row, QUART)
    offsets = own_row(rows_ref, me)
    for layer in range(layers):
        offset = offsets[layer]
        early = residue < lax.rem(offset, SIDE)
        lanes = slice(layer * width, (layer + 1) * width)
        for j in range(GROUP):
            start = lax.div(offset, SIDE) + first + j
            step = lax.rem(start + odd, 2)
            late_from = lax.div(lax.rem(start + step, devices), 2)
            early_from = lax.div(lax.rem(start + 2 - step, devices), 2)
            out_ref[j, :, lanes] = jnp.where(
                early,
                in_ref[early_from, :, lanes].astype(F32),
                in_ref[late_from, :, lanes].astype(F32),
            ).astype(BF16)


def sin_cos(value):
    turns = jnp.floor(value * (2.0 / math.pi) + 0.5)
    rest = value - turns * 1.5703125
    rest = rest - turns * 4.837512969970703125e-4
    rest = rest - turns * 7.549789948768648e-8
    square = rest * rest
    sine = rest + rest * square * (
        -1.6666654611e-1 + square * (8.3321608736e-3 - square * 1.9515295891e-4)
    )
    cosine = (
        1.0
        - 0.5 * square
        + square
        * square
        * (4.166664568298827e-2 + square * (-1.388731625493765e-3 + square * 2.443315711809948e-5))
    )
    quarter = turns.astype(jnp.int32)
    odd = (quarter & 1) == 1
    flip_sine = (quarter & 2) == 2
    flip_cosine = ((quarter + 1) & 2) == 2
    s = jnp.where(odd, cosine, sine)
    c = jnp.where(odd, sine, cosine)
    return jnp.where(flip_sine, -s, s), jnp.where(flip_cosine, -c, c)


def matmul(left, right):
    return lax.dot_general(
        left, right, (((1,), (0,)), ((), ())), preferred_element_type=F32
    )


def table_kernel(owner_ref, refs_ref, table):
    refer = refs_ref[owner_ref[0, 0]]
    wide = SIDE * SIDE
    pick_row = lax.broadcasted_iota(jnp.int32, (SIDE, wide), 0)
    pick_lane = lax.broadcasted_iota(jnp.int32, (SIDE, wide), 1)
    pick = (pick_row == ((SIDE - (pick_lane & 15)) & 15)).astype(F32)
    base = lax.dot_general(
        refer,
        pick,
        (((1,), (0,)), ((), ())),
        precision=lax.Precision.HIGHEST,
        preferred_element_type=F32,
    )
    for bit in range(4):
        moved = pltpu.roll(base, 1 << bit, axis=0)
        base = jnp.where(((pick_lane >> (4 + bit)) & 1) == 1, moved, base)
    for q in range(SIDE):
        if q == 0:
            block = base
        else:
            block = jnp.where(
                (pick_lane & 15) >= q,
                pltpu.roll(base, q, axis=1),
                pltpu.roll(base, wide + q - SIDE, axis=1),
            )
        high, low = split(block)
        table[pl.ds(q * SIDE, SIDE), :] = high
        table[pl.ds(wide + q * SIDE, SIDE), :] = high
        table[pl.ds(2 * wide + q * SIDE, SIDE), :] = low


def spots_kernel(
    stars,
    devices,
    total_tiles,
    rows_ref,
    cols_ref,
    wind_ref,
    in_ref,
    amp_ref,
    table,
    across_ref,
    down_ref,
    out_ref,
    turned,
    window,
    field,
):
    steps, layers = wind_ref.shape[0], wind_ref.shape[2]
    across = amp_ref.shape[1] // LANES
    me = lax.axis_index("star")
    place = lax.axis_index("dev")
    lane = lax.broadcasted_iota(jnp.int32, (SIDE, LANES), 1)
    offsets, lefts = own_row(rows_ref, me), own_row(cols_ref, me)
    shifts = [wind_ref[step] for step in range(steps)]

    half = GROUP // 2
    for x in range(GROUP):
        seen = in_ref[x].astype(F32)
        at = (x % 2) * half * SIDE + x // 2 * SIDE
        for unit in range(layers * THIRD):
            turned[unit, pl.ds(at, SIDE), :] = seen[:, unit * LANES : (unit + 1) * LANES]
    for layer in range(layers):
        odd = lax.rem(lax.div(offsets[layer], SIDE) + place, 2)
        for a in range(QUART):
            for b in range(THIRD):
                unit = layer * THIRD + b
                slot = layer * SPAN + THIRD * a + b
                one, two = (
                    turned[unit, pl.ds(parity * half * SIDE + a, SIDE, stride=QUART), :]
                    for parity in (odd, 1 - odd)
                )
                for turn, value in enumerate((one, two, one)):
                    window[slot, pl.ds(turn * SIDE, SIDE), :] = value

    for step in range(steps):
        phase = [None] * across
        for layer in range(layers):
            left = lefts[layer]
            tile = jnp.minimum(lax.div(left, LANES), total_tiles - SPAN)
            shift = left - tile * LANES + shifts[step][1, layer]
            skip = lax.div(shift, LANES)
            fine = lax.rem(shift, LANES)
            start = lax.rem(offsets[layer], SIDE) + shifts[step][0, layer]
            inside = lane < LANES - fine
            rolled = [
                pltpu.roll(
                    window[layer * SPAN + skip + t, pl.ds(start, SIDE), :],
                    lax.rem(LANES - fine, LANES),
                    axis=1,
                )
                for t in range(across + 1)
            ]
            for t in range(across):
                value = jnp.where(inside, rolled[t], rolled[t + 1])
                phase[t] = value if phase[t] is None else phase[t] + value
        for t in range(across):
            sine, cosine = sin_cos(phase[t])
            amp = amp_ref[:, t * LANES : (t + 1) * LANES]
            rows = pl.ds((step * across + t) * SIDE, SIDE)
            for part, value in enumerate((amp * cosine, amp * sine)):
                high, low = split(value)
                at = part * LANES
                field[rows, at : at + LANES] = high
                field[rows, at + 2 * LANES : at + 3 * LANES] = low
                field[rows, at + 4 * LANES : at + 5 * LANES] = high

    first = matmul(field[...], across_ref[...])

    wide_out = first.shape[1] // 2
    wide = SIDE * SIDE
    lane8 = lax.broadcasted_iota(jnp.int32, (8, LANES), 1)
    turns = steps * across
    found = []
    for big in range(0, turns, 8):
        smalls = []
        for turn in range(big, min(big + 8, turns)):
            rows = pl.ds(turn * SIDE, SIDE)
            real_high, real_low = split(first[turn * SIDE : (turn + 1) * SIDE, 0:wide_out])
            imag_high, imag_low = split(first[turn * SIDE : (turn + 1) * SIDE, wide_out : 2 * wide_out])
            stacked = jnp.concatenate(
                [real_high, imag_high, real_low, imag_low, real_high, imag_high], axis=0
            )
            spectrum = matmul(down_ref[...], stacked)
            power = spectrum * spectrum
            total = power[0:SIDE]
            for k in range(1, 2 * BIN):
                total = total + power[k * SIDE : (k + 1) * SIDE]
            small = total[:, 0:LANES]
            for k in range(1, BIN):
                small = small + total[:, k * LANES : (k + 1) * LANES]
            smalls.append(small)
        while len(smalls) < 8:
            smalls.append(jnp.ones((SIDE, LANES), F32))
        flipped = jnp.concatenate(smalls, axis=0).T
        halves = []
        for half in range(2):
            regs = [flipped[(half * 8 + q) * 8 : (half * 8 + q + 1) * 8] for q in range(8)]
            for jump in (4, 2, 1):
                keep = ((lane8 >> 4) & jump) == 0
                for i in range(8):
                    if i & jump == 0:
                        one, two = regs[i], regs[i + jump]
                        regs[i] = jnp.where(keep, one, pltpu.roll(two, jump * SIDE, axis=1))
                        regs[i + jump] = jnp.where(
                            keep, pltpu.roll(one, LANES - jump * SIDE, axis=1), two
                        )
            halves.append(regs)
        image = jnp.concatenate(
            [jnp.concatenate([halves[0][g], halves[1][g]], axis=1) for g in range(8)], axis=0
        )
        image = image * (1.0 / jnp.sum(image, axis=1, keepdims=True))
        high, low = split(image)
        found.append(jnp.concatenate([high, low, high], axis=1))
    out_ref[...] = matmul(jnp.concatenate(found, axis=0), table[...])[0 : out_ref.shape[0]]


def spots_call(stars, devices, total_tiles, foot_rows, foot_cols, wind, strips, amplitude, table):
    vmem = pl.BlockSpec(memory_space=pltpu.VMEM)
    steps, layers = wind.shape[0], wind.shape[2]
    depth = strips.shape[1]
    subs = amplitude.shape[1] // SIDE
    high, low = across_tables()
    table_across = np.concatenate([high, high, low], axis=0)
    count = steps * subs
    padded = -(-count // 64) * 64
    return pl.pallas_call(
        functools.partial(spots_kernel, stars, devices, total_tiles),
        out_shape=jax.ShapeDtypeStruct((count, SIDE * SIDE), F32),
        in_specs=[vmem] * 8,
        out_specs=vmem,
        scratch_shapes=[
            pltpu.VMEM((layers * THIRD, GROUP * depth, LANES), F32),
            pltpu.VMEM((layers * SPAN, 3 * SIDE, LANES), F32),
            pltpu.VMEM((count // 8 * SIDE, 6 * LANES), BF16),
        ],
        compiler_params=pltpu.CompilerParams(vmem_limit_bytes=16 << 20),
        name="spots",
    )(foot_rows, foot_cols, wind, strips, amplitude, table, table_across, down_table())


def shards(screens, foot_rows, foot_cols, wind, amplitude, owner, refs):
    stars, devices = lax.axis_size("star"), lax.axis_size("dev")
    layers, _, side, width = screens.shape
    steps = wind.shape[0]
    foot_rows, foot_cols = foot_rows.T, foot_cols.T
    wind = wind.transpose(0, 2, 1)
    tiles = width // LANES
    held = min(SPAN, tiles)
    subs = amplitude.shape[1] // side
    smem = pl.BlockSpec(memory_space=pltpu.SMEM)
    vmem = pl.BlockSpec(memory_space=pltpu.VMEM)
    hbm = pl.BlockSpec(memory_space=pltpu.HBM)
    screens = pltpu.with_memory_space_constraint(screens, pltpu.HBM)
    crops = pl.pallas_call(
        functools.partial(crop_kernel, stars, devices),
        out_shape=[jax.ShapeDtypeStruct((2 * layers, side, held * LANES), BF16)] * stars,
        in_specs=[hbm] * 3,
        out_specs=[vmem] * stars,
        scratch_shapes=[
            pltpu.SemaphoreType.DMA((stars, 2 * layers)),
            pltpu.SMEM(foot_rows.shape, jnp.int32),
            pltpu.SMEM(foot_cols.shape, jnp.int32),
            pltpu.SemaphoreType.DMA((2,)),
        ],
        compiler_params=pltpu.CompilerParams(vmem_limit_bytes=2 << 20),
        name="crop",
    )(
        pltpu.with_memory_space_constraint(foot_rows, pltpu.HBM),
        pltpu.with_memory_space_constraint(foot_cols, pltpu.HBM),
        screens,
    )
    parts = [crops[0]]
    for turn in range(1, stars):
        parts.append(
            lax.ppermute(crops[turn], "star", [(i, (i + turn) % stars) for i in range(stars)])
        )
    block = jax.ShapeDtypeStruct((devices // 2, SIDE, layers * THIRD * LANES), BF16)
    parities = [list(range(c, devices, 2)) for c in range(2)]
    groups = [[g + x for x in range(GROUP)] for g in range(0, devices, GROUP)]
    wide = SIDE * SIDE
    table = pl.pallas_call(
        table_kernel,
        out_shape=jax.ShapeDtypeStruct((3 * wide, wide), BF16),
        in_specs=[smem, vmem],
        out_specs=vmem,
        compiler_params=pltpu.CompilerParams(vmem_limit_bytes=2 << 20),
        name="table",
    )(owner, refs)
    sent = pl.pallas_call(
        functools.partial(spread_kernel, stars, devices, tiles),
        out_shape=block,
        in_specs=[vmem, vmem, pl.BlockSpec(memory_space=pl.ANY)] + [vmem] * stars,
        out_specs=vmem,
        scratch_shapes=[pltpu.VMEM((2, layers * THIRD, QUART * SIDE, LANES), F32)],
        compiler_params=pltpu.CompilerParams(vmem_limit_bytes=4 << 20),
        name="spread",
    )(foot_rows, foot_cols, table, *parts)
    held_rows = lax.all_to_all(sent, "dev", 0, 0, axis_index_groups=parities, tiled=True)
    chosen = pl.pallas_call(
        functools.partial(choose_kernel, devices),
        out_shape=jax.ShapeDtypeStruct((GROUP,) + block.shape[1:], BF16),
        in_specs=[vmem, vmem],
        out_specs=vmem,
        compiler_params=pltpu.CompilerParams(vmem_limit_bytes=2 << 20),
        name="choose",
    )(foot_rows, held_rows)
    strips = lax.all_to_all(chosen, "dev", 0, 0, axis_index_groups=groups, tiled=True)
    found = spots_call(
        stars, devices, stars * tiles, foot_rows, foot_cols, wind, strips, amplitude, table
    )
    return found.reshape(steps, 1, 1, subs, SIDE * SIDE)


def solution(mesh):
    in_specs = (P(None, None, "dev", "star"), P(), P(), P(), P("dev", None), P("star", "dev"), P())
    out_specs = P(None, "star", "dev", None, None)
    return jax.shard_map(shards, mesh=mesh, in_specs=in_specs, out_specs=out_specs, check_vma=False)
```

```python
import functools
import math

import jax
import jax.numpy as jnp
import numpy as np
from jax import lax
from jax.experimental import pallas as pl
from jax.experimental.pallas import tpu as pltpu
from jax.sharding import PartitionSpec as P

BIN = 4
SIDE = 16
LANES = 128
SPAN = 12
FULL = 10
HALF = FULL // 2
TAIL = 32
GROUP = 8

F32 = jnp.float32
BF16 = jnp.bfloat16


def split_np(table):
    high = table.astype(jnp.bfloat16)
    low = (table - high.astype(np.float64)).astype(jnp.bfloat16)
    return high, low


def split(value):
    high = value.astype(BF16)
    return high, (value - high.astype(F32)).astype(BF16)


def across_tables():
    length = BIN * SIDE
    freq = (np.arange(length) + length // 2) % length
    angle = 2.0 * math.pi * (np.outer(np.arange(SIDE), freq) % length) / length
    real, imag = np.cos(angle), -np.sin(angle)
    out = np.zeros((2, 8, SIDE, 2, BIN, SIDE, 8))
    for i in range(8):
        for b in range(BIN):
            re, im = real[:, b::BIN], imag[:, b::BIN]
            out[0, i, :, 0, b, :, i] = re
            out[1, i, :, 0, b, :, i] = -im
            out[0, i, :, 1, b, :, i] = im
            out[1, i, :, 1, b, :, i] = re
    return split_np(out.reshape(2 * 8 * SIDE, 2 * BIN * SIDE * 8))


def down_table():
    length = BIN * SIDE
    freq = (np.arange(length) + length // 2) % length
    angle = 2.0 * math.pi * (np.outer(freq, np.arange(SIDE)) % length) / length
    real, imag = np.cos(angle), -np.sin(angle)
    order = np.concatenate([np.arange(a, length, BIN) for a in range(BIN)])
    real, imag = real[order], imag[order]
    table = np.block([[real, -imag], [imag, real]])
    high, low = split_np(table)
    return np.concatenate([high, high, low], axis=1)


def place_of(rows_ref, cols_ref, layer, star, devices, total_tiles):
    offset = rows_ref[star, layer]
    strip = lax.div(offset, SIDE)
    part = lax.rem(offset, SIDE)
    tile = jnp.minimum(lax.div(cols_ref[star, layer], LANES), total_tiles - SPAN)
    return strip, part, tile


def own_row(ref, star):
    row = ref[pl.ds(star, 1), :]
    return [row[0, layer] for layer in range(ref.shape[1])]


def place_of_own(offset, left, total_tiles):
    strip = lax.div(offset, SIDE)
    part = lax.rem(offset, SIDE)
    tile = jnp.minimum(lax.div(left, LANES), total_tiles - SPAN)
    return strip, part, tile


def first_tile(tile, panel, tiles, held):
    return jnp.clip(tile - panel * tiles, 0, tiles - held)


def crop_kernel(stars, devices, rows_hbm, cols_hbm, screens_ref, *rest):
    outs, (sem, rows_ref, cols_ref, scalar_sem) = rest[:stars], rest[stars:]
    scalars = [
        pltpu.make_async_copy(rows_hbm, rows_ref, scalar_sem.at[0]),
        pltpu.make_async_copy(cols_hbm, cols_ref, scalar_sem.at[1]),
    ]
    for copy in scalars:
        copy.start()
    for copy in scalars:
        copy.wait()
    layers, bands, side, width = screens_ref.shape
    tiles = width // LANES
    held = min(SPAN, tiles)
    me = lax.axis_index("star")
    place = lax.axis_index("dev")
    copies = []
    for turn in range(stars):
        star = lax.rem(me + turn, stars)
        for layer in range(layers):
            strip, _, tile = place_of(rows_ref, cols_ref, layer, star, devices, stars * tiles)
            behind = lax.rem(place + bands * devices - strip, devices)
            band = lax.div(strip + behind, devices)
            start = first_tile(tile, me, tiles, held)
            columns = pl.ds(pl.multiple_of(start * LANES, LANES), held * LANES)
            for slot in range(2):
                copy = pltpu.make_async_copy(
                    screens_ref.at[layer, lax.rem(band + slot, bands), :, columns],
                    outs[turn].at[2 * layer + slot],
                    sem.at[turn, 2 * layer + slot],
                )
                copy.start()
                copies.append(copy)
    for copy in copies:
        copy.wait()


def spread_kernel(stars, devices, tiles, rows_ref, cols_ref, _, *rest):
    parts, out_ref, turned = rest[:stars], rest[stars], rest[stars + 1]
    layers = parts[0].shape[0] // 2
    held = parts[0].shape[2] // LANES
    me = lax.axis_index("star")
    place = lax.axis_index("dev")
    row = lax.broadcasted_iota(jnp.int32, (SIDE, LANES), 0)
    lane = lax.broadcasted_iota(jnp.int32, (SIDE, LANES), 1)
    tails = [None, None]
    offsets, lefts = own_row(rows_ref, me), own_row(cols_ref, me)
    for layer in range(layers):
        strip, part, tile = place_of_own(offsets[layer], lefts[layer], stars * tiles)
        behind = lax.rem(place + (1 << 20) * devices - strip, devices)
        wraps = row < jnp.where(behind == 0, SIDE, jnp.where(behind == 1, part, 0))
        shift = lefts[layer] - tile * LANES
        skip, fine = lax.div(shift, LANES), lax.rem(shift, LANES)
        inside = lane < LANES - fine
        rolled = []
        for t in range(FULL + 2):
            spot = tile + skip + t
            panel = lax.div(spot, tiles)
            pair = []
            for slot in range(2):
                value = None
                for turn in range(stars):
                    sender = lax.rem(me + stars - turn, stars)
                    start = first_tile(tile, sender, tiles, held)
                    local = jnp.clip(spot - sender * tiles - start, 0, held - 1)
                    lanes = pl.ds(pl.multiple_of(local * LANES, LANES), LANES)
                    seen = parts[turn][2 * layer + slot, :, lanes].astype(F32)
                    if value is None:
                        value = seen
                    else:
                        value = jnp.where(panel == sender, seen, value)
                pair.append(value)
            mixed = jnp.where(wraps, pair[1], pair[0])
            rolled.append(
                [pltpu.roll(v, lax.rem(LANES - fine, LANES), axis=1) for v in (pair[0], mixed)]
            )
        for kind in range(2):
            for t in range(FULL + 1):
                value = jnp.where(inside, rolled[t][kind], rolled[t + 1][kind])
                if t < FULL:
                    rows = pl.ds(t // HALF, SIDE, stride=2)
                    turned[kind, layer * HALF + t % HALF, rows, :] = value
                elif layer == 0:
                    tails[kind] = value
                else:
                    value = pltpu.roll(value, layer * TAIL, axis=1)
                    tails[kind] = jnp.where(lane < layer * TAIL, tails[kind], value)
    for kind in range(2):
        for side in range(2):
            turned[kind, layers * HALF, pl.ds(side, SIDE, stride=2), :] = tails[kind]
    half = GROUP // 2
    last = devices // GROUP - 1
    for m in range(half):
        for kind in range(2):
            rows = slice(m * 8, (m + 1) * 8)
            pieces = [turned[kind, unit, rows, :] for unit in range(layers * HALF + 1)]
            block = jnp.concatenate(pieces, axis=1).astype(BF16)
            if kind == 1:
                out_ref[last * half + m] = block
            else:
                for group in range(last):
                    out_ref[group * half + m] = block


def choose_kernel(devices, rows_ref, in_ref, out_ref):
    layers = rows_ref.shape[1]
    width = HALF * LANES
    me = lax.axis_index("star")
    place = lax.axis_index("dev")
    first = place - lax.rem(place, GROUP)
    odd = lax.rem(place, 2)
    m = lax.div(place - first, 2)
    row = lax.broadcasted_iota(jnp.int32, (8, width), 0)
    lane = lax.broadcasted_iota(jnp.int32, (8, LANES), 1)
    residue = m * 4 + lax.div(row, 2)
    offsets = own_row(rows_ref, me)
    last = slice(layers * width, layers * width + LANES)
    tails = [None] * GROUP
    for layer in range(layers):
        offset = offsets[layer]
        early = residue < lax.rem(offset, SIDE)
        lanes = slice(layer * width, (layer + 1) * width)
        for j in range(GROUP):
            start = lax.div(offset, SIDE) + first + j
            step = lax.rem(start + odd, 2)
            late_from = lax.div(lax.rem(start + step, devices), 2)
            early_from = lax.div(lax.rem(start + 2 - step, devices), 2)
            out_ref[j, :, lanes] = jnp.where(
                early,
                in_ref[early_from, :, lanes].astype(F32),
                in_ref[late_from, :, lanes].astype(F32),
            ).astype(BF16)
            tail = jnp.where(
                early[:, 0:LANES],
                in_ref[early_from, :, last].astype(F32),
                in_ref[late_from, :, last].astype(F32),
            )
            tails[j] = tail if layer == 0 else jnp.where(lane < layer * TAIL, tails[j], tail)
    for j in range(GROUP):
        out_ref[j, :, last] = tails[j].astype(BF16)


def sin_cos(value):
    turns = jnp.floor(value * (2.0 / math.pi) + 0.5)
    rest = value - turns * 1.5703125
    rest = rest - turns * 4.837512969970703125e-4
    rest = rest - turns * 7.549789948768648e-8
    square = rest * rest
    sine = rest + rest * square * (
        -1.6666654611e-1 + square * (8.3321608736e-3 - square * 1.9515295891e-4)
    )
    cosine = (
        1.0
        - 0.5 * square
        + square
        * square
        * (4.166664568298827e-2 + square * (-1.388731625493765e-3 + square * 2.443315711809948e-5))
    )
    quarter = turns.astype(jnp.int32)
    odd = (quarter & 1) == 1
    flip_sine = (quarter & 2) == 2
    flip_cosine = ((quarter + 1) & 2) == 2
    s = jnp.where(odd, cosine, sine)
    c = jnp.where(odd, sine, cosine)
    return jnp.where(flip_sine, -s, s), jnp.where(flip_cosine, -c, c)


def matmul(left, right):
    return lax.dot_general(
        left, right, (((1,), (0,)), ((), ())), preferred_element_type=F32
    )


def table_kernel(owner_ref, refs_ref, table):
    refer = refs_ref[owner_ref[0, 0]]
    wide = SIDE * SIDE
    pick_row = lax.broadcasted_iota(jnp.int32, (SIDE, wide), 0)
    pick_lane = lax.broadcasted_iota(jnp.int32, (SIDE, wide), 1)
    pick = (pick_row == ((SIDE - (pick_lane & 15)) & 15)).astype(F32)
    base = lax.dot_general(
        refer,
        pick,
        (((1,), (0,)), ((), ())),
        precision=lax.Precision.HIGHEST,
        preferred_element_type=F32,
    )
    for bit in range(4):
        moved = pltpu.roll(base, 1 << bit, axis=0)
        base = jnp.where(((pick_lane >> (4 + bit)) & 1) == 1, moved, base)
    for q in range(SIDE):
        if q == 0:
            block = base
        else:
            block = jnp.where(
                (pick_lane & 15) >= q,
                pltpu.roll(base, q, axis=1),
                pltpu.roll(base, wide + q - SIDE, axis=1),
            )
        high, low = split(block)
        table[pl.ds(q * SIDE, SIDE), :] = high
        table[pl.ds(wide + q * SIDE, SIDE), :] = high
        table[pl.ds(2 * wide + q * SIDE, SIDE), :] = low


def spots_kernel(
    stars,
    devices,
    total_tiles,
    rows_ref,
    cols_ref,
    wind_ref,
    in_ref,
    amp_ref,
    table,
    across_ref,
    down_ref,
    out_ref,
    turned,
    window,
    field,
):
    steps, layers = wind_ref.shape[0], wind_ref.shape[2]
    across = amp_ref.shape[1] // LANES
    me = lax.axis_index("star")
    place = lax.axis_index("dev")
    lane = lax.broadcasted_iota(jnp.int32, (SIDE, LANES), 1)
    offsets = own_row(rows_ref, me)
    shifts = [wind_ref[step] for step in range(steps)]

    half = GROUP // 2
    for x in range(GROUP):
        seen = in_ref[x].astype(F32)
        at = (x % 2) * half * 8 + x // 2 * 8
        for unit in range(layers * HALF + 1):
            turned[unit, pl.ds(at, 8), :] = seen[:, unit * LANES : (unit + 1) * LANES]
    for layer in range(layers):
        odd = lax.rem(lax.div(offsets[layer], SIDE) + place, 2)
        for t in range(FULL + 1):
            unit = layer * HALF + t % HALF if t < FULL else layers * HALF
            at = t // HALF if t < FULL else 0
            one, two = (
                turned[unit, pl.ds(parity * half * 8 + at, SIDE, stride=2), :]
                for parity in (odd, 1 - odd)
            )
            if t == FULL and layer > 0:
                one, two = (pltpu.roll(v, LANES - layer * TAIL, axis=1) for v in (one, two))
            for turn, value in enumerate((one, two, one)):
                window[layer * (FULL + 1) + t, pl.ds(turn * SIDE, SIDE), :] = value

    for step in range(steps):
        phase = [None] * across
        for layer in range(layers):
            fine = shifts[step][1, layer]
            start = lax.rem(offsets[layer], SIDE) + shifts[step][0, layer]
            inside = lane < LANES - fine
            rolled = [
                pltpu.roll(
                    window[layer * (FULL + 1) + t, pl.ds(start, SIDE), :],
                    lax.rem(LANES - fine, LANES),
                    axis=1,
                )
                for t in range(across + 1)
            ]
            for t in range(across):
                value = jnp.where(inside, rolled[t], rolled[t + 1])
                phase[t] = value if phase[t] is None else phase[t] + value
        for t in range(across):
            sine, cosine = sin_cos(phase[t])
            amp = amp_ref[:, t * LANES : (t + 1) * LANES]
            rows = pl.ds((step * across + t) * SIDE, SIDE)
            for part, value in enumerate((amp * cosine, amp * sine)):
                high, low = split(value)
                at = part * LANES
                field[rows, at : at + LANES] = high
                field[rows, at + 2 * LANES : at + 3 * LANES] = low
                field[rows, at + 4 * LANES : at + 5 * LANES] = high

    first = matmul(field[...], across_ref[...])

    wide_out = first.shape[1] // 2
    wide = SIDE * SIDE
    lane8 = lax.broadcasted_iota(jnp.int32, (8, LANES), 1)
    turns = steps * across
    found = []
    for big in range(0, turns, 8):
        smalls = []
        for turn in range(big, min(big + 8, turns)):
            rows = pl.ds(turn * SIDE, SIDE)
            real_high, real_low = split(first[turn * SIDE : (turn + 1) * SIDE, 0:wide_out])
            imag_high, imag_low = split(first[turn * SIDE : (turn + 1) * SIDE, wide_out : 2 * wide_out])
            stacked = jnp.concatenate(
                [real_high, imag_high, real_low, imag_low, real_high, imag_high], axis=0
            )
            spectrum = matmul(down_ref[...], stacked)
            power = spectrum * spectrum
            total = power[0:SIDE]
            for k in range(1, 2 * BIN):
                total = total + power[k * SIDE : (k + 1) * SIDE]
            small = total[:, 0:LANES]
            for k in range(1, BIN):
                small = small + total[:, k * LANES : (k + 1) * LANES]
            smalls.append(small)
        while len(smalls) < 8:
            smalls.append(jnp.ones((SIDE, LANES), F32))
        flipped = jnp.concatenate(smalls, axis=0).T
        halves = []
        for half in range(2):
            regs = [flipped[(half * 8 + q) * 8 : (half * 8 + q + 1) * 8] for q in range(8)]
            for jump in (4, 2, 1):
                keep = ((lane8 >> 4) & jump) == 0
                for i in range(8):
                    if i & jump == 0:
                        one, two = regs[i], regs[i + jump]
                        regs[i] = jnp.where(keep, one, pltpu.roll(two, jump * SIDE, axis=1))
                        regs[i + jump] = jnp.where(
                            keep, pltpu.roll(one, LANES - jump * SIDE, axis=1), two
                        )
            halves.append(regs)
        image = jnp.concatenate(
            [jnp.concatenate([halves[0][g], halves[1][g]], axis=1) for g in range(8)], axis=0
        )
        image = image * (1.0 / jnp.sum(image, axis=1, keepdims=True))
        high, low = split(image)
        found.append(jnp.concatenate([high, low, high], axis=1))
    out_ref[...] = matmul(jnp.concatenate(found, axis=0), table[...])[0 : out_ref.shape[0]]


def spots_call(stars, devices, total_tiles, foot_rows, foot_cols, wind, strips, amplitude, table):
    vmem = pl.BlockSpec(memory_space=pltpu.VMEM)
    steps, layers = wind.shape[0], wind.shape[2]
    depth = strips.shape[1]
    subs = amplitude.shape[1] // SIDE
    high, low = across_tables()
    table_across = np.concatenate([high, high, low], axis=0)
    count = steps * subs
    padded = -(-count // 64) * 64
    return pl.pallas_call(
        functools.partial(spots_kernel, stars, devices, total_tiles),
        out_shape=jax.ShapeDtypeStruct((count, SIDE * SIDE), F32),
        in_specs=[vmem] * 8,
        out_specs=vmem,
        scratch_shapes=[
            pltpu.VMEM((layers * HALF + 1, GROUP * depth, LANES), F32),
            pltpu.VMEM((layers * (FULL + 1), 3 * SIDE, LANES), F32),
            pltpu.VMEM((count // 8 * SIDE, 6 * LANES), BF16),
        ],
        compiler_params=pltpu.CompilerParams(vmem_limit_bytes=16 << 20),
        name="spots",
    )(foot_rows, foot_cols, wind, strips, amplitude, table, table_across, down_table())


def shards(screens, foot_rows, foot_cols, wind, amplitude, owner, refs):
    stars, devices = lax.axis_size("star"), lax.axis_size("dev")
    layers, _, side, width = screens.shape
    steps = wind.shape[0]
    foot_rows, foot_cols = foot_rows.T, foot_cols.T
    wind = wind.transpose(0, 2, 1)
    tiles = width // LANES
    held = min(SPAN, tiles)
    subs = amplitude.shape[1] // side
    smem = pl.BlockSpec(memory_space=pltpu.SMEM)
    vmem = pl.BlockSpec(memory_space=pltpu.VMEM)
    hbm = pl.BlockSpec(memory_space=pltpu.HBM)
    screens = pltpu.with_memory_space_constraint(screens, pltpu.HBM)
    crops = pl.pallas_call(
        functools.partial(crop_kernel, stars, devices),
        out_shape=[jax.ShapeDtypeStruct((2 * layers, side, held * LANES), BF16)] * stars,
        in_specs=[hbm] * 3,
        out_specs=[vmem] * stars,
        scratch_shapes=[
            pltpu.SemaphoreType.DMA((stars, 2 * layers)),
            pltpu.SMEM(foot_rows.shape, jnp.int32),
            pltpu.SMEM(foot_cols.shape, jnp.int32),
            pltpu.SemaphoreType.DMA((2,)),
        ],
        compiler_params=pltpu.CompilerParams(vmem_limit_bytes=2 << 20),
        name="crop",
    )(
        pltpu.with_memory_space_constraint(foot_rows, pltpu.HBM),
        pltpu.with_memory_space_constraint(foot_cols, pltpu.HBM),
        screens,
    )
    parts = [crops[0]]
    for turn in range(1, stars):
        parts.append(
            lax.ppermute(crops[turn], "star", [(i, (i + turn) % stars) for i in range(stars)])
        )
    block = jax.ShapeDtypeStruct((devices // 2, 8, (layers * HALF + 1) * LANES), BF16)
    parities = [list(range(c, devices, 2)) for c in range(2)]
    groups = [[g + x for x in range(GROUP)] for g in range(0, devices, GROUP)]
    wide = SIDE * SIDE
    table = pl.pallas_call(
        table_kernel,
        out_shape=jax.ShapeDtypeStruct((3 * wide, wide), BF16),
        in_specs=[smem, vmem],
        out_specs=vmem,
        compiler_params=pltpu.CompilerParams(vmem_limit_bytes=2 << 20),
        name="table",
    )(owner, refs)
    sent = pl.pallas_call(
        functools.partial(spread_kernel, stars, devices, tiles),
        out_shape=block,
        in_specs=[vmem, vmem, pl.BlockSpec(memory_space=pl.ANY)] + [vmem] * stars,
        out_specs=vmem,
        scratch_shapes=[pltpu.VMEM((2, layers * HALF + 1, 2 * SIDE, LANES), F32)],
        compiler_params=pltpu.CompilerParams(vmem_limit_bytes=4 << 20),
        name="spread",
    )(foot_rows, foot_cols, table, *parts)
    held_rows = lax.all_to_all(sent, "dev", 0, 0, axis_index_groups=parities, tiled=True)
    chosen = pl.pallas_call(
        functools.partial(choose_kernel, devices),
        out_shape=jax.ShapeDtypeStruct((GROUP,) + block.shape[1:], BF16),
        in_specs=[vmem, vmem],
        out_specs=vmem,
        compiler_params=pltpu.CompilerParams(vmem_limit_bytes=2 << 20),
        name="choose",
    )(foot_rows, held_rows)
    strips = lax.all_to_all(chosen, "dev", 0, 0, axis_index_groups=groups, tiled=True)
    found = spots_call(
        stars, devices, stars * tiles, foot_rows, foot_cols, wind, strips, amplitude, table
    )
    return found.reshape(steps, 1, 1, subs, SIDE * SIDE)


def solution(mesh):
    in_specs = (P(None, None, "dev", "star"), P(), P(), P(), P("dev", None), P("star", "dev"), P())
    out_specs = P(None, "star", "dev", None, None)
    return jax.shard_map(shards, mesh=mesh, in_specs=in_specs, out_specs=out_specs, check_vma=False)
```

```python
import functools
import math

import jax
import jax.numpy as jnp
import numpy as np
from jax import lax
from jax.experimental import pallas as pl
from jax.experimental.pallas import tpu as pltpu
from jax.sharding import PartitionSpec as P

BIN = 4
SIDE = 16
LANES = 128
SPAN = 12
FULL = 10
HALF = FULL // 2
TAIL = 32
GROUP = 8

F32 = jnp.float32
BF16 = jnp.bfloat16


def split_np(table):
    high = table.astype(jnp.bfloat16)
    low = (table - high.astype(np.float64)).astype(jnp.bfloat16)
    return high, low


def split(value):
    high = value.astype(BF16)
    return high, (value - high.astype(F32)).astype(BF16)


def across_tables():
    length = BIN * SIDE
    freq = (np.arange(length) + length // 2) % length
    angle = 2.0 * math.pi * (np.outer(np.arange(SIDE), freq) % length) / length
    real, imag = np.cos(angle), -np.sin(angle)
    out = np.zeros((2, 8, SIDE, 2, BIN, SIDE, 8))
    for i in range(8):
        for b in range(BIN):
            re, im = real[:, b::BIN], imag[:, b::BIN]
            out[0, i, :, 0, b, :, i] = re
            out[1, i, :, 0, b, :, i] = -im
            out[0, i, :, 1, b, :, i] = im
            out[1, i, :, 1, b, :, i] = re
    return split_np(out.reshape(2 * 8 * SIDE, 2 * BIN * SIDE * 8))


def down_table():
    length = BIN * SIDE
    freq = (np.arange(length) + length // 2) % length
    angle = 2.0 * math.pi * (np.outer(freq, np.arange(SIDE)) % length) / length
    real, imag = np.cos(angle), -np.sin(angle)
    order = np.concatenate([np.arange(a, length, BIN) for a in range(BIN)])
    real, imag = real[order], imag[order]
    table = np.block([[real, -imag], [imag, real]])
    high, low = split_np(table)
    return np.concatenate([high, high, low], axis=1)


def place_of(rows_ref, cols_ref, layer, star, devices, total_tiles):
    offset = rows_ref[star, layer]
    strip = lax.div(offset, SIDE)
    part = lax.rem(offset, SIDE)
    tile = jnp.minimum(lax.div(cols_ref[star, layer], LANES), total_tiles - SPAN)
    return strip, part, tile


def own_row(ref, star):
    row = ref[pl.ds(star, 1), :]
    return [row[0, layer] for layer in range(ref.shape[1])]


def place_of_own(offset, left, total_tiles):
    strip = lax.div(offset, SIDE)
    part = lax.rem(offset, SIDE)
    tile = jnp.minimum(lax.div(left, LANES), total_tiles - SPAN)
    return strip, part, tile


def first_tile(tile, panel, tiles, held):
    return jnp.clip(tile - panel * tiles, 0, tiles - held)


def crop_kernel(stars, devices, rows_hbm, cols_hbm, screens_ref, *rest):
    outs, (sem, rows_ref, cols_ref, scalar_sem) = rest[:stars], rest[stars:]
    scalars = [
        pltpu.make_async_copy(rows_hbm, rows_ref, scalar_sem.at[0]),
        pltpu.make_async_copy(cols_hbm, cols_ref, scalar_sem.at[1]),
    ]
    for copy in scalars:
        copy.start()
    for copy in scalars:
        copy.wait()
    layers, bands, side, width = screens_ref.shape
    tiles = width // LANES
    held = min(SPAN, tiles)
    me = lax.axis_index("star")
    place = lax.axis_index("dev")
    copies = []
    for turn in range(stars):
        star = lax.rem(me + turn, stars)
        for layer in range(layers):
            strip, _, tile = place_of(rows_ref, cols_ref, layer, star, devices, stars * tiles)
            behind = lax.rem(place + bands * devices - strip, devices)
            band = lax.div(strip + behind, devices)
            start = first_tile(tile, me, tiles, held)
            columns = pl.ds(pl.multiple_of(start * LANES, LANES), held * LANES)
            for slot in range(2):
                copy = pltpu.make_async_copy(
                    screens_ref.at[layer, lax.rem(band + slot, bands), :, columns],
                    outs[turn].at[2 * layer + slot],
                    sem.at[turn, 2 * layer + slot],
                )
                copy.start()
                copies.append(copy)
    for copy in copies:
        copy.wait()


def spread_kernel(stars, devices, tiles, rows_ref, cols_ref, _, *rest):
    parts, out_ref, turned = rest[:stars], rest[stars], rest[stars + 1]
    layers = parts[0].shape[0] // 2
    held = parts[0].shape[2] // LANES
    me = lax.axis_index("star")
    place = lax.axis_index("dev")
    row = lax.broadcasted_iota(jnp.int32, (SIDE, LANES), 0)
    lane = lax.broadcasted_iota(jnp.int32, (SIDE, LANES), 1)
    tails = [None, None]
    offsets, lefts = own_row(rows_ref, me), own_row(cols_ref, me)
    for layer in range(layers):
        strip, part, tile = place_of_own(offsets[layer], lefts[layer], stars * tiles)
        behind = lax.rem(place + (1 << 20) * devices - strip, devices)
        wraps = row < jnp.where(behind == 0, SIDE, jnp.where(behind == 1, part, 0))
        shift = lefts[layer] - tile * LANES
        skip, fine = lax.div(shift, LANES), lax.rem(shift, LANES)
        inside = lane < LANES - fine
        rolled = []
        for t in range(FULL + 2):
            spot = tile + skip + t
            panel = lax.div(spot, tiles)
            pair = []
            for slot in range(2):
                value = None
                for turn in range(stars):
                    sender = lax.rem(me + stars - turn, stars)
                    start = first_tile(tile, sender, tiles, held)
                    local = jnp.clip(spot - sender * tiles - start, 0, held - 1)
                    lanes = pl.ds(pl.multiple_of(local * LANES, LANES), LANES)
                    seen = parts[turn][2 * layer + slot, :, lanes].astype(F32)
                    if value is None:
                        value = seen
                    else:
                        value = jnp.where(panel == sender, seen, value)
                pair.append(value)
            mixed = jnp.where(wraps, pair[1], pair[0])
            rolled.append(
                [pltpu.roll(v, lax.rem(LANES - fine, LANES), axis=1) for v in (pair[0], mixed)]
            )
        for kind in range(2):
            for t in range(FULL + 1):
                value = jnp.where(inside, rolled[t][kind], rolled[t + 1][kind])
                if t < FULL:
                    rows = pl.ds(t // HALF, SIDE, stride=2)
                    turned[kind, layer * HALF + t % HALF, rows, :] = value
                elif layer == 0:
                    tails[kind] = value
                else:
                    value = pltpu.roll(value, layer * TAIL, axis=1)
                    tails[kind] = jnp.where(lane < layer * TAIL, tails[kind], value)
    for kind in range(2):
        for side in range(2):
            turned[kind, layers * HALF, pl.ds(side, SIDE, stride=2), :] = tails[kind]
    half = GROUP // 2
    last = devices // GROUP - 1
    for m in range(half):
        for kind in range(2):
            rows = slice(m * 8, (m + 1) * 8)
            pieces = [turned[kind, unit, rows, :] for unit in range(layers * HALF + 1)]
            block = jnp.concatenate(pieces, axis=1).astype(BF16)
            if kind == 1:
                out_ref[last * half + m] = block
            else:
                for group in range(last):
                    out_ref[group * half + m] = block


def choose_kernel(devices, rows_ref, in_ref, out_ref):
    layers = rows_ref.shape[1]
    width = HALF * LANES
    me = lax.axis_index("star")
    place = lax.axis_index("dev")
    first = place - lax.rem(place, GROUP)
    odd = lax.rem(place, 2)
    m = lax.div(place - first, 2)
    row = lax.broadcasted_iota(jnp.int32, (8, width), 0)
    lane = lax.broadcasted_iota(jnp.int32, (8, LANES), 1)
    residue = m * 4 + lax.div(row, 2)
    offsets = own_row(rows_ref, me)
    last = slice(layers * width, layers * width + LANES)
    tails = [None] * GROUP
    for layer in range(layers):
        offset = offsets[layer]
        early = residue < lax.rem(offset, SIDE)
        lanes = slice(layer * width, (layer + 1) * width)
        for j in range(GROUP):
            start = lax.div(offset, SIDE) + first + j
            step = lax.rem(start + odd, 2)
            late_from = lax.div(lax.rem(start + step, devices), 2)
            early_from = lax.div(lax.rem(start + 2 - step, devices), 2)
            out_ref[j, :, lanes] = jnp.where(
                early,
                in_ref[early_from, :, lanes].astype(F32),
                in_ref[late_from, :, lanes].astype(F32),
            ).astype(BF16)
            tail = jnp.where(
                early[:, 0:LANES],
                in_ref[early_from, :, last].astype(F32),
                in_ref[late_from, :, last].astype(F32),
            )
            tails[j] = tail if layer == 0 else jnp.where(lane < layer * TAIL, tails[j], tail)
    for j in range(GROUP):
        out_ref[j, :, last] = tails[j].astype(BF16)


def sin_cos(value):
    turns = jnp.floor(value * (2.0 / math.pi) + 0.5)
    rest = value - turns * 1.5703125
    rest = rest - turns * 4.837512969970703125e-4
    rest = rest - turns * 7.549789948768648e-8
    square = rest * rest
    sine = rest + rest * square * (
        -1.6666654611e-1 + square * (8.3321608736e-3 - square * 1.9515295891e-4)
    )
    cosine = (
        1.0
        - 0.5 * square
        + square
        * square
        * (4.166664568298827e-2 + square * (-1.388731625493765e-3 + square * 2.443315711809948e-5))
    )
    quarter = turns.astype(jnp.int32)
    odd = (quarter & 1) == 1
    flip_sine = (quarter & 2) == 2
    flip_cosine = ((quarter + 1) & 2) == 2
    s = jnp.where(odd, cosine, sine)
    c = jnp.where(odd, sine, cosine)
    return jnp.where(flip_sine, -s, s), jnp.where(flip_cosine, -c, c)


def matmul(left, right):
    return lax.dot_general(
        left, right, (((1,), (0,)), ((), ())), preferred_element_type=F32
    )


def table_kernel(owner_ref, refs_ref, table):
    refer = refs_ref[owner_ref[0, 0]]
    wide = SIDE * SIDE
    pick_row = lax.broadcasted_iota(jnp.int32, (SIDE, wide), 0)
    pick_lane = lax.broadcasted_iota(jnp.int32, (SIDE, wide), 1)
    pick = (pick_row == ((SIDE - (pick_lane & 15)) & 15)).astype(F32)
    base = lax.dot_general(
        refer,
        pick,
        (((1,), (0,)), ((), ())),
        precision=lax.Precision.HIGHEST,
        preferred_element_type=F32,
    )
    for bit in range(4):
        moved = pltpu.roll(base, 1 << bit, axis=0)
        base = jnp.where(((pick_lane >> (4 + bit)) & 1) == 1, moved, base)
    for q in range(SIDE):
        if q == 0:
            block = base
        else:
            block = jnp.where(
                (pick_lane & 15) >= q,
                pltpu.roll(base, q, axis=1),
                pltpu.roll(base, wide + q - SIDE, axis=1),
            )
        high, low = split(block)
        table[pl.ds(q * SIDE, SIDE), :] = high
        table[pl.ds(wide + q * SIDE, SIDE), :] = high
        table[pl.ds(2 * wide + q * SIDE, SIDE), :] = low


def spots_kernel(
    stars,
    devices,
    total_tiles,
    rows_ref,
    cols_ref,
    wind_ref,
    in_ref,
    amp_ref,
    table,
    across_ref,
    down_ref,
    out_ref,
    turned,
    window,
    field,
):
    steps, layers = wind_ref.shape[0], wind_ref.shape[2]
    across = amp_ref.shape[1] // LANES
    me = lax.axis_index("star")
    place = lax.axis_index("dev")
    lane = lax.broadcasted_iota(jnp.int32, (SIDE, LANES), 1)
    offsets = own_row(rows_ref, me)
    shifts = [wind_ref[step] for step in range(steps)]

    half = GROUP // 2
    for x in range(GROUP):
        seen = in_ref[x].astype(F32)
        at = (x % 2) * half * 8 + x // 2 * 8
        for unit in range(layers * HALF + 1):
            turned[unit, pl.ds(at, 8), :] = seen[:, unit * LANES : (unit + 1) * LANES]
    for layer in range(layers):
        odd = lax.rem(lax.div(offsets[layer], SIDE) + place, 2)
        for t in range(FULL + 1):
            unit = layer * HALF + t % HALF if t < FULL else layers * HALF
            at = t // HALF if t < FULL else 0
            one, two = (
                turned[unit, pl.ds(parity * half * 8 + at, SIDE, stride=2), :]
                for parity in (odd, 1 - odd)
            )
            if t == FULL and layer > 0:
                one, two = (pltpu.roll(v, LANES - layer * TAIL, axis=1) for v in (one, two))
            for turn, value in enumerate((one, two, one)):
                window[layer * (FULL + 1) + t, pl.ds(turn * SIDE, SIDE), :] = value

    for step in range(steps):
        phase = [None] * across
        for layer in range(layers):
            fine = shifts[step][1, layer]
            start = lax.rem(offsets[layer], SIDE) + shifts[step][0, layer]
            inside = lane < LANES - fine
            rolled = [
                pltpu.roll(
                    window[layer * (FULL + 1) + t, pl.ds(start, SIDE), :],
                    lax.rem(LANES - fine, LANES),
                    axis=1,
                )
                for t in range(across + 1)
            ]
            for t in range(across):
                value = jnp.where(inside, rolled[t], rolled[t + 1])
                phase[t] = value if phase[t] is None else phase[t] + value
        for t in range(across):
            sine, cosine = sin_cos(phase[t])
            amp = amp_ref[:, t * LANES : (t + 1) * LANES]
            rows = pl.ds((step * across + t) * SIDE, SIDE)
            for part, value in enumerate((amp * cosine, amp * sine)):
                high, low = split(value)
                at = part * LANES
                field[rows, at : at + LANES] = high
                field[rows, at + 2 * LANES : at + 3 * LANES] = low
                field[rows, at + 4 * LANES : at + 5 * LANES] = high

    first = matmul(field[...], across_ref[...])

    wide_out = first.shape[1] // 2
    wide = SIDE * SIDE
    lane8 = lax.broadcasted_iota(jnp.int32, (8, LANES), 1)
    turns = steps * across
    found, scales = [], []
    for big in range(0, turns, 8):
        smalls = []
        for turn in range(big, min(big + 8, turns)):
            rows = pl.ds(turn * SIDE, SIDE)
            real_high, real_low = split(first[turn * SIDE : (turn + 1) * SIDE, 0:wide_out])
            imag_high, imag_low = split(first[turn * SIDE : (turn + 1) * SIDE, wide_out : 2 * wide_out])
            stacked = jnp.concatenate(
                [real_high, imag_high, real_low, imag_low, real_high, imag_high], axis=0
            )
            spectrum = matmul(down_ref[...], stacked)
            power = spectrum * spectrum
            total = power[0:SIDE]
            for k in range(1, 2 * BIN):
                total = total + power[k * SIDE : (k + 1) * SIDE]
            small = total[:, 0:LANES]
            for k in range(1, BIN):
                small = small + total[:, k * LANES : (k + 1) * LANES]
            smalls.append(small)
        while len(smalls) < 8:
            smalls.append(jnp.ones((SIDE, LANES), F32))
        flipped = jnp.concatenate(smalls, axis=0).T
        halves = []
        for half in range(2):
            regs = [flipped[(half * 8 + q) * 8 : (half * 8 + q + 1) * 8] for q in range(8)]
            for jump in (4, 2, 1):
                keep = ((lane8 >> 4) & jump) == 0
                for i in range(8):
                    if i & jump == 0:
                        one, two = regs[i], regs[i + jump]
                        regs[i] = jnp.where(keep, one, pltpu.roll(two, jump * SIDE, axis=1))
                        regs[i + jump] = jnp.where(
                            keep, pltpu.roll(one, LANES - jump * SIDE, axis=1), two
                        )
            halves.append(regs)
        image = jnp.concatenate(
            [jnp.concatenate([halves[0][g], halves[1][g]], axis=1) for g in range(8)], axis=0
        )
        scales.append(1.0 / jnp.sum(image, axis=1, keepdims=True))
        high, low = split(image)
        found.append(jnp.concatenate([high, low, high], axis=1))
    result = matmul(jnp.concatenate(found, axis=0), table[...]) * jnp.concatenate(scales, axis=0)
    out_ref[...] = result[0 : out_ref.shape[0]]


def spots_call(stars, devices, total_tiles, foot_rows, foot_cols, wind, strips, amplitude, table):
    vmem = pl.BlockSpec(memory_space=pltpu.VMEM)
    steps, layers = wind.shape[0], wind.shape[2]
    depth = strips.shape[1]
    subs = amplitude.shape[1] // SIDE
    high, low = across_tables()
    table_across = np.concatenate([high, high, low], axis=0)
    count = steps * subs
    padded = -(-count // 64) * 64
    return pl.pallas_call(
        functools.partial(spots_kernel, stars, devices, total_tiles),
        out_shape=jax.ShapeDtypeStruct((count, SIDE * SIDE), F32),
        in_specs=[vmem] * 8,
        out_specs=vmem,
        scratch_shapes=[
            pltpu.VMEM((layers * HALF + 1, GROUP * depth, LANES), F32),
            pltpu.VMEM((layers * (FULL + 1), 3 * SIDE, LANES), F32),
            pltpu.VMEM((count // 8 * SIDE, 6 * LANES), BF16),
        ],
        compiler_params=pltpu.CompilerParams(vmem_limit_bytes=16 << 20),
        name="spots",
    )(foot_rows, foot_cols, wind, strips, amplitude, table, table_across, down_table())


def shards(screens, foot_rows, foot_cols, wind, amplitude, owner, refs):
    stars, devices = lax.axis_size("star"), lax.axis_size("dev")
    layers, _, side, width = screens.shape
    steps = wind.shape[0]
    foot_rows, foot_cols = foot_rows.T, foot_cols.T
    wind = wind.transpose(0, 2, 1)
    tiles = width // LANES
    held = min(SPAN, tiles)
    subs = amplitude.shape[1] // side
    smem = pl.BlockSpec(memory_space=pltpu.SMEM)
    vmem = pl.BlockSpec(memory_space=pltpu.VMEM)
    hbm = pl.BlockSpec(memory_space=pltpu.HBM)
    screens = pltpu.with_memory_space_constraint(screens, pltpu.HBM)
    crops = pl.pallas_call(
        functools.partial(crop_kernel, stars, devices),
        out_shape=[jax.ShapeDtypeStruct((2 * layers, side, held * LANES), BF16)] * stars,
        in_specs=[hbm] * 3,
        out_specs=[vmem] * stars,
        scratch_shapes=[
            pltpu.SemaphoreType.DMA((stars, 2 * layers)),
            pltpu.SMEM(foot_rows.shape, jnp.int32),
            pltpu.SMEM(foot_cols.shape, jnp.int32),
            pltpu.SemaphoreType.DMA((2,)),
        ],
        compiler_params=pltpu.CompilerParams(vmem_limit_bytes=2 << 20),
        name="crop",
    )(
        pltpu.with_memory_space_constraint(foot_rows, pltpu.HBM),
        pltpu.with_memory_space_constraint(foot_cols, pltpu.HBM),
        screens,
    )
    parts = [crops[0]]
    for turn in range(1, stars):
        parts.append(
            lax.ppermute(crops[turn], "star", [(i, (i + turn) % stars) for i in range(stars)])
        )
    block = jax.ShapeDtypeStruct((devices // 2, 8, (layers * HALF + 1) * LANES), BF16)
    parities = [list(range(c, devices, 2)) for c in range(2)]
    groups = [[g + x for x in range(GROUP)] for g in range(0, devices, GROUP)]
    wide = SIDE * SIDE
    table = pl.pallas_call(
        table_kernel,
        out_shape=jax.ShapeDtypeStruct((3 * wide, wide), BF16),
        in_specs=[smem, vmem],
        out_specs=vmem,
        compiler_params=pltpu.CompilerParams(vmem_limit_bytes=2 << 20),
        name="table",
    )(owner, refs)
    sent = pl.pallas_call(
        functools.partial(spread_kernel, stars, devices, tiles),
        out_shape=block,
        in_specs=[vmem, vmem, pl.BlockSpec(memory_space=pl.ANY)] + [vmem] * stars,
        out_specs=vmem,
        scratch_shapes=[pltpu.VMEM((2, layers * HALF + 1, 2 * SIDE, LANES), F32)],
        compiler_params=pltpu.CompilerParams(vmem_limit_bytes=4 << 20),
        name="spread",
    )(foot_rows, foot_cols, table, *parts)
    held_rows = lax.all_to_all(sent, "dev", 0, 0, axis_index_groups=parities, tiled=True)
    chosen = pl.pallas_call(
        functools.partial(choose_kernel, devices),
        out_shape=jax.ShapeDtypeStruct((GROUP,) + block.shape[1:], BF16),
        in_specs=[vmem, vmem],
        out_specs=vmem,
        compiler_params=pltpu.CompilerParams(vmem_limit_bytes=2 << 20),
        name="choose",
    )(foot_rows, held_rows)
    strips = lax.all_to_all(chosen, "dev", 0, 0, axis_index_groups=groups, tiled=True)
    found = spots_call(
        stars, devices, stars * tiles, foot_rows, foot_cols, wind, strips, amplitude, table
    )
    return found.reshape(steps, 1, 1, subs, SIDE * SIDE)


def solution(mesh):
    in_specs = (P(None, None, "dev", "star"), P(), P(), P(), P("dev", None), P("star", "dev"), P())
    out_specs = P(None, "star", "dev", None, None)
    return jax.shard_map(shards, mesh=mesh, in_specs=in_specs, out_specs=out_specs, check_vma=False)
```

```python
import functools
import math

import jax
import jax.numpy as jnp
import numpy as np
from jax import lax
from jax.experimental import pallas as pl
from jax.experimental.pallas import tpu as pltpu
from jax.sharding import PartitionSpec as P

BIN = 4
SIDE = 16
LANES = 128
SPAN = 12
FULL = 10
HALF = FULL // 2
TAIL = 32
GROUP = 8

F32 = jnp.float32
BF16 = jnp.bfloat16


def split_np(table):
    high = table.astype(jnp.bfloat16)
    low = (table - high.astype(np.float64)).astype(jnp.bfloat16)
    return high, low


def split(value):
    high = value.astype(BF16)
    return high, (value - high.astype(F32)).astype(BF16)


def across_tables():
    length = BIN * SIDE
    freq = (np.arange(length) + length // 2) % length
    angle = 2.0 * math.pi * (np.outer(np.arange(SIDE), freq) % length) / length
    real, imag = np.cos(angle), -np.sin(angle)
    out = np.zeros((2, 8, SIDE, 2, BIN, SIDE, 8))
    for i in range(8):
        for b in range(BIN):
            re, im = real[:, b::BIN], imag[:, b::BIN]
            out[0, i, :, 0, b, :, i] = re
            out[1, i, :, 0, b, :, i] = -im
            out[0, i, :, 1, b, :, i] = im
            out[1, i, :, 1, b, :, i] = re
    return split_np(out.reshape(2 * 8 * SIDE, 2 * BIN * SIDE * 8))


def down_table():
    length = BIN * SIDE
    freq = (np.arange(length) + length // 2) % length
    angle = 2.0 * math.pi * (np.outer(freq, np.arange(SIDE)) % length) / length
    real, imag = np.cos(angle), -np.sin(angle)
    order = np.concatenate([np.arange(a, length, BIN) for a in range(BIN)])
    real, imag = real[order], imag[order]
    table = np.block([[real, -imag], [imag, real]])
    high, low = split_np(table)
    return np.concatenate([high, high, low], axis=1)


def place_of(rows_ref, cols_ref, layer, star, devices, total_tiles):
    offset = rows_ref[star, layer]
    strip = lax.div(offset, SIDE)
    part = lax.rem(offset, SIDE)
    tile = jnp.minimum(lax.div(cols_ref[star, layer], LANES), total_tiles - SPAN)
    return strip, part, tile


def own_row(ref, star):
    row = ref[pl.ds(star, 1), :]
    return [row[0, layer] for layer in range(ref.shape[1])]


def place_of_own(offset, left, total_tiles):
    strip = lax.div(offset, SIDE)
    part = lax.rem(offset, SIDE)
    tile = jnp.minimum(lax.div(left, LANES), total_tiles - SPAN)
    return strip, part, tile


def first_tile(tile, panel, tiles, held):
    return jnp.clip(tile - panel * tiles, 0, tiles - held)


def crop_kernel(stars, devices, rows_hbm, cols_hbm, screens_ref, *rest):
    outs, (sem, rows_ref, cols_ref, scalar_sem) = rest[:stars], rest[stars:]
    scalars = [
        pltpu.make_async_copy(rows_hbm, rows_ref, scalar_sem.at[0]),
        pltpu.make_async_copy(cols_hbm, cols_ref, scalar_sem.at[1]),
    ]
    for copy in scalars:
        copy.start()
    for copy in scalars:
        copy.wait()
    layers, bands, side, width = screens_ref.shape
    tiles = width // LANES
    held = min(SPAN, tiles)
    me = lax.axis_index("star")
    place = lax.axis_index("dev")
    copies = []
    for turn in range(stars):
        star = lax.rem(me + turn, stars)
        for layer in range(layers):
            strip, _, tile = place_of(rows_ref, cols_ref, layer, star, devices, stars * tiles)
            behind = lax.rem(place + bands * devices - strip, devices)
            band = lax.div(strip + behind, devices)
            start = first_tile(tile, me, tiles, held)
            columns = pl.ds(pl.multiple_of(start * LANES, LANES), held * LANES)
            for slot in range(2):
                copy = pltpu.make_async_copy(
                    screens_ref.at[layer, lax.rem(band + slot, bands), :, columns],
                    outs[turn].at[2 * layer + slot],
                    sem.at[turn, 2 * layer + slot],
                )
                copy.start()
                copies.append(copy)
    for copy in copies:
        copy.wait()


def spread_kernel(stars, devices, tiles, rows_ref, cols_ref, _, *rest):
    parts, out_ref, turned = rest[:stars], rest[stars], rest[stars + 1]
    layers = parts[0].shape[0] // 2
    held = parts[0].shape[2] // LANES
    me = lax.axis_index("star")
    place = lax.axis_index("dev")
    row = lax.broadcasted_iota(jnp.int32, (SIDE, LANES), 0)
    lane = lax.broadcasted_iota(jnp.int32, (SIDE, LANES), 1)
    tails = [None, None]
    offsets, lefts = own_row(rows_ref, me), own_row(cols_ref, me)
    for layer in range(layers):
        strip, part, tile = place_of_own(offsets[layer], lefts[layer], stars * tiles)
        behind = lax.rem(place + (1 << 20) * devices - strip, devices)
        wraps = row < jnp.where(behind == 0, SIDE, jnp.where(behind == 1, part, 0))
        shift = lefts[layer] - tile * LANES
        skip, fine = lax.div(shift, LANES), lax.rem(shift, LANES)
        inside = lane < LANES - fine
        rolled = []
        for t in range(FULL + 2):
            spot = tile + skip + t
            panel = lax.div(spot, tiles)
            pair = []
            for slot in range(2):
                value = None
                for turn in range(stars):
                    sender = lax.rem(me + stars - turn, stars)
                    start = first_tile(tile, sender, tiles, held)
                    local = jnp.clip(spot - sender * tiles - start, 0, held - 1)
                    lanes = pl.ds(pl.multiple_of(local * LANES, LANES), LANES)
                    seen = parts[turn][2 * layer + slot, :, lanes].astype(F32)
                    if value is None:
                        value = seen
                    else:
                        value = jnp.where(panel == sender, seen, value)
                pair.append(value)
            mixed = jnp.where(wraps, pair[1], pair[0])
            rolled.append(
                [pltpu.roll(v, lax.rem(LANES - fine, LANES), axis=1) for v in (pair[0], mixed)]
            )
        for kind in range(2):
            for t in range(FULL + 1):
                value = jnp.where(inside, rolled[t][kind], rolled[t + 1][kind])
                if t < FULL:
                    rows = pl.ds(t // HALF, SIDE, stride=2)
                    turned[kind, layer * HALF + t % HALF, rows, :] = value
                elif layer == 0:
                    tails[kind] = value
                else:
                    value = pltpu.roll(value, layer * TAIL, axis=1)
                    tails[kind] = jnp.where(lane < layer * TAIL, tails[kind], value)
    for kind in range(2):
        for side in range(2):
            turned[kind, layers * HALF, pl.ds(side, SIDE, stride=2), :] = tails[kind]
    half = GROUP // 2
    last = devices // GROUP - 1
    for m in range(half):
        for kind in range(2):
            rows = slice(m * 8, (m + 1) * 8)
            pieces = [turned[kind, unit, rows, :] for unit in range(layers * HALF + 1)]
            block = jnp.concatenate(pieces, axis=1).astype(BF16)
            if kind == 1:
                out_ref[last * half + m] = block
            else:
                for group in range(last):
                    out_ref[group * half + m] = block


def choose_kernel(devices, rows_ref, in_ref, out_ref):
    layers = rows_ref.shape[1]
    width = HALF * LANES
    me = lax.axis_index("star")
    place = lax.axis_index("dev")
    first = place - lax.rem(place, GROUP)
    odd = lax.rem(place, 2)
    m = lax.div(place - first, 2)
    row = lax.broadcasted_iota(jnp.int32, (8, width), 0)
    lane = lax.broadcasted_iota(jnp.int32, (8, LANES), 1)
    residue = m * 4 + lax.div(row, 2)
    offsets = own_row(rows_ref, me)
    last = slice(layers * width, layers * width + LANES)
    tails = [None] * GROUP
    for layer in range(layers):
        offset = offsets[layer]
        early = residue < lax.rem(offset, SIDE)
        lanes = slice(layer * width, (layer + 1) * width)
        for j in range(GROUP):
            start = lax.div(offset, SIDE) + first + j
            step = lax.rem(start + odd, 2)
            late_from = lax.div(lax.rem(start + step, devices), 2)
            early_from = lax.div(lax.rem(start + 2 - step, devices), 2)
            out_ref[j, :, lanes] = jnp.where(
                early,
                in_ref[early_from, :, lanes].astype(F32),
                in_ref[late_from, :, lanes].astype(F32),
            ).astype(BF16)
            tail = jnp.where(
                early[:, 0:LANES],
                in_ref[early_from, :, last].astype(F32),
                in_ref[late_from, :, last].astype(F32),
            )
            tails[j] = tail if layer == 0 else jnp.where(lane < layer * TAIL, tails[j], tail)
    for j in range(GROUP):
        out_ref[j, :, last] = tails[j].astype(BF16)


def sin_cos(value):
    turns = jnp.floor(value * (2.0 / math.pi) + 0.5)
    rest = value - turns * 1.5703125
    rest = rest - turns * 4.837512969970703125e-4
    rest = rest - turns * 7.549789948768648e-8
    square = rest * rest
    sine = rest + rest * square * (
        -1.6666654611e-1 + square * (8.3321608736e-3 - square * 1.9515295891e-4)
    )
    cosine = (
        1.0
        - 0.5 * square
        + square
        * square
        * (4.166664568298827e-2 + square * (-1.388731625493765e-3 + square * 2.443315711809948e-5))
    )
    quarter = turns.astype(jnp.int32)
    odd = (quarter & 1) == 1
    flip_sine = (quarter & 2) == 2
    flip_cosine = ((quarter + 1) & 2) == 2
    s = jnp.where(odd, cosine, sine)
    c = jnp.where(odd, sine, cosine)
    return jnp.where(flip_sine, -s, s), jnp.where(flip_cosine, -c, c)


def matmul(left, right):
    return lax.dot_general(
        left, right, (((1,), (0,)), ((), ())), preferred_element_type=F32
    )


def table_kernel(owner_ref, refs_ref, table):
    refer = refs_ref[owner_ref[0, 0]]
    wide = SIDE * SIDE
    pick_row = lax.broadcasted_iota(jnp.int32, (SIDE, wide), 0)
    pick_lane = lax.broadcasted_iota(jnp.int32, (SIDE, wide), 1)
    pick = (pick_row == ((SIDE - (pick_lane & 15)) & 15)).astype(F32)
    base = lax.dot_general(
        refer,
        pick,
        (((1,), (0,)), ((), ())),
        precision=lax.Precision.HIGHEST,
        preferred_element_type=F32,
    )
    for bit in range(4):
        moved = pltpu.roll(base, 1 << bit, axis=0)
        base = jnp.where(((pick_lane >> (4 + bit)) & 1) == 1, moved, base)
    for q in range(SIDE):
        if q == 0:
            block = base
        else:
            block = jnp.where(
                (pick_lane & 15) >= q,
                pltpu.roll(base, q, axis=1),
                pltpu.roll(base, wide + q - SIDE, axis=1),
            )
        high, low = split(block)
        table[pl.ds(q * SIDE, SIDE), :] = high
        table[pl.ds(wide + q * SIDE, SIDE), :] = high
        table[pl.ds(2 * wide + q * SIDE, SIDE), :] = low


def spots_kernel(
    stars,
    devices,
    rows_ref,
    wind_ref,
    in_ref,
    amp_ref,
    table,
    across_ref,
    down_ref,
    out_ref,
    turned,
    window,
    field,
):
    steps, layers = wind_ref.shape[0], wind_ref.shape[2]
    across = amp_ref.shape[1] // LANES
    me = lax.axis_index("star")
    place = lax.axis_index("dev")
    lane = lax.broadcasted_iota(jnp.int32, (SIDE, LANES), 1)
    offsets = own_row(rows_ref, me)
    shifts = [wind_ref[step] for step in range(steps)]

    half = GROUP // 2
    for x in range(GROUP):
        seen = in_ref[x].astype(F32)
        at = (x % 2) * half * 8 + x // 2 * 8
        for unit in range(layers * HALF + 1):
            turned[unit, pl.ds(at, 8), :] = seen[:, unit * LANES : (unit + 1) * LANES]
    for layer in range(layers):
        odd = lax.rem(lax.div(offsets[layer], SIDE) + place, 2)
        for t in range(FULL + 1):
            unit = layer * HALF + t % HALF if t < FULL else layers * HALF
            at = t // HALF if t < FULL else 0
            one, two = (
                turned[unit, pl.ds(parity * half * 8 + at, SIDE, stride=2), :]
                for parity in (odd, 1 - odd)
            )
            if t == FULL and layer > 0:
                one, two = (pltpu.roll(v, LANES - layer * TAIL, axis=1) for v in (one, two))
            for turn, value in enumerate((one, two, one)):
                window[layer * (FULL + 1) + t, pl.ds(turn * SIDE, SIDE), :] = value

    for step in range(steps):
        phase = [None] * across
        for layer in range(layers):
            fine = shifts[step][1, layer]
            start = lax.rem(offsets[layer], SIDE) + shifts[step][0, layer]
            inside = lane < LANES - fine
            rolled = [
                pltpu.roll(
                    window[layer * (FULL + 1) + t, pl.ds(start, SIDE), :],
                    lax.rem(LANES - fine, LANES),
                    axis=1,
                )
                for t in range(across + 1)
            ]
            for t in range(across):
                value = jnp.where(inside, rolled[t], rolled[t + 1])
                phase[t] = value if phase[t] is None else phase[t] + value
        for t in range(across):
            sine, cosine = sin_cos(phase[t])
            amp = amp_ref[:, t * LANES : (t + 1) * LANES]
            rows = pl.ds((step * across + t) * SIDE, SIDE)
            for part, value in enumerate((amp * cosine, amp * sine)):
                high, low = split(value)
                at = part * LANES
                field[rows, at : at + LANES] = high
                field[rows, at + 2 * LANES : at + 3 * LANES] = low
                field[rows, at + 4 * LANES : at + 5 * LANES] = high

    first = matmul(field[...], across_ref[...])

    wide_out = first.shape[1] // 2
    wide = SIDE * SIDE
    lane8 = lax.broadcasted_iota(jnp.int32, (8, LANES), 1)
    turns = steps * across
    found, scales = [], []
    for big in range(0, turns, 8):
        smalls = []
        for turn in range(big, min(big + 8, turns)):
            rows = pl.ds(turn * SIDE, SIDE)
            real_high, real_low = split(first[turn * SIDE : (turn + 1) * SIDE, 0:wide_out])
            imag_high, imag_low = split(first[turn * SIDE : (turn + 1) * SIDE, wide_out : 2 * wide_out])
            stacked = jnp.concatenate(
                [real_high, imag_high, real_low, imag_low, real_high, imag_high], axis=0
            )
            spectrum = matmul(down_ref[...], stacked)
            power = spectrum * spectrum
            total = power[0:SIDE]
            for k in range(1, 2 * BIN):
                total = total + power[k * SIDE : (k + 1) * SIDE]
            small = total[:, 0:LANES]
            for k in range(1, BIN):
                small = small + total[:, k * LANES : (k + 1) * LANES]
            smalls.append(small)
        while len(smalls) < 8:
            smalls.append(jnp.ones((SIDE, LANES), F32))
        flipped = jnp.concatenate(smalls, axis=0).T
        halves = []
        for half in range(2):
            regs = [flipped[(half * 8 + q) * 8 : (half * 8 + q + 1) * 8] for q in range(8)]
            for jump in (4, 2, 1):
                keep = ((lane8 >> 4) & jump) == 0
                for i in range(8):
                    if i & jump == 0:
                        one, two = regs[i], regs[i + jump]
                        regs[i] = jnp.where(keep, one, pltpu.roll(two, jump * SIDE, axis=1))
                        regs[i + jump] = jnp.where(
                            keep, pltpu.roll(one, LANES - jump * SIDE, axis=1), two
                        )
            halves.append(regs)
        image = jnp.concatenate(
            [jnp.concatenate([halves[0][g], halves[1][g]], axis=1) for g in range(8)], axis=0
        )
        scales.append(1.0 / jnp.sum(image, axis=1, keepdims=True))
        high, low = split(image)
        found.append(jnp.concatenate([high, low, high], axis=1))
    result = matmul(jnp.concatenate(found, axis=0), table[...]) * jnp.concatenate(scales, axis=0)
    out_ref[...] = result[0 : out_ref.shape[0]]


def spots_call(stars, devices, foot_rows, wind, strips, amplitude, table):
    vmem = pl.BlockSpec(memory_space=pltpu.VMEM)
    steps, layers = wind.shape[0], wind.shape[2]
    depth = strips.shape[1]
    subs = amplitude.shape[1] // SIDE
    high, low = across_tables()
    table_across = np.concatenate([high, high, low], axis=0)
    count = steps * subs
    padded = -(-count // 64) * 64
    return pl.pallas_call(
        functools.partial(spots_kernel, stars, devices),
        out_shape=jax.ShapeDtypeStruct((count, SIDE * SIDE), F32),
        in_specs=[vmem] * 7,
        out_specs=vmem,
        scratch_shapes=[
            pltpu.VMEM((layers * HALF + 1, GROUP * depth, LANES), F32),
            pltpu.VMEM((layers * (FULL + 1), 3 * SIDE, LANES), F32),
            pltpu.VMEM((count // 8 * SIDE, 6 * LANES), BF16),
        ],
        compiler_params=pltpu.CompilerParams(vmem_limit_bytes=16 << 20),
        name="spots",
    )(foot_rows, wind, strips, amplitude, table, table_across, down_table())


def shards(screens, foot_rows, foot_cols, wind, amplitude, owner, refs):
    stars, devices = lax.axis_size("star"), lax.axis_size("dev")
    layers, _, side, width = screens.shape
    steps = wind.shape[0]
    foot_rows, foot_cols = foot_rows.T, foot_cols.T
    wind = wind.transpose(0, 2, 1)
    tiles = width // LANES
    held = min(SPAN, tiles)
    subs = amplitude.shape[1] // side
    smem = pl.BlockSpec(memory_space=pltpu.SMEM)
    vmem = pl.BlockSpec(memory_space=pltpu.VMEM)
    hbm = pl.BlockSpec(memory_space=pltpu.HBM)
    screens = pltpu.with_memory_space_constraint(screens, pltpu.HBM)
    crops = pl.pallas_call(
        functools.partial(crop_kernel, stars, devices),
        out_shape=[jax.ShapeDtypeStruct((2 * layers, side, held * LANES), BF16)] * stars,
        in_specs=[hbm] * 3,
        out_specs=[vmem] * stars,
        scratch_shapes=[
            pltpu.SemaphoreType.DMA((stars, 2 * layers)),
            pltpu.SMEM(foot_rows.shape, jnp.int32),
            pltpu.SMEM(foot_cols.shape, jnp.int32),
            pltpu.SemaphoreType.DMA((2,)),
        ],
        compiler_params=pltpu.CompilerParams(vmem_limit_bytes=2 << 20),
        name="crop",
    )(
        pltpu.with_memory_space_constraint(foot_rows, pltpu.HBM),
        pltpu.with_memory_space_constraint(foot_cols, pltpu.HBM),
        screens,
    )
    parts = [crops[0]]
    for turn in range(1, stars):
        parts.append(
            lax.ppermute(crops[turn], "star", [(i, (i + turn) % stars) for i in range(stars)])
        )
    block = jax.ShapeDtypeStruct((devices // 2, 8, (layers * HALF + 1) * LANES), BF16)
    parities = [list(range(c, devices, 2)) for c in range(2)]
    groups = [[g + x for x in range(GROUP)] for g in range(0, devices, GROUP)]
    wide = SIDE * SIDE
    table = pl.pallas_call(
        table_kernel,
        out_shape=jax.ShapeDtypeStruct((3 * wide, wide), BF16),
        in_specs=[smem, vmem],
        out_specs=vmem,
        compiler_params=pltpu.CompilerParams(vmem_limit_bytes=2 << 20),
        name="table",
    )(owner, refs)
    sent = pl.pallas_call(
        functools.partial(spread_kernel, stars, devices, tiles),
        out_shape=block,
        in_specs=[vmem, vmem, pl.BlockSpec(memory_space=pl.ANY)] + [vmem] * stars,
        out_specs=vmem,
        scratch_shapes=[pltpu.VMEM((2, layers * HALF + 1, 2 * SIDE, LANES), F32)],
        compiler_params=pltpu.CompilerParams(vmem_limit_bytes=4 << 20),
        name="spread",
    )(foot_rows, foot_cols, table, *parts)
    held_rows = lax.all_to_all(sent, "dev", 0, 0, axis_index_groups=parities, tiled=True)
    chosen = pl.pallas_call(
        functools.partial(choose_kernel, devices),
        out_shape=jax.ShapeDtypeStruct((GROUP,) + block.shape[1:], BF16),
        in_specs=[vmem, vmem],
        out_specs=vmem,
        compiler_params=pltpu.CompilerParams(vmem_limit_bytes=2 << 20),
        name="choose",
    )(foot_rows, held_rows)
    strips = lax.all_to_all(chosen, "dev", 0, 0, axis_index_groups=groups, tiled=True)
    found = spots_call(
        stars, devices, foot_rows, wind, strips, amplitude, table
    )
    return found.reshape(steps, 1, 1, subs, SIDE * SIDE)


def solution(mesh):
    in_specs = (P(None, None, "dev", "star"), P(), P(), P(), P("dev", None), P("star", "dev"), P())
    out_specs = P(None, "star", "dev", None, None)
    return jax.shard_map(shards, mesh=mesh, in_specs=in_specs, out_specs=out_specs, check_vma=False)
```
